32 devices in a mesh: seq: 8 (over y, x, core), head: 4 (over z).
Axes of the slice: x: 2, y: 2, z: 4, core: 2. Of those that a mesh axis runs over, the one named last changes fastest.
Arguments:
- queries: bfloat16 [2048, 4096], P('seq', 'head'), may hold values from -0.59765625 to 0.59765625
- keys: bfloat16 [2048, 4096], P('seq', 'head'), may hold values from -0.59765625 to 0.59765625
- values: bfloat16 [2048, 4096], P('seq', 'head'), may hold values from -6 to 6
- log_decay: float32 [32, 2048], P('head', 'seq'), may hold values from -0.8 to 0, as said below
- lengths: int32 [16], replicated, may hold values from 1 to 512, as said below
- out_weight: bfloat16 [4096, 4096], P('seq', 'head'), may hold values from -0.09375 to 0.09375
- out_grad: bfloat16 [2048, 4096], P('seq', 'head'), may hold values from -0.29882812 to 0.29882812
Outputs:
- mixed: bfloat16 [2048, 4096], P('seq', 'head')
- grad_queries: bfloat16 [2048, 4096], P('seq', 'head')
- grad_keys: bfloat16 [2048, 4096], P('seq', 'head')
- grad_values: bfloat16 [2048, 4096], P('seq', 'head')
- grad_weight: float32 [4096, 4096], P('seq', 'head')
The draws below stay inside these ranges and needn't reach their ends.
Inputs may be any that keep to these rules, and one draw needn't show every extreme that they name: `log_decay`: every entry is negative; tokens where a document starts cut the state whatever their value. The 16 lengths sum to 2048; the longest document has exactly 512 tokens.
All inputs are finite; a program needn't handle non-finite values.
Results may differ from the reference program's by a relative error of at most 0.015.
Values may be sent and summed in bfloat16 or wider, within the bound.
A program may use at most 64 MiB of HBM per device.

```python
import math
import jax
import jax.numpy as jnp
from jax import lax

D = 4096
ATTENTION_HEADS = 32
HD = 128
TOK_DEV = 256
NDOCS = 16
PACKED_TOKENS = 2048
MOST = 512


def draw_log_decay(key, part):
    random_split_keys = jax.random.split(key, 7)
    fast_top = 1.0 / 40.0
    base_low = 0.05 / MOST
    baseline_decay_rate = jnp.exp(jax.random.uniform(random_split_keys[0], (ATTENTION_HEADS, 1), minval=math.log(base_low), maxval=math.log(fast_top)))
    shards = PACKED_TOKENS // TOK_DEV
    damping_factor = jnp.exp(jax.random.uniform(random_split_keys[3], (ATTENTION_HEADS, shards, 1), minval=-0.5, maxval=0.5))
    damping_factor = jnp.broadcast_to(damping_factor, (ATTENTION_HEADS, shards, TOK_DEV)).reshape(ATTENTION_HEADS, PACKED_TOKENS)
    random_jitter = jnp.exp(jax.random.uniform(random_split_keys[4], (ATTENTION_HEADS, PACKED_TOKENS), minval=-0.4, maxval=0.4))
    spike_position = jax.random.uniform(random_split_keys[5], (ATTENTION_HEADS, PACKED_TOKENS)) < 4.0 / PACKED_TOKENS
    spike_loss_value = jnp.log(jax.random.uniform(random_split_keys[6], (ATTENTION_HEADS, PACKED_TOKENS), minval=0.5, maxval=0.8))
    return (-(baseline_decay_rate * damping_factor * random_jitter) + jnp.where(spike_position, spike_loss_value, 0.0)).astype(jnp.float32)


def draw_lengths(key, part):
    others = NDOCS - 3
    lowest = max(TOK_DEV // 4, 1)
    highest = 3 * TOK_DEV // 4 + 1
    offsets = jax.random.randint(jax.random.fold_in(key, 12), (2,), lowest, highest, dtype=jnp.int32)
    first_long = (MOST - offsets[0]).astype(jnp.int32)
    third_long = (MOST - offsets[1]).astype(jnp.int32)
    spare = (MOST + offsets[0] + offsets[1] - others).astype(jnp.int32)
    weights = jax.random.randint(jax.random.fold_in(key, 11), (others,), 50, 101, dtype=jnp.int32)
    running = jnp.cumsum(weights, dtype=jnp.int32)
    total_weight = running[-1]
    bounds = spare * running // total_weight
    earlier = jnp.concatenate([jnp.zeros((1,), jnp.int32), bounds[:-1]])
    rest = (1 + bounds - earlier).astype(jnp.int32)
    longs = jnp.stack([first_long, jnp.asarray(MOST, jnp.int32), third_long]).astype(jnp.int32)
    return jnp.concatenate([longs, rest]).astype(jnp.int32)


def spiked(values, rng, source, target, parts, factor):
    owner, partner = [(jnp.arange(values.shape[axis_at]) // (values.shape[axis_at] // parts)).reshape([-1 if axis == axis_at else 1 for axis in range(values.ndim)]) for axis_at in (source, target)]
    chosen = jax.random.permutation(rng, parts)[partner]
    strong = (owner == chosen) | (owner == (partner + parts // 2) % parts)
    return jnp.where(strong, factor * values, values)


def steps_of(rng, dims, pieces, low, high):
    level = 1.0
    for dim, shards_of in pieces:
        steps = jax.random.uniform(jax.random.fold_in(jax.random.fold_in(rng, 6), dim), (shards_of,), jnp.float32, low / len(pieces), high / len(pieces))
        level = level * jnp.repeat(jnp.exp(steps), dims[dim] // shards_of).reshape((-1,) + (1,) * (len(dims) - 1 - dim))
    return level


def noise(own_key, dims, width, reach, cuts=(), kind=jnp.bfloat16):
    factor_of = steps_of(own_key, dims, cuts, -0.22, 0.18) if cuts else 1.0
    values = jax.random.normal(own_key, dims, jnp.float32) * width * factor_of
    return jnp.minimum(jnp.maximum(values, -reach), reach).astype(kind)


def gaussian_with(rng, extent, scale, limit, cuts, heavy, kind=jnp.bfloat16):
    drawn = scale * jax.random.normal(rng, extent, jnp.float32)
    if cuts:
        drawn = drawn * steps_of(rng, extent, cuts, -0.22, 0.18)
    return jnp.clip(spiked(drawn, jax.random.fold_in(rng, 3), *heavy), -limit, limit).astype(kind)


def setup_inputs(seed: int = 0) -> dict:
    seeds = jax.random.split(jax.random.key(seed), 8)
    return {
        "queries": noise(seeds[0], (PACKED_TOKENS, ATTENTION_HEADS * HD), 0.1, 0.59765625, ((0, 8), (1, 4))),
        "keys": noise(seeds[1], (PACKED_TOKENS, ATTENTION_HEADS * HD), 0.1, 0.59765625, ((0, 8), (1, 4))),
        "values": noise(seeds[2], (PACKED_TOKENS, ATTENTION_HEADS * HD), 1.0, 6.0, ((0, 8), (1, 4))),
        "log_decay": draw_log_decay(jax.random.fold_in(seeds[7], 71), 0),
        "lengths": draw_lengths(jax.random.fold_in(seeds[7], 71), 0),
        "out_weight": noise(seeds[5], (D, ATTENTION_HEADS * HD), (ATTENTION_HEADS * HD) ** -0.5, 0.09375, ((0, 8), (1, 4))),
        "out_grad": gaussian_with(seeds[6], (PACKED_TOKENS, D), 0.05, 0.29882812, ((0, 8), (1, 4)), (0, 1, 8, 2.0)),
    }


HIGH = lax.Precision.HIGHEST


def doc_index(lengths, positions):
    starts = jnp.cumsum(lengths, dtype=jnp.int32) - lengths
    above = (positions[:, None] >= starts[None, :]).astype(jnp.int32)
    return jnp.sum(above, axis=1, dtype=jnp.int32) - 1


def block_masks(log_decay, docs, prev_doc, last_doc, next_doc):
    count = docs.shape[0]
    cumul = jnp.cumsum(log_decay, axis=1)
    order = jnp.arange(count, dtype=jnp.int32)
    joint = jnp.logical_and(order[:, None] >= order[None, :], docs[:, None] == docs[None, :])[None]
    spread = jnp.where(joint, cumul[:, :, None] - cumul[:, None, :], 0.0)
    decay = jnp.where(joint, jnp.exp(spread), 0.0)
    zero = jnp.zeros_like(cumul)
    tail = cumul[:, -1:] - cumul
    enter = jnp.where((docs == prev_doc)[None], jnp.exp(cumul), zero)
    keep = jnp.where((docs == last_doc)[None], jnp.exp(tail), zero)
    leave = jnp.where((docs == next_doc)[None], jnp.exp(tail), zero)
    through = jnp.where(prev_doc == last_doc, jnp.exp(cumul[:, -1]), jnp.zeros_like(cumul[:, -1]))
    return decay, enter, keep, leave, through


def reference(queries, keys, values, log_decay, lengths, out_weight, out_grad):
    blocks = PACKED_TOKENS // TOK_DEV
    rows = TOK_DEV

    def split(x):
        return x.reshape(blocks, rows, ATTENTION_HEADS, HD)

    qs, ks, vs = split(queries), split(keys), split(values)
    decays = log_decay.reshape(ATTENTION_HEADS, blocks, rows).transpose(1, 0, 2)
    docs = doc_index(lengths, jnp.arange(PACKED_TOKENS, dtype=jnp.int32)).reshape(blocks, rows)
    starts = jnp.arange(blocks, dtype=jnp.int32) * rows
    prevs = doc_index(lengths, (starts - 1).astype(jnp.int32))
    lasts = doc_index(lengths, (starts + rows - 1).astype(jnp.int32))
    nexts = doc_index(lengths, (starts + rows).astype(jnp.int32))

    def forward(state, item):
        qb, kb, vb, lb, db, pb, tb, nb = item
        decay, enter, keep, leave, through = block_masks(lb, db, pb, tb, nb)
        q32, k32, v32 = qb.astype(jnp.float32), kb.astype(jnp.float32), vb.astype(jnp.float32)
        scores = jnp.einsum('the,she->hts', q32, k32)
        attn = lax.optimization_barrier((scores * decay).astype(jnp.bfloat16)).astype(jnp.float32)
        local = jnp.einsum('hts,shf->thf', attn, v32)
        carry = jnp.einsum('the,hef->thf', q32, state, precision=HIGH) * enter.T[:, :, None]
        out = (local + carry).astype(jnp.bfloat16)
        summary = jnp.einsum('the,thf->hef', k32 * keep.T[:, :, None], v32, precision=HIGH)
        return through[:, None, None] * state + summary, (out, state)

    init = jnp.zeros((ATTENTION_HEADS, HD, HD), jnp.float32)
    items = (qs, ks, vs, decays, docs, prevs, lasts, nexts)
    _, (outs, states) = lax.scan(forward, init, items)
    attended = outs.reshape(PACKED_TOKENS, ATTENTION_HEADS * HD)
    mixed = jnp.dot(attended, out_weight.T, preferred_element_type=jnp.float32).astype(jnp.bfloat16)
    grad_att = jnp.dot(out_grad, out_weight, preferred_element_type=jnp.float32).astype(jnp.bfloat16)
    grad_weight = jnp.dot(out_grad.T, attended, preferred_element_type=jnp.float32)
    gs = split(grad_att)

    def backward(carry, item):
        qb, kb, vb, gb, lb, db, pb, tb, nb, state = item
        decay, enter, keep, leave, through = block_masks(lb, db, pb, tb, nb)
        q32, k32, v32, g32 = qb.astype(jnp.float32), kb.astype(jnp.float32), vb.astype(jnp.float32), gb.astype(jnp.float32)
        scores = jnp.einsum('the,she->hts', q32, k32)
        attn = lax.optimization_barrier((scores * decay).astype(jnp.bfloat16)).astype(jnp.float32)
        pulls = jnp.einsum('thf,shf->hts', g32, v32)
        back = lax.optimization_barrier((pulls * decay).astype(jnp.bfloat16)).astype(jnp.float32)
        dq = jnp.einsum('hts,she->the', back, k32) + jnp.einsum('hef,thf->the', state, g32, precision=HIGH) * enter.T[:, :, None]
        dk = jnp.einsum('hts,the->she', back, q32) + jnp.einsum('hef,thf->the', carry, v32, precision=HIGH) * leave.T[:, :, None]
        dv = jnp.einsum('hts,thf->shf', attn, g32) + jnp.einsum('hef,the->thf', carry, k32, precision=HIGH) * leave.T[:, :, None]
        summary = jnp.einsum('the,thf->hef', q32 * enter.T[:, :, None], g32, precision=HIGH)
        new_carry = through[:, None, None] * carry + summary
        return new_carry, (dq.astype(jnp.bfloat16), dk.astype(jnp.bfloat16), dv.astype(jnp.bfloat16))

    items_back = (qs, ks, vs, gs, decays, docs, prevs, lasts, nexts, states)
    _, (dqs, dks, dvs) = lax.scan(backward, init, items_back, reverse=True)
    shape = (PACKED_TOKENS, ATTENTION_HEADS * HD)
    return mixed, dqs.reshape(shape), dks.reshape(shape), dvs.reshape(shape), grad_weight
```

```python
import functools
import math

import jax
import jax.numpy as jnp
from jax import lax
from jax.experimental import pallas as pl
from jax.experimental.pallas import tpu as pltpu
from jax.sharding import PartitionSpec as P

MESH = pl.DeviceIdType.MESH
F32 = jnp.float32
BF16 = jnp.bfloat16
HD = 128
TILE = 256


def dot(a, b, ca, cb):
    return lax.dot_general(a, b, (((ca,), (cb,)), ((), ())), preferred_element_type=F32)


def kernel(
    n_seq, n_head, hops,
    lengths, q_ref, k_ref, v_ref, ld_ref, w_ref, g_ref,
    mixed_ref, gq_ref, gk_ref, gv_ref, gw_ref,
    w_full, a_full, g_full, g_cols, part_send, part_recv,
    local, local2, decay_s, attn_s, enter_s, leave_s, state_s, ga_s, thr, thr_prev, thr_next,
    sum_f, sum_b, recv_f, recv_b,
    w_ss, w_rs, a_ss, a_rs, g_ss, g_rs, c_ss, c_rs, p_ss, p_rs,
    f_ss, f_rs, b_ss, b_rs, tp_ss, tp_rs, tn_ss, tn_rs,
):
    s, h = lax.axis_index("seq"), lax.axis_index("head")
    rows, width = q_ref.shape
    heads = width // HD
    wrows = w_ref.shape[0]
    gwidth = g_ref.shape[1]
    chips = n_seq // 2
    side = math.isqrt(chips)
    chip, core = s // 2, s % 2
    x, y = chip % side, chip // side
    partner = chip * 2 + (1 - core)
    offs = [(dy, dx) for dy in range(side) for dx in range(side) if (dy, dx) != (0, 0)]

    def rcopy(src, dst, ss, rs, seq, head):
        return pltpu.make_async_remote_copy(
            src_ref=src, dst_ref=dst, send_sem=ss, recv_sem=rs,
            device_id=(seq, head), device_id_type=MESH,
        )

    def away(i, sign):
        dy, dx = offs[i]
        if sign > 0:
            return ((y + dy) % side) * side + (x + dx) % side
        return ((y + side - dy) % side) * side + (x + side - dx) % side

    barrier = pltpu.get_barrier_semaphore()
    for j in range(1, n_seq):
        pl.semaphore_signal(barrier, inc=1, device_id=((s + j) % n_seq, h), device_id_type=MESH)
    for j in range(1, n_head):
        pl.semaphore_signal(barrier, inc=1, device_id=(s, (h + j) % n_head), device_id_type=MESH)
    pl.semaphore_wait(barrier, n_seq + n_head - 2)

    xn, yn, dn = y * side + (1 - x), (1 - y) * side + x, (1 - y) * side + (1 - x)

    class Plane:
        def __init__(self, src, full, size, ss, rs):
            self.src, self.full, self.size, self.ss, self.rs = src, full, size, ss, rs
            self.sent = []

        def block(self, index, half=None):
            at, size = index * self.size, self.size
            if half is not None:
                size = self.size // 2
                at = at + half * size
            return self.full.at[pl.ds(pl.multiple_of(at, size), size)]

        def send(self, src, dst, index, seq):
            copy = rcopy(src, dst, self.ss.at[index], self.rs.at[index], seq, h)
            copy.start()
            self.sent.append(copy)

        def arrived(self, ref, index):
            rcopy(ref, ref, self.ss.at[index], self.rs.at[index], partner, h).wait_recv()

        def pass_on(self, ref, index, cross):
            self.arrived(ref, index)
            self.send(ref, ref, cross, partner)

        def start(self):
            mine = self.block(s)
            if side == 2:
                self.send(self.src, mine, 0, xn * 2 + core)
                self.send(self.src, mine, 1, yn * 2 + core)
            else:
                for i in range(chips - 1):
                    self.send(self.src, mine, i, away(i, 1) * 2 + core)
            self.send(self.src, mine, 2 * chips, partner)

        def forward(self):
            if side == 2:
                bx, by = self.block(xn * 2 + core), self.block(yn * 2 + core)
                hx, hy = self.block(xn * 2 + core, 0), self.block(yn * 2 + core, 1)
                self.arrived(bx, 0)
                self.send(hx, hx, 2, yn * 2 + core)
                self.arrived(by, 1)
                self.send(hy, hy, 3, xn * 2 + core)
                self.send(bx, bx, chips, partner)
                self.send(by, by, chips + 1, partner)

        def finish(self):
            if side == 2:
                for half in range(2):
                    self.pass_on(self.block(dn * 2 + core, half), 2 + half, chips + 2 + half)
            else:
                for i in range(chips - 1):
                    self.pass_on(self.block(away(i, -1) * 2 + core), i, chips + i)

        def near(self):
            other = 1 - core
            if side == 2:
                self.arrived(self.block(xn * 2 + other), chips)
                self.arrived(self.block(yn * 2 + other), chips + 1)
            self.arrived(self.block(partner), 2 * chips)

        def far(self):
            other = 1 - core
            if side == 2:
                for half in range(2):
                    self.arrived(self.block(dn * 2 + other, half), chips + 2 + half)
            else:
                for i in range(chips - 1):
                    self.arrived(self.block(away(i, -1) * 2 + other), chips + i)

        def drain(self):
            for copy in self.sent:
                copy.wait_send()

    w_plane = Plane(w_ref, w_full, wrows, w_ss, w_rs)
    w_plane.start()

    def g_right(d):
        b = (h + n_head - d + 1) % n_head
        src = g_ref if d == 1 else g_full.at[b]
        return rcopy(src, g_full.at[b], g_ss.at[d - 1], g_rs.at[d - 1], s, (h + 1) % n_head)

    def g_left(d):
        b, i = (h + d - 1) % n_head, n_head - 2 + d
        src = g_ref if d == 1 else g_full.at[b]
        return rcopy(src, g_full.at[b], g_ss.at[i], g_rs.at[i], s, (h + n_head - 1) % n_head)

    def g_each(d, act):
        @pl.when(jnp.logical_and(h + 1 < n_head, h >= d - 1))
        def _():
            act(g_right(d))

        @pl.when(jnp.logical_and(h >= 1, h + d - 1 < n_head))
        def _():
            act(g_left(d))

    def g_step(d):
        @pl.when(h >= d)
        def _():
            slot = g_full.at[(h + n_head - d) % n_head]
            rcopy(slot, slot, g_ss.at[d - 1], g_rs.at[d - 1], s, (h + 1) % n_head).wait_recv()

        @pl.when(h + d < n_head)
        def _():
            slot = g_full.at[(h + d) % n_head]
            i = n_head - 2 + d
            rcopy(slot, slot, g_ss.at[i], g_rs.at[i], s, (h + 1) % n_head).wait_recv()

        if d + 1 < n_head:
            g_each(d + 1, lambda copy: copy.start())

    g_each(1, lambda copy: copy.start())

    g_full[h] = g_ref[...]
    w_full[pl.ds(pl.multiple_of(s * wrows, wrows), wrows), :] = w_ref[...]

    first = s * rows
    r_i = lax.broadcasted_iota(jnp.int32, (rows, rows), 0)
    c_i = lax.broadcasted_iota(jnp.int32, (rows, rows), 1)
    p_col = first + lax.broadcasted_iota(jnp.int32, (rows, 1), 0)
    p_row = first + lax.broadcasted_iota(jnp.int32, (1, rows), 1)
    doc_col = jnp.full((rows, 1), -1, jnp.int32)
    doc_row = jnp.full((1, rows), -1, jnp.int32)
    edges = [jnp.full((1, 1), -1, jnp.int32) for _ in range(3)]
    points = [jnp.full((1, 1), 0, jnp.int32) + p for p in (first - 1, first + rows - 1, first + rows)]
    begin = jnp.int32(0)
    for j in range(lengths.shape[0]):
        doc_col = doc_col + jnp.where(p_col >= begin, 1, 0)
        doc_row = doc_row + jnp.where(p_row >= begin, 1, 0)
        edges = [e + jnp.where(p >= begin, 1, 0) for e, p in zip(edges, points)]
        begin = begin + lengths[j]
    prev_doc, last_doc, next_doc = edges
    tri = r_i >= c_i
    eye = r_i == c_i
    joint = jnp.logical_and(tri, doc_col == doc_row)

    def lanes(i):
        return pl.ds(pl.multiple_of(i * HD, HD), HD)

    def pass1(i, carry):
        at = lanes(i)
        q, k, v = q_ref[:, at], k_ref[:, at], v_ref[:, at]
        ld = ld_ref[pl.ds(i, 1), :]
        cum = jnp.sum(jnp.where(tri, ld, 0.0), axis=1, keepdims=True)
        cum_row = jnp.sum(jnp.where(eye, cum, 0.0), axis=0, keepdims=True)
        total = cum[rows - 1 : rows, :]
        decay = jnp.where(joint, jnp.exp(jnp.where(joint, cum - cum_row, 0.0)), 0.0)
        tail = jnp.exp(total - cum)
        enter = jnp.where(doc_col == prev_doc, jnp.exp(cum), 0.0)
        keep = jnp.where(doc_col == last_doc, tail, 0.0)
        leave = jnp.where(doc_col == next_doc, tail, 0.0)
        through = jnp.where(prev_doc == last_doc, jnp.exp(total), 0.0)
        thr[i] = jnp.broadcast_to(through, (8, HD))
        enter_s[i] = jnp.broadcast_to(enter, (rows, HD))
        leave_s[i] = jnp.broadcast_to(leave, (rows, HD))
        sum_f[i] = dot((k.astype(F32) * keep).astype(BF16), v, 0, 0).astype(BF16)
        decay_s[i] = decay
        attn = (dot(q, k, 1, 1) * decay).astype(BF16)
        attn_s[i] = attn
        local[:, at] = dot(attn, v, 1, 0)
        return carry

    lax.fori_loop(0, heads, pass1, 0)

    def fwd_copy(d):
        return rcopy(sum_f, recv_f.at[d - 1], f_ss.at[d - 1], f_rs.at[d - 1], (s + d) % n_seq, h)

    def bwd_copy(d):
        return rcopy(sum_b, recv_b.at[d - 1], b_ss.at[d - 1], b_rs.at[d - 1], (s + n_seq - d) % n_seq, h)

    def thr_copies(d):
        return (
            rcopy(thr, thr_prev.at[d - 1], tp_ss.at[d - 1], tp_rs.at[d - 1], (s + d) % n_seq, h),
            rcopy(thr, thr_next.at[d - 1], tn_ss.at[d - 1], tn_rs.at[d - 1], (s + n_seq - d) % n_seq, h),
        )

    for d in range(1, hops + 1):
        fwd_copy(d).start()
        for copy in thr_copies(d):
            copy.start()
    g_step(1)
    w_plane.forward()
    for d in range(2, n_head - 1):
        g_step(d)
    for d in range(1, hops + 1):
        fwd_copy(d).wait_recv()
        for copy in thr_copies(d):
            copy.wait_recv()

    def combined(i, recv, factors, valid):
        total = jnp.zeros((HD, HD), F32)
        scale = jnp.ones((1, HD), F32)
        for d in range(1, hops + 1):
            total = total + jnp.where(valid(d), recv[d - 1, i].astype(F32) * scale, 0.0)
            scale = scale * factors[d - 1, i, 0:1, :]
        return total.astype(BF16)

    def pass2(i, carry):
        at = lanes(i)
        state = combined(i, recv_f, thr_prev, lambda d: s >= d)
        state_s[i] = state
        out = local[:, at] + dot(q_ref[:, at], state, 1, 0) * enter_s[i]
        a_full[pl.ds(pl.multiple_of(s * rows, rows), rows), at] = out.astype(BF16)
        return carry

    lax.fori_loop(0, heads, pass2, 0)

    a_plane = Plane(a_full.at[pl.ds(pl.multiple_of(s * rows, rows), rows)], a_full, rows, a_ss, a_rs)
    a_plane.start()

    per = gwidth // wrows

    def col_copy(j):
        t = (s + j) % n_seq
        src = g_full.at[t // per, :, pl.ds(pl.multiple_of((t % per) * wrows, wrows), wrows)]
        dst = g_cols.at[pl.ds(pl.multiple_of(s * rows, rows), rows)]
        return rcopy(src, dst, c_ss.at[j - 1], c_rs.at[j - 1], t, h)


    def part(target, store):
        def tile(j, carry):
            at = pl.multiple_of(target * gwidth + j * TILE, TILE)
            value = dot(
                a_full[pl.ds(pl.multiple_of(s * rows, rows), rows), :], w_full[pl.ds(at, TILE), :], 1, 1
            )
            store(pl.ds(pl.multiple_of(j * TILE, TILE), TILE), value)
            return carry

        lax.fori_loop(0, gwidth // TILE, tile, 0)

    def part_copy(j):
        return rcopy(
            part_send.at[j - 1], part_recv.at[j - 1], p_ss.at[j - 1], p_rs.at[j - 1], s, (h + j) % n_head
        )

    def send_part(target, j):
        def keep_part(at, value):
            part_send[j, :, at] = value.astype(BF16)

        part(target, keep_part)
        rcopy(part_send.at[j], part_recv.at[j], p_ss.at[j], p_rs.at[j], s, target).start()

    def send_if_other(target):
        @pl.when(target != h)
        def _():
            send_part(target, (target + n_head - h) % n_head - 1)

    by_chip = side == 2 and n_head == chips and gwidth == 2 * wrows
    w_plane.near()
    if by_chip:
        for target in (chip, xn, yn):
            send_if_other(target)
    g_step(n_head - 1)
    g_cols[pl.ds(pl.multiple_of(s * rows, rows), rows), :] = g_full[
        s // per, :, pl.ds(pl.multiple_of((s % per) * wrows, wrows), wrows)
    ]
    w_plane.finish()
    w_plane.far()
    if by_chip:
        send_if_other(dn)
    else:
        for j in range(1, n_head):
            send_part((h + j) % n_head, j - 1)

    for j in range(1, n_seq // 2):
        col_copy(j).start()

    def pull(j, carry):
        at = pl.ds(pl.multiple_of(j * TILE, TILE), TILE)
        value = jnp.zeros((rows, TILE), F32)
        for b in range(n_head):
            value = value + dot(g_full[b], w_full[b * gwidth : (b + 1) * gwidth, at], 1, 0)
        ga_s[:, at] = value.astype(BF16)
        return carry

    lax.fori_loop(0, width // TILE, pull, 0)

    def pass3(i, carry):
        at = lanes(i)
        g = ga_s[:, at]
        sum_b[i] = dot((q_ref[:, at].astype(F32) * enter_s[i]).astype(BF16), g, 0, 0).astype(BF16)
        return carry

    lax.fori_loop(0, heads, pass3, 0)

    for d in range(1, hops + 1):
        bwd_copy(d).start()
    for j in range(n_seq // 2, n_seq):
        col_copy(j).start()
    a_plane.forward()

    def own_part(at, value):
        local2[:, at] = value

    part(h, own_part)

    def pass4(i, carry):
        at = lanes(i)
        q, k, v, g = q_ref[:, at], k_ref[:, at], v_ref[:, at], ga_s[:, at]
        back = (dot(g, v, 1, 1) * decay_s[i]).astype(BF16)
        gq = dot(back, k, 1, 0) + dot(g, state_s[i], 1, 1) * enter_s[i]
        gq_ref[:, at] = gq.astype(BF16)
        local[:, at] = dot(back, q, 0, 0)
        return carry

    lax.fori_loop(0, heads, pass4, 0)

    a_plane.finish()
    for d in range(1, hops + 1):
        bwd_copy(d).wait_recv()

    def pass5(i, carry):
        at = lanes(i)
        k, v, g = k_ref[:, at], v_ref[:, at], ga_s[:, at]
        state = combined(i, recv_b, thr_next, lambda d: s + d < n_seq)
        gk = local[:, at] + dot(v, state, 1, 1) * leave_s[i]
        gv = dot(attn_s[i], g, 0, 0) + dot(k, state, 1, 0) * leave_s[i]
        gk_ref[:, at] = gk.astype(BF16)
        gv_ref[:, at] = gv.astype(BF16)
        return carry

    lax.fori_loop(0, heads, pass5, 0)

    a_plane.near()
    a_plane.far()
    for j in range(1, n_seq):
        slot = g_cols.at[pl.ds(pl.multiple_of(((s + n_seq - j) % n_seq) * rows, rows), rows)]
        rcopy(slot, slot, c_ss.at[j - 1], c_rs.at[j - 1], (s + j) % n_seq, h).wait_recv()

    mt = min(TILE, wrows)
    depth = min(2048, n_seq * rows)
    for b in range(n_seq * rows // depth):

        def outer(j, carry, b=b):
            m, n = j // (width // TILE), j % (width // TILE)
            rm = pl.ds(pl.multiple_of(m * mt, mt), mt)
            rn = pl.ds(pl.multiple_of(n * TILE, TILE), TILE)
            value = dot(
                g_cols[b * depth : (b + 1) * depth, rm], a_full[b * depth : (b + 1) * depth, rn], 0, 0
            )
            if b > 0:
                value = value + gw_ref[rm, rn]
            gw_ref[rm, rn] = value
            return carry

        lax.fori_loop(0, (wrows // mt) * (width // TILE), outer, 0)

    for j in range(1, n_head):
        part_copy(j).wait_recv()
    total = local2[...]
    for j in range(1, n_head):
        total = total + part_recv[j - 1].astype(F32)
    mixed_ref[...] = total.astype(BF16)

    w_plane.drain()
    a_plane.drain()
    for j in range(1, n_head):
        g_each(j, lambda copy: copy.wait_send())
        part_copy(j).wait_send()
    for j in range(1, n_seq):
        col_copy(j).wait_send()
    for d in range(1, hops + 1):
        fwd_copy(d).wait_send()
        bwd_copy(d).wait_send()
        for copy in thr_copies(d):
            copy.wait_send()


def square_kernel(
    n_head,
    lengths, q_ref, k_ref, v_ref, ld_ref, w_ref, g_ref,
    mixed_ref, gq_ref, gk_ref, gv_ref, gw_ref,
    w_full, g_full, g_pair, a_pair, part_send, part_recv, wg_send, wg_recv,
    local, local2, decay_s, attn_s, enter_s, leave_s, ga_s, thr,
    sum_f, raw_f, out_f, in_f, sum_b, raw_b, out_b, in_b,
    w_ss, w_rs, g_ss, g_rs, x_ss, x_rs, a_ss, a_rs, p_ss, p_rs, wg_ss, wg_rs, st_ss, st_rs,
):
    s, h = lax.axis_index("seq"), lax.axis_index("head")
    n_seq = 8
    rows, width = q_ref.shape
    heads = width // HD
    wrows = w_ref.shape[0]
    gwidth = g_ref.shape[1]
    half = wrows // 2
    chip, core = s // 2, s % 2
    other = 1 - core
    x, y = chip % 2, chip // 2
    partner = chip * 2 + other
    xn, yn, dn = y * 2 + (1 - x), (1 - y) * 2 + x, (1 - y) * 2 + (1 - x)
    sent = []

    def rcopy(src, dst, ss, rs, seq, head):
        return pltpu.make_async_remote_copy(
            src_ref=src, dst_ref=dst, send_sem=ss, recv_sem=rs,
            device_id=(seq, head), device_id_type=MESH,
        )

    def ship(src, dst, ss, rs, i, seq):
        copy = rcopy(src, dst, ss.at[i], rs.at[i], seq, h)
        copy.start()
        sent.append(copy)

    def got(ref, ss, rs, i):
        rcopy(ref, ref, ss.at[i], rs.at[i], partner, h).wait_recv()

    barrier = pltpu.get_barrier_semaphore()
    for j in range(1, n_seq):
        pl.semaphore_signal(barrier, inc=1, device_id=((s + j) % n_seq, h), device_id_type=MESH)
    for j in range(1, n_head):
        pl.semaphore_signal(barrier, inc=1, device_id=(s, (h + j) % n_head), device_id_type=MESH)
    pl.semaphore_wait(barrier, n_seq + n_head - 2)

    def w_at(seq, part):
        return w_full.at[pl.ds(pl.multiple_of(seq * wrows + part * half, half), half)]

    def w_own(part):
        return w_ref.at[pl.ds(part * half, half)]

    xs, ys = xn * 2 + core, yn * 2 + core
    ship(w_own(0), w_at(s, 0), w_ss, w_rs, 0, xs)
    ship(w_own(1), w_at(s, 1), w_ss, w_rs, 2, ys)
    ship(w_own(1), w_at(s, 1), w_ss, w_rs, 1, xs)
    ship(w_own(0), w_at(s, 0), w_ss, w_rs, 3, ys)

    def g_right(d):
        b = (h + n_head - d + 1) % n_head
        src = g_ref if d == 1 else g_full.at[b]
        return rcopy(src, g_full.at[b], g_ss.at[d - 1], g_rs.at[d - 1], s, (h + 1) % n_head)

    def g_left(d):
        b, i = (h + d - 1) % n_head, n_head - 2 + d
        src = g_ref if d == 1 else g_full.at[b]
        return rcopy(src, g_full.at[b], g_ss.at[i], g_rs.at[i], s, (h + n_head - 1) % n_head)

    def g_each(d, act):
        @pl.when(jnp.logical_and(h + 1 < n_head, h >= d - 1))
        def _():
            act(g_right(d))

        @pl.when(jnp.logical_and(h >= 1, h + d - 1 < n_head))
        def _():
            act(g_left(d))

    def core_cols(c):
        return pl.ds(pl.multiple_of(c * wrows, wrows), wrows)

    def core_rows(c):
        return pl.ds(pl.multiple_of(c * rows, rows), rows)

    def g_cross(f, src):
        return rcopy(src.at[:, core_cols(other)], g_pair.at[f, core_rows(core)], x_ss.at[f], x_rs.at[f], partner, h)

    def g_across(f):
        g_cross(f, g_full.at[f]).start()
        g_pair[f, core_rows(core), :] = g_full[f, :, core_cols(core)]

    def g_step(d):
        @pl.when(h >= d)
        def _():
            slot = g_full.at[(h + n_head - d) % n_head]
            rcopy(slot, slot, g_ss.at[d - 1], g_rs.at[d - 1], s, (h + 1) % n_head).wait_recv()

        @pl.when(h + d < n_head)
        def _():
            slot = g_full.at[(h + d) % n_head]
            i = n_head - 2 + d
            rcopy(slot, slot, g_ss.at[i], g_rs.at[i], s, (h + 1) % n_head).wait_recv()

        if d + 1 < n_head:
            g_each(d + 1, lambda copy: copy.start())

        @pl.when(h >= d)
        def _():
            g_across((h + n_head - d) % n_head)

        @pl.when(h + d < n_head)
        def _():
            g_across((h + d) % n_head)

    g_each(1, lambda copy: copy.start())
    ship(w_ref, w_full.at[pl.ds(pl.multiple_of(s * wrows, wrows), wrows)], w_ss, w_rs, 8, partner)

    g_full[h] = g_ref[...]
    g_cross(h, g_ref).start()
    g_pair[h, core_rows(core), :] = g_ref[:, core_cols(core)]
    w_full[pl.ds(pl.multiple_of(s * wrows, wrows), wrows), :] = w_ref[...]

    first = s * rows
    r_i = lax.broadcasted_iota(jnp.int32, (rows, rows), 0)
    c_i = lax.broadcasted_iota(jnp.int32, (rows, rows), 1)
    p_col = first + lax.broadcasted_iota(jnp.int32, (rows, 1), 0)
    p_row = first + lax.broadcasted_iota(jnp.int32, (1, rows), 1)
    doc_col = jnp.full((rows, 1), -1, jnp.int32)
    doc_row = jnp.full((1, rows), -1, jnp.int32)
    edges = [jnp.full((1, 1), -1, jnp.int32) for _ in range(3)]
    points = [jnp.full((1, 1), 0, jnp.int32) + p for p in (first - 1, first + rows - 1, first + rows)]
    begin = jnp.int32(0)
    for j in range(lengths.shape[0]):
        doc_col = doc_col + jnp.where(p_col >= begin, 1, 0)
        doc_row = doc_row + jnp.where(p_row >= begin, 1, 0)
        edges = [e + jnp.where(p >= begin, 1, 0) for e, p in zip(edges, points)]
        begin = begin + lengths[j]
    prev_doc, last_doc, next_doc = edges
    tri = r_i >= c_i
    eye = r_i == c_i
    joint = jnp.logical_and(tri, doc_col == doc_row)

    def lanes(i):
        return pl.ds(pl.multiple_of(i * HD, HD), HD)

    def pass1(i, carry):
        at = lanes(i)
        q, k, v = q_ref[:, at], k_ref[:, at], v_ref[:, at]
        ld = ld_ref[pl.ds(i, 1), :]
        cum = jnp.sum(jnp.where(tri, ld, 0.0), axis=1, keepdims=True)
        cum_row = jnp.sum(jnp.where(eye, cum, 0.0), axis=0, keepdims=True)
        total = cum[rows - 1 : rows, :]
        decay = jnp.where(joint, jnp.exp(jnp.where(joint, cum - cum_row, 0.0)), 0.0)
        tail = jnp.exp(total - cum)
        enter = jnp.where(doc_col == prev_doc, jnp.exp(cum), 0.0)
        keep = jnp.where(doc_col == last_doc, tail, 0.0)
        leave = jnp.where(doc_col == next_doc, tail, 0.0)
        through = jnp.where(prev_doc == last_doc, jnp.exp(total), 0.0)
        thr[i] = jnp.broadcast_to(through, (8, HD))
        enter_s[i] = jnp.broadcast_to(enter, (rows, HD))
        leave_s[i] = jnp.broadcast_to(leave, (rows, HD))
        sum_f[i] = dot((k.astype(F32) * keep).astype(BF16), v, 0, 0).astype(BF16)
        decay_s[i] = decay
        attn = (dot(q, k, 1, 1) * decay).astype(BF16)
        attn_s[i] = attn
        local[:, at] = dot(attn, v, 1, 0)
        return carry

    lax.fori_loop(0, heads, pass1, 0)

    def chain(lead, step, sums, raw, out, inn, i):
        to = (s + n_seq + step) % n_seq
        has_next = s < n_seq - 1 if step > 0 else s > 0
        has_last = s > 0 if step > 0 else s < n_seq - 1
        raw_copy = rcopy(sums, raw, st_ss.at[i], st_rs.at[i], to, h)
        out_copy = rcopy(out, inn, st_ss.at[i + 1], st_rs.at[i + 1], to, h)
        leads = core == lead

        def add(base):
            def one(j, carry):
                out[j] = (sums[j].astype(F32) + base[j].astype(F32) * thr[j, 0:1, :]).astype(BF16)
                return carry

            lax.fori_loop(0, heads, one, 0)

        def begin():
            @pl.when(leads)
            def _():
                raw_copy.start()

            @pl.when(jnp.logical_not(leads))
            def _():
                raw_copy.wait_recv()

                @pl.when(has_next)
                def _():
                    add(raw)
                    out_copy.start()

        def end():
            @pl.when(has_last)
            def _():
                out_copy.wait_recv()

            @pl.when(jnp.logical_not(has_last))
            def _():
                inn[...] = jnp.zeros_like(inn)

            @pl.when(leads)
            def _():
                add(inn)
                out_copy.start()

        def drain():
            @pl.when(leads)
            def _():
                raw_copy.wait_send()

            @pl.when(jnp.logical_or(leads, has_next))
            def _():
                out_copy.wait_send()

        return begin, end, drain

    f_begin, f_end, f_drain = chain(0, 1, sum_f, raw_f, out_f, in_f, 0)
    b_begin, b_end, b_drain = chain(1, -1, sum_b, raw_b, out_b, in_b, 2)

    f_begin()

    def w_pass(i, seq, part, ahead, to, across):
        ref = w_at(seq, part)
        got(ref, w_ss, w_rs, i)
        if ahead is not None:
            ship(ref, ref, w_ss, w_rs, ahead, to)
        ship(ref, ref, w_ss, w_rs, across, partner)

    w_pass(0, xs, 0, 4, ys, 9)
    w_pass(2, ys, 1, 5, xs, 10)
    g_step(1)

    f_end()

    def pass2(i, carry):
        at = lanes(i)
        out = local[:, at] + dot(q_ref[:, at], in_f[i], 1, 0) * enter_s[i]
        a_pair[core_rows(core), at] = out.astype(BF16)
        return carry

    lax.fori_loop(0, heads, pass2, 0)

    mine = a_pair.at[core_rows(core)]
    ship(mine, mine, a_ss, a_rs, 0, partner)

    def part(target, store):
        def tile(j, carry):
            at = pl.multiple_of(target * gwidth + j * TILE, TILE)
            value = dot(a_pair[core_rows(core), :], w_full[pl.ds(at, TILE), :], 1, 1)
            store(pl.ds(pl.multiple_of(j * TILE, TILE), TILE), value)
            return carry

        lax.fori_loop(0, gwidth // TILE, tile, 0)

    def part_copy(j):
        return rcopy(
            part_send.at[j - 1], part_recv.at[j - 1], p_ss.at[j - 1], p_rs.at[j - 1], s, (h + j) % n_head
        )

    def send_part(target, j):
        def keep_part(at, value):
            part_send[j, :, at] = value.astype(BF16)

        part(target, keep_part)
        rcopy(part_send.at[j], part_recv.at[j], p_ss.at[j], p_rs.at[j], s, target).start()

    def send_if_other(target):
        @pl.when(target != h)
        def _():
            send_part(target, (target + n_head - h) % n_head - 1)

    got(w_full.at[pl.ds(pl.multiple_of(partner * wrows, wrows), wrows)], w_ss, w_rs, 8)
    send_if_other(chip)

    w_pass(1, xs, 1, None, None, 11)
    w_pass(3, ys, 0, None, None, 12)
    g_step(2)
    xo, yo, do = xn * 2 + other, yn * 2 + other, dn * 2 + other
    got(w_at(xo, 0), w_ss, w_rs, 9)
    got(w_at(xo, 1), w_ss, w_rs, 11)
    send_if_other(xn)
    got(w_at(yo, 1), w_ss, w_rs, 10)
    got(w_at(yo, 0), w_ss, w_rs, 12)
    send_if_other(yn)
    w_pass(4, dn * 2 + core, 0, None, None, 13)
    w_pass(5, dn * 2 + core, 1, None, None, 14)
    for d in range(3, n_head):
        g_step(d)

    other_half = a_pair.at[core_rows(other)]
    got(other_half, a_ss, a_rs, 0)
    for f in range(n_head):
        slot = g_pair.at[f, core_rows(other)]
        got(slot, x_ss, x_rs, f)

    def gw_block(f, part, store):
        def tile(j, carry):
            at = pl.ds(pl.multiple_of(j * TILE, TILE), TILE)
            store(at, dot(g_pair[f, :, part * half : (part + 1) * half], a_pair[:, at], 0, 0))
            return carry

        lax.fori_loop(0, width // TILE, tile, 0)

    def send_gw(i, f, part, to, extra=None):
        def keep_gw(at, value):
            if extra is not None:
                value = value + wg_recv[extra, :, at].astype(F32)
            wg_send[i, :, at] = value.astype(BF16)

        gw_block(f, part, keep_gw)
        ship(wg_send.at[i], wg_recv.at[i], wg_ss, wg_rs, i, to)

    send_gw(0, dn, 0, xs)
    send_gw(1, dn, 1, ys)

    got(w_at(do, 0), w_ss, w_rs, 13)
    got(w_at(do, 1), w_ss, w_rs, 14)
    send_if_other(dn)
    send_gw(2, xn, 0, xs)
    send_gw(3, yn, 1, ys)

    def pull(j, carry):
        at = pl.ds(pl.multiple_of(j * TILE, TILE), TILE)
        value = jnp.zeros((rows, TILE), F32)
        for b in range(n_head):
            value = value + dot(g_full[b], w_full[b * gwidth : (b + 1) * gwidth, at], 1, 0)
        ga_s[:, at] = value.astype(BF16)
        return carry

    lax.fori_loop(0, width // TILE, pull, 0)

    def pass3(i, carry):
        at = lanes(i)
        g = ga_s[:, at]
        sum_b[i] = dot((q_ref[:, at].astype(F32) * enter_s[i]).astype(BF16), g, 0, 0).astype(BF16)
        return carry

    lax.fori_loop(0, heads, pass3, 0)
    b_begin()

    got(wg_recv.at[0], wg_ss, wg_rs, 0)
    send_gw(4, yn, 0, ys, 0)
    got(wg_recv.at[1], wg_ss, wg_rs, 1)
    send_gw(5, xn, 1, xs, 1)

    def pass4(i, carry):
        at = lanes(i)
        q, k, v, g = q_ref[:, at], k_ref[:, at], v_ref[:, at], ga_s[:, at]
        back = (dot(g, v, 1, 1) * decay_s[i]).astype(BF16)
        gq = dot(back, k, 1, 0) + dot(g, in_f[i], 1, 1) * enter_s[i]
        gq_ref[:, at] = gq.astype(BF16)
        local[:, at] = dot(back, q, 0, 0)
        return carry

    lax.fori_loop(0, heads, pass4, 0)

    b_end()

    def pass5(i, carry):
        at = lanes(i)
        k, v, g = k_ref[:, at], v_ref[:, at], ga_s[:, at]
        gk = local[:, at] + dot(v, in_b[i], 1, 1) * leave_s[i]
        gv = dot(attn_s[i], g, 0, 0) + dot(k, in_b[i], 1, 0) * leave_s[i]
        gk_ref[:, at] = gk.astype(BF16)
        gv_ref[:, at] = gv.astype(BF16)
        return carry

    lax.fori_loop(0, heads, pass5, 0)

    def own_part(at, value):
        local2[:, at] = value

    part(h, own_part)

    for p in range(2):
        got(wg_recv.at[2 + p], wg_ss, wg_rs, 2 + p)

        def keep_own(at, value, p=p):
            gw_ref[p * half : (p + 1) * half, at] = value + wg_recv[2 + p, :, at].astype(F32)

        gw_block(chip, p, keep_own)

    for j in range(1, n_head):
        part_copy(j).wait_recv()
    total = local2[...]
    for j in range(1, n_head):
        total = total + part_recv[j - 1].astype(F32)
    mixed_ref[...] = total.astype(BF16)

    for p in range(2):
        got(wg_recv.at[4 + p], wg_ss, wg_rs, 4 + p)
        at = pl.ds(p * half, half)
        gw_ref[at, :] = gw_ref[at, :] + wg_recv[4 + p].astype(F32)

    for copy in sent:
        copy.wait_send()
    for f in range(n_head):
        g_cross(f, g_full.at[f]).wait_send()
    for j in range(1, n_head):
        g_each(j, lambda copy: copy.wait_send())
        part_copy(j).wait_send()
    f_drain()
    b_drain()


def square_call(n_head, queries, keys, values, log_decay, lengths, out_weight, out_grad):
    rows, width = queries.shape
    heads = log_decay.shape[0]
    wrows = out_weight.shape[0]
    gwidth = out_grad.shape[1]
    dma = lambda n: pltpu.SemaphoreType.DMA((n,))
    vm = pltpu.VMEM
    scratch = [
        vm((8 * wrows, width), BF16),
        vm((n_head, rows, gwidth), BF16),
        vm((n_head, 2 * rows, wrows), BF16),
        vm((2 * rows, width), BF16),
        vm((n_head - 1, rows, gwidth), BF16),
        vm((n_head - 1, rows, gwidth), BF16),
        vm((6, wrows // 2, width), BF16),
        vm((6, wrows // 2, width), BF16),
        vm((rows, width), F32),
        vm((rows, gwidth), F32),
        vm((heads, rows, rows), F32),
        vm((heads, rows, rows), BF16),
        vm((heads, rows, HD), F32),
        vm((heads, rows, HD), F32),
        vm((rows, width), BF16),
        vm((heads, 8, HD), F32),
    ] + [vm((heads, HD, HD), BF16)] * 8 + [
        dma(15), dma(15), dma(2 * n_head - 2), dma(2 * n_head - 2), dma(n_head), dma(n_head), dma(1), dma(1),
        dma(n_head - 1), dma(n_head - 1), dma(6), dma(6), dma(4), dma(4),
    ]
    spec = pl.BlockSpec(memory_space=pltpu.VMEM)
    return pl.pallas_call(
        functools.partial(square_kernel, n_head),
        out_shape=[vm((rows, gwidth), BF16)] + [vm((rows, width), BF16)] * 3 + [vm((wrows, width), F32)],
        in_specs=[pl.BlockSpec(memory_space=pltpu.SMEM)] + [spec] * 6,
        out_specs=[spec] * 5,
        scratch_shapes=scratch,
        compiler_params=pltpu.CompilerParams(
            collective_id=1, has_side_effects=True, vmem_limit_bytes=61360 * 1024
        ),
    )(lengths, queries, keys, values, log_decay, out_weight, out_grad)


def body(n_seq, n_head, queries, keys, values, log_decay, lengths, out_weight, out_grad):
    rows, width = queries.shape
    heads = log_decay.shape[0]
    wrows = out_weight.shape[0]
    gwidth = out_grad.shape[1]
    chips = n_seq // 2
    longest = n_seq * rows // 4
    hops = (longest - 1) // rows + 1
    if chips == 4 and n_head == chips and gwidth == 2 * wrows and wrows % 32 == 0 and hops == 2:
        return square_call(n_head, queries, keys, values, log_decay, lengths, out_weight, out_grad)
    dma = lambda n: pltpu.SemaphoreType.DMA((n,))
    vm = pltpu.VMEM
    scratch = [
        vm((n_seq * wrows, width), BF16),
        vm((n_seq * rows, width), BF16),
        vm((n_head, rows, gwidth), BF16),
        vm((n_seq * rows, wrows), BF16),
        vm((n_head - 1, rows, gwidth), BF16),
        vm((n_head - 1, rows, gwidth), BF16),
        vm((rows, width), F32),
        vm((rows, gwidth), F32),
        vm((heads, rows, rows), F32),
        vm((heads, rows, rows), BF16),
        vm((heads, rows, HD), F32),
        vm((heads, rows, HD), F32),
        vm((heads, HD, HD), BF16),
        vm((rows, width), BF16),
        vm((heads, 8, HD), F32),
        vm((hops, heads, 8, HD), F32),
        vm((hops, heads, 8, HD), F32),
        vm((heads, HD, HD), BF16),
        vm((heads, HD, HD), BF16),
        vm((hops, heads, HD, HD), BF16),
        vm((hops, heads, HD, HD), BF16),
        dma(2 * chips + 1), dma(2 * chips + 1), dma(2 * chips + 1), dma(2 * chips + 1),
        dma(2 * n_head - 2), dma(2 * n_head - 2), dma(n_seq - 1), dma(n_seq - 1), dma(n_head - 1), dma(n_head - 1),
        dma(hops), dma(hops), dma(hops), dma(hops), dma(hops), dma(hops), dma(hops), dma(hops),
    ]
    spec = pl.BlockSpec(memory_space=pltpu.VMEM)
    return pl.pallas_call(
        functools.partial(kernel, n_seq, n_head, hops),
        out_shape=[vm((rows, gwidth), BF16)] + [vm((rows, width), BF16)] * 3 + [vm((wrows, width), F32)],
        in_specs=[pl.BlockSpec(memory_space=pltpu.SMEM)] + [spec] * 6,
        out_specs=[spec] * 5,
        scratch_shapes=scratch,
        compiler_params=pltpu.CompilerParams(
            collective_id=0, has_side_effects=True, vmem_limit_bytes=61360 * 1024
        ),
    )(lengths, queries, keys, values, log_decay, out_weight, out_grad)


def solution(mesh):
    both = P("seq", "head")
    in_specs = (both, both, both, P("head", "seq"), P(), both, both)
    return jax.shard_map(
        functools.partial(body, mesh.shape["seq"], mesh.shape["head"]),
        mesh=mesh, in_specs=in_specs, out_specs=(both,) * 5, check_vma=False,
    )
```

```python
import functools
import math

import jax
import jax.numpy as jnp
from jax import lax
from jax.experimental import pallas as pl
from jax.experimental.pallas import tpu as pltpu
from jax.sharding import PartitionSpec as P

MESH = pl.DeviceIdType.MESH
F32 = jnp.float32
BF16 = jnp.bfloat16
HD = 128
TILE = 256


def dot(a, b, ca, cb):
    return lax.dot_general(a, b, (((ca,), (cb,)), ((), ())), preferred_element_type=F32)


def kernel(
    n_seq, n_head, hops,
    lengths, q_ref, k_ref, v_ref, ld_ref, w_ref, g_ref,
    mixed_ref, gq_ref, gk_ref, gv_ref, gw_ref,
    w_full, a_full, g_full, g_cols, part_send, part_recv,
    local, local2, decay_s, attn_s, enter_s, leave_s, state_s, ga_s, thr, thr_prev, thr_next,
    sum_f, sum_b, recv_f, recv_b,
    w_ss, w_rs, a_ss, a_rs, g_ss, g_rs, c_ss, c_rs, p_ss, p_rs,
    f_ss, f_rs, b_ss, b_rs, tp_ss, tp_rs, tn_ss, tn_rs,
):
    s, h = lax.axis_index("seq"), lax.axis_index("head")
    rows, width = q_ref.shape
    heads = width // HD
    wrows = w_ref.shape[0]
    gwidth = g_ref.shape[1]
    chips = n_seq // 2
    side = math.isqrt(chips)
    chip, core = s // 2, s % 2
    x, y = chip % side, chip // side
    partner = chip * 2 + (1 - core)
    offs = [(dy, dx) for dy in range(side) for dx in range(side) if (dy, dx) != (0, 0)]

    def rcopy(src, dst, ss, rs, seq, head):
        return pltpu.make_async_remote_copy(
            src_ref=src, dst_ref=dst, send_sem=ss, recv_sem=rs,
            device_id=(seq, head), device_id_type=MESH,
        )

    def away(i, sign):
        dy, dx = offs[i]
        if sign > 0:
            return ((y + dy) % side) * side + (x + dx) % side
        return ((y + side - dy) % side) * side + (x + side - dx) % side

    barrier = pltpu.get_barrier_semaphore()
    for j in range(1, n_seq):
        pl.semaphore_signal(barrier, inc=1, device_id=((s + j) % n_seq, h), device_id_type=MESH)
    for j in range(1, n_head):
        pl.semaphore_signal(barrier, inc=1, device_id=(s, (h + j) % n_head), device_id_type=MESH)
    pl.semaphore_wait(barrier, n_seq + n_head - 2)

    xn, yn, dn = y * side + (1 - x), (1 - y) * side + x, (1 - y) * side + (1 - x)

    class Plane:
        def __init__(self, src, full, size, ss, rs):
            self.src, self.full, self.size, self.ss, self.rs = src, full, size, ss, rs
            self.sent = []

        def block(self, index, half=None):
            at, size = index * self.size, self.size
            if half is not None:
                size = self.size // 2
                at = at + half * size
            return self.full.at[pl.ds(pl.multiple_of(at, size), size)]

        def send(self, src, dst, index, seq):
            copy = rcopy(src, dst, self.ss.at[index], self.rs.at[index], seq, h)
            copy.start()
            self.sent.append(copy)

        def arrived(self, ref, index):
            rcopy(ref, ref, self.ss.at[index], self.rs.at[index], partner, h).wait_recv()

        def pass_on(self, ref, index, cross):
            self.arrived(ref, index)
            self.send(ref, ref, cross, partner)

        def start(self):
            mine = self.block(s)
            if side == 2:
                self.send(self.src, mine, 0, xn * 2 + core)
                self.send(self.src, mine, 1, yn * 2 + core)
            else:
                for i in range(chips - 1):
                    self.send(self.src, mine, i, away(i, 1) * 2 + core)
            self.send(self.src, mine, 2 * chips, partner)

        def forward(self):
            if side == 2:
                bx, by = self.block(xn * 2 + core), self.block(yn * 2 + core)
                hx, hy = self.block(xn * 2 + core, 0), self.block(yn * 2 + core, 1)
                self.arrived(bx, 0)
                self.send(hx, hx, 2, yn * 2 + core)
                self.arrived(by, 1)
                self.send(hy, hy, 3, xn * 2 + core)
                self.send(bx, bx, chips, partner)
                self.send(by, by, chips + 1, partner)

        def finish(self):
            if side == 2:
                for half in range(2):
                    self.pass_on(self.block(dn * 2 + core, half), 2 + half, chips + 2 + half)
            else:
                for i in range(chips - 1):
                    self.pass_on(self.block(away(i, -1) * 2 + core), i, chips + i)

        def near(self):
            other = 1 - core
            if side == 2:
                self.arrived(self.block(xn * 2 + other), chips)
                self.arrived(self.block(yn * 2 + other), chips + 1)
            self.arrived(self.block(partner), 2 * chips)

        def far(self):
            other = 1 - core
            if side == 2:
                for half in range(2):
                    self.arrived(self.block(dn * 2 + other, half), chips + 2 + half)
            else:
                for i in range(chips - 1):
                    self.arrived(self.block(away(i, -1) * 2 + other), chips + i)

        def drain(self):
            for copy in self.sent:
                copy.wait_send()

    w_plane = Plane(w_ref, w_full, wrows, w_ss, w_rs)
    w_plane.start()

    def g_right(d):
        b = (h + n_head - d + 1) % n_head
        src = g_ref if d == 1 else g_full.at[b]
        return rcopy(src, g_full.at[b], g_ss.at[d - 1], g_rs.at[d - 1], s, (h + 1) % n_head)

    def g_left(d):
        b, i = (h + d - 1) % n_head, n_head - 2 + d
        src = g_ref if d == 1 else g_full.at[b]
        return rcopy(src, g_full.at[b], g_ss.at[i], g_rs.at[i], s, (h + n_head - 1) % n_head)

    def g_each(d, act):
        @pl.when(jnp.logical_and(h + 1 < n_head, h >= d - 1))
        def _():
            act(g_right(d))

        @pl.when(jnp.logical_and(h >= 1, h + d - 1 < n_head))
        def _():
            act(g_left(d))

    def g_step(d):
        @pl.when(h >= d)
        def _():
            slot = g_full.at[(h + n_head - d) % n_head]
            rcopy(slot, slot, g_ss.at[d - 1], g_rs.at[d - 1], s, (h + 1) % n_head).wait_recv()

        @pl.when(h + d < n_head)
        def _():
            slot = g_full.at[(h + d) % n_head]
            i = n_head - 2 + d
            rcopy(slot, slot, g_ss.at[i], g_rs.at[i], s, (h + 1) % n_head).wait_recv()

        if d + 1 < n_head:
            g_each(d + 1, lambda copy: copy.start())

    g_each(1, lambda copy: copy.start())

    g_full[h] = g_ref[...]
    w_full[pl.ds(pl.multiple_of(s * wrows, wrows), wrows), :] = w_ref[...]

    first = s * rows
    r_i = lax.broadcasted_iota(jnp.int32, (rows, rows), 0)
    c_i = lax.broadcasted_iota(jnp.int32, (rows, rows), 1)
    p_col = first + lax.broadcasted_iota(jnp.int32, (rows, 1), 0)
    p_row = first + lax.broadcasted_iota(jnp.int32, (1, rows), 1)
    doc_col = jnp.full((rows, 1), -1, jnp.int32)
    doc_row = jnp.full((1, rows), -1, jnp.int32)
    edges = [jnp.full((1, 1), -1, jnp.int32) for _ in range(3)]
    points = [jnp.full((1, 1), 0, jnp.int32) + p for p in (first - 1, first + rows - 1, first + rows)]
    begin = jnp.int32(0)
    for j in range(lengths.shape[0]):
        doc_col = doc_col + jnp.where(p_col >= begin, 1, 0)
        doc_row = doc_row + jnp.where(p_row >= begin, 1, 0)
        edges = [e + jnp.where(p >= begin, 1, 0) for e, p in zip(edges, points)]
        begin = begin + lengths[j]
    prev_doc, last_doc, next_doc = edges
    tri = r_i >= c_i
    eye = r_i == c_i
    joint = jnp.logical_and(tri, doc_col == doc_row)

    def lanes(i):
        return pl.ds(pl.multiple_of(i * HD, HD), HD)

    def pass1(i, carry):
        at = lanes(i)
        q, k, v = q_ref[:, at], k_ref[:, at], v_ref[:, at]
        ld = ld_ref[pl.ds(i, 1), :]
        cum = jnp.sum(jnp.where(tri, ld, 0.0), axis=1, keepdims=True)
        cum_row = jnp.sum(jnp.where(eye, cum, 0.0), axis=0, keepdims=True)
        total = cum[rows - 1 : rows, :]
        decay = jnp.where(joint, jnp.exp(jnp.where(joint, cum - cum_row, 0.0)), 0.0)
        tail = jnp.exp(total - cum)
        enter = jnp.where(doc_col == prev_doc, jnp.exp(cum), 0.0)
        keep = jnp.where(doc_col == last_doc, tail, 0.0)
        leave = jnp.where(doc_col == next_doc, tail, 0.0)
        through = jnp.where(prev_doc == last_doc, jnp.exp(total), 0.0)
        thr[i] = jnp.broadcast_to(through, (8, HD))
        enter_s[i] = jnp.broadcast_to(enter, (rows, HD))
        leave_s[i] = jnp.broadcast_to(leave, (rows, HD))
        sum_f[i] = dot((k.astype(F32) * keep).astype(BF16), v, 0, 0).astype(BF16)
        decay_s[i] = decay
        attn = (dot(q, k, 1, 1) * decay).astype(BF16)
        attn_s[i] = attn
        local[:, at] = dot(attn, v, 1, 0)
        return carry

    lax.fori_loop(0, heads, pass1, 0)

    def fwd_copy(d):
        return rcopy(sum_f, recv_f.at[d - 1], f_ss.at[d - 1], f_rs.at[d - 1], (s + d) % n_seq, h)

    def bwd_copy(d):
        return rcopy(sum_b, recv_b.at[d - 1], b_ss.at[d - 1], b_rs.at[d - 1], (s + n_seq - d) % n_seq, h)

    def thr_copies(d):
        return (
            rcopy(thr, thr_prev.at[d - 1], tp_ss.at[d - 1], tp_rs.at[d - 1], (s + d) % n_seq, h),
            rcopy(thr, thr_next.at[d - 1], tn_ss.at[d - 1], tn_rs.at[d - 1], (s + n_seq - d) % n_seq, h),
        )

    for d in range(1, hops + 1):
        fwd_copy(d).start()
        for copy in thr_copies(d):
            copy.start()
    g_step(1)
    w_plane.forward()
    for d in range(2, n_head - 1):
        g_step(d)
    for d in range(1, hops + 1):
        fwd_copy(d).wait_recv()
        for copy in thr_copies(d):
            copy.wait_recv()

    def combined(i, recv, factors, valid):
        total = jnp.zeros((HD, HD), F32)
        scale = jnp.ones((1, HD), F32)
        for d in range(1, hops + 1):
            total = total + jnp.where(valid(d), recv[d - 1, i].astype(F32) * scale, 0.0)
            scale = scale * factors[d - 1, i, 0:1, :]
        return total.astype(BF16)

    def pass2(i, carry):
        at = lanes(i)
        state = combined(i, recv_f, thr_prev, lambda d: s >= d)
        state_s[i] = state
        out = local[:, at] + dot(q_ref[:, at], state, 1, 0) * enter_s[i]
        a_full[pl.ds(pl.multiple_of(s * rows, rows), rows), at] = out.astype(BF16)
        return carry

    lax.fori_loop(0, heads, pass2, 0)

    a_plane = Plane(a_full.at[pl.ds(pl.multiple_of(s * rows, rows), rows)], a_full, rows, a_ss, a_rs)
    a_plane.start()

    per = gwidth // wrows

    def col_copy(j):
        t = (s + j) % n_seq
        src = g_full.at[t // per, :, pl.ds(pl.multiple_of((t % per) * wrows, wrows), wrows)]
        dst = g_cols.at[pl.ds(pl.multiple_of(s * rows, rows), rows)]
        return rcopy(src, dst, c_ss.at[j - 1], c_rs.at[j - 1], t, h)


    def part(target, store):
        def tile(j, carry):
            at = pl.multiple_of(target * gwidth + j * TILE, TILE)
            value = dot(
                a_full[pl.ds(pl.multiple_of(s * rows, rows), rows), :], w_full[pl.ds(at, TILE), :], 1, 1
            )
            store(pl.ds(pl.multiple_of(j * TILE, TILE), TILE), value)
            return carry

        lax.fori_loop(0, gwidth // TILE, tile, 0)

    def part_copy(j):
        return rcopy(
            part_send.at[j - 1], part_recv.at[j - 1], p_ss.at[j - 1], p_rs.at[j - 1], s, (h + j) % n_head
        )

    def send_part(target, j):
        def keep_part(at, value):
            part_send[j, :, at] = value.astype(BF16)

        part(target, keep_part)
        rcopy(part_send.at[j], part_recv.at[j], p_ss.at[j], p_rs.at[j], s, target).start()

    def send_if_other(target):
        @pl.when(target != h)
        def _():
            send_part(target, (target + n_head - h) % n_head - 1)

    by_chip = side == 2 and n_head == chips and gwidth == 2 * wrows
    w_plane.near()
    if by_chip:
        for target in (chip, xn, yn):
            send_if_other(target)
    g_step(n_head - 1)
    g_cols[pl.ds(pl.multiple_of(s * rows, rows), rows), :] = g_full[
        s // per, :, pl.ds(pl.multiple_of((s % per) * wrows, wrows), wrows)
    ]
    w_plane.finish()
    w_plane.far()
    if by_chip:
        send_if_other(dn)
    else:
        for j in range(1, n_head):
            send_part((h + j) % n_head, j - 1)

    for j in range(1, n_seq // 2):
        col_copy(j).start()

    def pull(j, carry):
        at = pl.ds(pl.multiple_of(j * TILE, TILE), TILE)
        value = jnp.zeros((rows, TILE), F32)
        for b in range(n_head):
            value = value + dot(g_full[b], w_full[b * gwidth : (b + 1) * gwidth, at], 1, 0)
        ga_s[:, at] = value.astype(BF16)
        return carry

    lax.fori_loop(0, width // TILE, pull, 0)

    def pass3(i, carry):
        at = lanes(i)
        g = ga_s[:, at]
        sum_b[i] = dot((q_ref[:, at].astype(F32) * enter_s[i]).astype(BF16), g, 0, 0).astype(BF16)
        return carry

    lax.fori_loop(0, heads, pass3, 0)

    for d in range(1, hops + 1):
        bwd_copy(d).start()
    for j in range(n_seq // 2, n_seq):
        col_copy(j).start()
    a_plane.forward()

    def own_part(at, value):
        local2[:, at] = value

    part(h, own_part)

    def pass4(i, carry):
        at = lanes(i)
        q, k, v, g = q_ref[:, at], k_ref[:, at], v_ref[:, at], ga_s[:, at]
        back = (dot(g, v, 1, 1) * decay_s[i]).astype(BF16)
        gq = dot(back, k, 1, 0) + dot(g, state_s[i], 1, 1) * enter_s[i]
        gq_ref[:, at] = gq.astype(BF16)
        local[:, at] = dot(back, q, 0, 0)
        return carry

    lax.fori_loop(0, heads, pass4, 0)

    a_plane.finish()
    for d in range(1, hops + 1):
        bwd_copy(d).wait_recv()

    def pass5(i, carry):
        at = lanes(i)
        k, v, g = k_ref[:, at], v_ref[:, at], ga_s[:, at]
        state = combined(i, recv_b, thr_next, lambda d: s + d < n_seq)
        gk = local[:, at] + dot(v, state, 1, 1) * leave_s[i]
        gv = dot(attn_s[i], g, 0, 0) + dot(k, state, 1, 0) * leave_s[i]
        gk_ref[:, at] = gk.astype(BF16)
        gv_ref[:, at] = gv.astype(BF16)
        return carry

    lax.fori_loop(0, heads, pass5, 0)

    a_plane.near()
    a_plane.far()
    for j in range(1, n_seq):
        slot = g_cols.at[pl.ds(pl.multiple_of(((s + n_seq - j) % n_seq) * rows, rows), rows)]
        rcopy(slot, slot, c_ss.at[j - 1], c_rs.at[j - 1], (s + j) % n_seq, h).wait_recv()

    mt = min(TILE, wrows)
    depth = min(2048, n_seq * rows)
    for b in range(n_seq * rows // depth):

        def outer(j, carry, b=b):
            m, n = j // (width // TILE), j % (width // TILE)
            rm = pl.ds(pl.multiple_of(m * mt, mt), mt)
            rn = pl.ds(pl.multiple_of(n * TILE, TILE), TILE)
            value = dot(
                g_cols[b * depth : (b + 1) * depth, rm], a_full[b * depth : (b + 1) * depth, rn], 0, 0
            )
            if b > 0:
                value = value + gw_ref[rm, rn]
            gw_ref[rm, rn] = value
            return carry

        lax.fori_loop(0, (wrows // mt) * (width // TILE), outer, 0)

    for j in range(1, n_head):
        part_copy(j).wait_recv()
    total = local2[...]
    for j in range(1, n_head):
        total = total + part_recv[j - 1].astype(F32)
    mixed_ref[...] = total.astype(BF16)

    w_plane.drain()
    a_plane.drain()
    for j in range(1, n_head):
        g_each(j, lambda copy: copy.wait_send())
        part_copy(j).wait_send()
    for j in range(1, n_seq):
        col_copy(j).wait_send()
    for d in range(1, hops + 1):
        fwd_copy(d).wait_send()
        bwd_copy(d).wait_send()
        for copy in thr_copies(d):
            copy.wait_send()


def square_kernel(
    n_head,
    lengths, q_ref, k_ref, v_ref, ld_ref, w_ref, g_ref,
    mixed_ref, gq_ref, gk_ref, gv_ref, gw_ref,
    w_full, g_full, g_pair, a_pair, z_send, near, fold, merged, wg_send, wg_recv,
    local, local2, decay_s, attn_s, enter_s, leave_s, ga_s, thr,
    sum_f, raw_f, out_f, in_f, sum_b, raw_b, out_b, in_b,
    w_ss, w_rs, g_ss, g_rs, x_ss, x_rs, a_ss, a_rs, z_ss, n_rs, f_rs, m_rs, wg_ss, wg_rs, st_ss, st_rs,
):
    s, h = lax.axis_index("seq"), lax.axis_index("head")
    n_seq = 8
    rows, width = q_ref.shape
    heads = width // HD
    wrows = w_ref.shape[0]
    gwidth = g_ref.shape[1]
    half = wrows // 2
    chip, core = s // 2, s % 2
    other = 1 - core
    x, y = chip % 2, chip // 2
    partner = chip * 2 + other
    xn, yn, dn = y * 2 + (1 - x), (1 - y) * 2 + x, (1 - y) * 2 + (1 - x)
    sent = []

    def rcopy(src, dst, ss, rs, seq, head):
        return pltpu.make_async_remote_copy(
            src_ref=src, dst_ref=dst, send_sem=ss, recv_sem=rs,
            device_id=(seq, head), device_id_type=MESH,
        )

    def ship(src, dst, ss, rs, i, seq):
        copy = rcopy(src, dst, ss.at[i], rs.at[i], seq, h)
        copy.start()
        sent.append(copy)

    def got(ref, ss, rs, i):
        rcopy(ref, ref, ss.at[i], rs.at[i], partner, h).wait_recv()

    barrier = pltpu.get_barrier_semaphore()
    for j in range(1, n_seq):
        pl.semaphore_signal(barrier, inc=1, device_id=((s + j) % n_seq, h), device_id_type=MESH)
    for j in range(1, n_head):
        pl.semaphore_signal(barrier, inc=1, device_id=(s, (h + j) % n_head), device_id_type=MESH)
    pl.semaphore_wait(barrier, n_seq + n_head - 2)

    def w_at(seq, part):
        return w_full.at[pl.ds(pl.multiple_of(seq * wrows + part * half, half), half)]

    def w_own(part):
        return w_ref.at[pl.ds(part * half, half)]

    xs, ys = xn * 2 + core, yn * 2 + core
    ship(w_own(0), w_at(s, 0), w_ss, w_rs, 0, xs)
    ship(w_own(1), w_at(s, 1), w_ss, w_rs, 2, ys)

    def g_right(d):
        b = (h + n_head - d + 1) % n_head
        src = g_ref if d == 1 else g_full.at[b]
        return rcopy(src, g_full.at[b], g_ss.at[d - 1], g_rs.at[d - 1], s, (h + 1) % n_head)

    def g_left(d):
        b, i = (h + d - 1) % n_head, n_head - 2 + d
        src = g_ref if d == 1 else g_full.at[b]
        return rcopy(src, g_full.at[b], g_ss.at[i], g_rs.at[i], s, (h + n_head - 1) % n_head)

    def g_each(d, act):
        @pl.when(jnp.logical_and(h + 1 < n_head, h >= d - 1))
        def _():
            act(g_right(d))

        @pl.when(jnp.logical_and(h >= 1, h + d - 1 < n_head))
        def _():
            act(g_left(d))

    def core_cols(c):
        return pl.ds(pl.multiple_of(c * wrows, wrows), wrows)

    def core_rows(c):
        return pl.ds(pl.multiple_of(c * rows, rows), rows)

    def g_cross(f, src):
        return rcopy(src.at[:, core_cols(other)], g_pair.at[f, core_rows(core)], x_ss.at[f], x_rs.at[f], partner, h)

    def g_across(f):
        g_cross(f, g_full.at[f]).start()
        g_pair[f, core_rows(core), :] = g_full[f, :, core_cols(core)]

    def g_step(d):
        @pl.when(h >= d)
        def _():
            slot = g_full.at[(h + n_head - d) % n_head]
            rcopy(slot, slot, g_ss.at[d - 1], g_rs.at[d - 1], s, (h + 1) % n_head).wait_recv()

        @pl.when(h + d < n_head)
        def _():
            slot = g_full.at[(h + d) % n_head]
            i = n_head - 2 + d
            rcopy(slot, slot, g_ss.at[i], g_rs.at[i], s, (h + 1) % n_head).wait_recv()

        if d + 1 < n_head:
            g_each(d + 1, lambda copy: copy.start())

        @pl.when(h >= d)
        def _():
            g_across((h + n_head - d) % n_head)

        @pl.when(h + d < n_head)
        def _():
            g_across((h + d) % n_head)

    g_each(1, lambda copy: copy.start())
    ship(w_ref, w_full.at[pl.ds(pl.multiple_of(s * wrows, wrows), wrows)], w_ss, w_rs, 8, partner)

    g_full[h] = g_ref[...]
    g_cross(h, g_ref).start()
    g_pair[h, core_rows(core), :] = g_ref[:, core_cols(core)]
    w_full[pl.ds(pl.multiple_of(s * wrows, wrows), wrows), :] = w_ref[...]

    first = s * rows
    r_i = lax.broadcasted_iota(jnp.int32, (rows, rows), 0)
    c_i = lax.broadcasted_iota(jnp.int32, (rows, rows), 1)
    p_col = first + lax.broadcasted_iota(jnp.int32, (rows, 1), 0)
    p_row = first + lax.broadcasted_iota(jnp.int32, (1, rows), 1)
    doc_col = jnp.full((rows, 1), -1, jnp.int32)
    doc_row = jnp.full((1, rows), -1, jnp.int32)
    edges = [jnp.full((1, 1), -1, jnp.int32) for _ in range(3)]
    points = [jnp.full((1, 1), 0, jnp.int32) + p for p in (first - 1, first + rows - 1, first + rows)]
    begin = jnp.int32(0)
    for j in range(lengths.shape[0]):
        doc_col = doc_col + jnp.where(p_col >= begin, 1, 0)
        doc_row = doc_row + jnp.where(p_row >= begin, 1, 0)
        edges = [e + jnp.where(p >= begin, 1, 0) for e, p in zip(edges, points)]
        begin = begin + lengths[j]
    prev_doc, last_doc, next_doc = edges
    tri = r_i >= c_i
    eye = r_i == c_i
    joint = jnp.logical_and(tri, doc_col == doc_row)

    def lanes(i):
        return pl.ds(pl.multiple_of(i * HD, HD), HD)

    def pass1(i, carry):
        at = lanes(i)
        q, k, v = q_ref[:, at], k_ref[:, at], v_ref[:, at]
        ld = ld_ref[pl.ds(i, 1), :]
        cum = jnp.sum(jnp.where(tri, ld, 0.0), axis=1, keepdims=True)
        cum_row = jnp.sum(jnp.where(eye, cum, 0.0), axis=0, keepdims=True)
        total = cum[rows - 1 : rows, :]
        decay = jnp.where(joint, jnp.exp(jnp.where(joint, cum - cum_row, 0.0)), 0.0)
        tail = jnp.exp(total - cum)
        enter = jnp.where(doc_col == prev_doc, jnp.exp(cum), 0.0)
        keep = jnp.where(doc_col == last_doc, tail, 0.0)
        leave = jnp.where(doc_col == next_doc, tail, 0.0)
        through = jnp.where(prev_doc == last_doc, jnp.exp(total), 0.0)
        thr[i] = jnp.broadcast_to(through, (8, HD))
        enter_s[i] = jnp.broadcast_to(enter, (rows, HD))
        leave_s[i] = jnp.broadcast_to(leave, (rows, HD))
        sum_f[i] = dot((k.astype(F32) * keep).astype(BF16), v, 0, 0).astype(BF16)
        decay_s[i] = decay
        attn = (dot(q, k, 1, 1) * decay).astype(BF16)
        attn_s[i] = attn
        local[:, at] = dot(attn, v, 1, 0)
        return carry

    lax.fori_loop(0, heads, pass1, 0)

    def chain(lead, step, sums, raw, out, inn, i):
        to = (s + n_seq + step) % n_seq
        has_next = s < n_seq - 1 if step > 0 else s > 0
        has_last = s > 0 if step > 0 else s < n_seq - 1
        raw_copy = rcopy(sums, raw, st_ss.at[i], st_rs.at[i], to, h)
        out_copy = rcopy(out, inn, st_ss.at[i + 1], st_rs.at[i + 1], to, h)
        leads = core == lead

        def add(base):
            def one(j, carry):
                out[j] = (sums[j].astype(F32) + base[j].astype(F32) * thr[j, 0:1, :]).astype(BF16)
                return carry

            lax.fori_loop(0, heads, one, 0)

        def begin():
            @pl.when(leads)
            def _():
                raw_copy.start()

            @pl.when(jnp.logical_not(leads))
            def _():
                raw_copy.wait_recv()

                @pl.when(has_next)
                def _():
                    add(raw)
                    out_copy.start()

        def end():
            @pl.when(has_last)
            def _():
                out_copy.wait_recv()

            @pl.when(jnp.logical_not(has_last))
            def _():
                inn[...] = jnp.zeros_like(inn)

            @pl.when(leads)
            def _():
                add(inn)
                out_copy.start()

        def drain():
            @pl.when(leads)
            def _():
                raw_copy.wait_send()

            @pl.when(jnp.logical_or(leads, has_next))
            def _():
                out_copy.wait_send()

        return begin, end, drain

    f_begin, f_end, f_drain = chain(0, 1, sum_f, raw_f, out_f, in_f, 0)
    b_begin, b_end, b_drain = chain(1, -1, sum_b, raw_b, out_b, in_b, 2)

    f_begin()
    ship(w_own(1), w_at(s, 1), w_ss, w_rs, 1, xs)
    ship(w_own(0), w_at(s, 0), w_ss, w_rs, 3, ys)

    def w_pass(i, seq, part, ahead, to, across):
        ref = w_at(seq, part)
        got(ref, w_ss, w_rs, i)
        if ahead is not None:
            ship(ref, ref, w_ss, w_rs, ahead, to)
        ship(ref, ref, w_ss, w_rs, across, partner)

    w_pass(0, xs, 0, 4, ys, 9)
    w_pass(2, ys, 1, 5, xs, 10)
    g_step(1)

    f_end()

    def pass2(i, carry):
        at = lanes(i)
        out = local[:, at] + dot(q_ref[:, at], in_f[i], 1, 0) * enter_s[i]
        a_pair[core_rows(core), at] = out.astype(BF16)
        return carry

    lax.fori_loop(0, heads, pass2, 0)

    mine = a_pair.at[core_rows(core)]
    ship(mine, mine, a_ss, a_rs, 0, partner)

    inner = jnp.logical_and(h > 0, h < n_head - 1)
    mate = h + 1 - 2 * (h % 2)

    def part(target, p, store):
        def tile(c, carry):
            at = pl.multiple_of(target * gwidth + c * wrows + p * half, half)
            value = dot(a_pair[core_rows(core), :], w_full[pl.ds(at, half), :], 1, 1)
            store(c, value)
            return carry

        lax.fori_loop(0, gwidth // wrows, tile, 0)

    def chunk_cols(c):
        return pl.ds(pl.multiple_of(c * half, half), half)

    def z_copy(b, p, dst, rs, to):
        return rcopy(z_send.at[b, p], dst, z_ss.at[b * 2 + p], rs, s, to)

    def z_near(b, p):
        z_copy(b, p, near.at[p], n_rs.at[p], mate).start()

    def z_fold(b, p):
        return z_copy(b, p, fold.at[b % 2, p], f_rs.at[(b % 2) * 2 + p], mate)

    def make_parts(chunks):
        for b, p in chunks:

            @pl.when(b != h)
            def _(b=b, p=p):
                def keep_part(c, value):
                    z_send[b, p, :, chunk_cols(c)] = value.astype(BF16)

                part(b, p, keep_part)

            @pl.when(jnp.logical_and(jnp.logical_not(inner), b == mate))
            def _(b=b, p=p):
                z_near(b, p)

            @pl.when(jnp.logical_and(jnp.logical_not(inner), jnp.logical_and(b != h, b != mate)))
            def _(b=b, p=p):
                z_fold(b, p).start()

    def pass_parts(chunks):
        for b, p in chunks:

            @pl.when(jnp.logical_and(inner, b == mate))
            def _(b=b, p=p):
                z_near(b, p)

            @pl.when(jnp.logical_and(inner, jnp.logical_and(b != h, b != mate)))
            def _(b=b, p=p):
                z_fold(b, p).wait_recv()
                z_send[b, p] = (z_send[b, p].astype(F32) + fold[b % 2, p].astype(F32)).astype(BF16)
                z_copy(b, p, merged.at[p], m_rs.at[p], b).start()

    xo, yo, do = xn * 2 + other, yn * 2 + other, dn * 2 + other
    got(w_full.at[pl.ds(pl.multiple_of(partner * wrows, wrows), wrows)], w_ss, w_rs, 8)
    got(w_at(xo, 0), w_ss, w_rs, 9)
    got(w_at(yo, 1), w_ss, w_rs, 10)
    early = [(chip, 0), (chip, 1), (xn, 0), (yn, 1)]
    make_parts(early)

    w_pass(1, xs, 1, None, None, 11)
    w_pass(3, ys, 0, None, None, 12)
    g_step(2)
    got(w_at(xo, 1), w_ss, w_rs, 11)
    got(w_at(yo, 0), w_ss, w_rs, 12)
    middle = [(xn, 1), (yn, 0)]
    make_parts(middle)
    w_pass(4, dn * 2 + core, 0, None, None, 13)
    w_pass(5, dn * 2 + core, 1, None, None, 14)
    for d in range(3, n_head):
        g_step(d)

    other_half = a_pair.at[core_rows(other)]
    got(other_half, a_ss, a_rs, 0)
    for f in range(n_head):
        slot = g_pair.at[f, core_rows(other)]
        got(slot, x_ss, x_rs, f)

    def gw_block(f, part, store):
        def tile(j, carry):
            at = pl.ds(pl.multiple_of(j * TILE, TILE), TILE)
            store(at, dot(g_pair[f, :, part * half : (part + 1) * half], a_pair[:, at], 0, 0))
            return carry

        lax.fori_loop(0, width // TILE, tile, 0)

    def send_gw(i, f, part, to, extra=None):
        def keep_gw(at, value):
            if extra is not None:
                value = value + wg_recv[extra, :, at].astype(F32)
            wg_send[i, :, at] = value.astype(BF16)

        gw_block(f, part, keep_gw)
        ship(wg_send.at[i], wg_recv.at[i], wg_ss, wg_rs, i, to)

    send_gw(0, dn, 0, xs)
    send_gw(1, dn, 1, ys)

    got(w_at(do, 0), w_ss, w_rs, 13)
    got(w_at(do, 1), w_ss, w_rs, 14)
    late = [(dn, 0), (dn, 1)]
    make_parts(late)
    send_gw(2, xn, 0, xs)
    send_gw(3, yn, 1, ys)
    pass_parts(early)

    def pull(j, carry):
        at = pl.ds(pl.multiple_of(j * TILE, TILE), TILE)
        value = jnp.zeros((rows, TILE), F32)
        for b in range(n_head):
            value = value + dot(g_full[b], w_full[b * gwidth : (b + 1) * gwidth, at], 1, 0)
        ga_s[:, at] = value.astype(BF16)
        return carry

    lax.fori_loop(0, width // TILE, pull, 0)

    def pass3(i, carry):
        at = lanes(i)
        g = ga_s[:, at]
        sum_b[i] = dot((q_ref[:, at].astype(F32) * enter_s[i]).astype(BF16), g, 0, 0).astype(BF16)
        return carry

    lax.fori_loop(0, heads, pass3, 0)
    b_begin()

    got(wg_recv.at[0], wg_ss, wg_rs, 0)
    send_gw(4, yn, 0, ys, 0)
    got(wg_recv.at[1], wg_ss, wg_rs, 1)
    send_gw(5, xn, 1, xs, 1)
    pass_parts(middle + late)

    def pass4(i, carry):
        at = lanes(i)
        q, k, v, g = q_ref[:, at], k_ref[:, at], v_ref[:, at], ga_s[:, at]
        back = (dot(g, v, 1, 1) * decay_s[i]).astype(BF16)
        gq = dot(back, k, 1, 0) + dot(g, in_f[i], 1, 1) * enter_s[i]
        gq_ref[:, at] = gq.astype(BF16)
        local[:, at] = dot(back, q, 0, 0)
        return carry

    lax.fori_loop(0, heads, pass4, 0)

    b_end()

    def pass5(i, carry):
        at = lanes(i)
        k, v, g = k_ref[:, at], v_ref[:, at], ga_s[:, at]
        gk = local[:, at] + dot(v, in_b[i], 1, 1) * leave_s[i]
        gv = dot(attn_s[i], g, 0, 0) + dot(k, in_b[i], 1, 0) * leave_s[i]
        gk_ref[:, at] = gk.astype(BF16)
        gv_ref[:, at] = gv.astype(BF16)
        return carry

    lax.fori_loop(0, heads, pass5, 0)

    for p in range(2):

        def own_part(c, value, p=p):
            local2[:, pl.ds(pl.multiple_of(c * wrows + p * half, half), half)] = value

        part(h, p, own_part)

    for p in range(2):
        got(wg_recv.at[2 + p], wg_ss, wg_rs, 2 + p)

        def keep_own(at, value, p=p):
            gw_ref[p * half : (p + 1) * half, at] = value + wg_recv[2 + p, :, at].astype(F32)

        gw_block(chip, p, keep_own)

    for p in range(2):
        rcopy(near.at[p], near.at[p], z_ss.at[0], n_rs.at[p], s, mate).wait_recv()
        rcopy(merged.at[p], merged.at[p], z_ss.at[0], m_rs.at[p], s, mate).wait_recv()
        for c in range(gwidth // wrows):
            at, cols = pl.ds(c * wrows + p * half, half), pl.ds(c * half, half)
            total = local2[:, at] + near[p, :, cols].astype(F32) + merged[p, :, cols].astype(F32)
            mixed_ref[:, at] = total.astype(BF16)

    for p in range(2):
        got(wg_recv.at[4 + p], wg_ss, wg_rs, 4 + p)
        at = pl.ds(p * half, half)
        gw_ref[at, :] = gw_ref[at, :] + wg_recv[4 + p].astype(F32)

    for copy in sent:
        copy.wait_send()
    for f in range(n_head):
        g_cross(f, g_full.at[f]).wait_send()
    for j in range(1, n_head):
        g_each(j, lambda copy: copy.wait_send())
        for p in range(2):
            z_copy((h + j) % n_head, p, near.at[p], n_rs.at[p], mate).wait_send()
    f_drain()
    b_drain()


def square_call(n_head, queries, keys, values, log_decay, lengths, out_weight, out_grad):
    rows, width = queries.shape
    heads = log_decay.shape[0]
    wrows = out_weight.shape[0]
    gwidth = out_grad.shape[1]
    dma = lambda n: pltpu.SemaphoreType.DMA((n,))
    vm = pltpu.VMEM
    scratch = [
        vm((8 * wrows, width), BF16),
        vm((n_head, rows, gwidth), BF16),
        vm((n_head, 2 * rows, wrows), BF16),
        vm((2 * rows, width), BF16),
        vm((n_head, 2, rows, wrows), BF16),
        vm((2, rows, wrows), BF16),
        vm((2, 2, rows, wrows), BF16),
        vm((2, rows, wrows), BF16),
        vm((6, wrows // 2, width), BF16),
        vm((6, wrows // 2, width), BF16),
        vm((rows, width), F32),
        vm((rows, gwidth), F32),
        vm((heads, rows, rows), F32),
        vm((heads, rows, rows), BF16),
        vm((heads, rows, HD), F32),
        vm((heads, rows, HD), F32),
        vm((rows, width), BF16),
        vm((heads, 8, HD), F32),
    ] + [vm((heads, HD, HD), BF16)] * 8 + [
        dma(15), dma(15), dma(2 * n_head - 2), dma(2 * n_head - 2), dma(n_head), dma(n_head), dma(1), dma(1),
        dma(2 * n_head), dma(2), dma(4), dma(2), dma(6), dma(6), dma(4), dma(4),
    ]
    spec = pl.BlockSpec(memory_space=pltpu.VMEM)
    return pl.pallas_call(
        functools.partial(square_kernel, n_head),
        out_shape=[vm((rows, gwidth), BF16)] + [vm((rows, width), BF16)] * 3 + [vm((wrows, width), F32)],
        in_specs=[pl.BlockSpec(memory_space=pltpu.SMEM)] + [spec] * 6,
        out_specs=[spec] * 5,
        scratch_shapes=scratch,
        compiler_params=pltpu.CompilerParams(
            collective_id=1, has_side_effects=True, vmem_limit_bytes=61360 * 1024
        ),
    )(lengths, queries, keys, values, log_decay, out_weight, out_grad)


def body(n_seq, n_head, queries, keys, values, log_decay, lengths, out_weight, out_grad):
    rows, width = queries.shape
    heads = log_decay.shape[0]
    wrows = out_weight.shape[0]
    gwidth = out_grad.shape[1]
    chips = n_seq // 2
    longest = n_seq * rows // 4
    hops = (longest - 1) // rows + 1
    if chips == 4 and n_head == 4 and gwidth == 2 * wrows and wrows % 32 == 0 and hops == 2:
        return square_call(n_head, queries, keys, values, log_decay, lengths, out_weight, out_grad)
    dma = lambda n: pltpu.SemaphoreType.DMA((n,))
    vm = pltpu.VMEM
    scratch = [
        vm((n_seq * wrows, width), BF16),
        vm((n_seq * rows, width), BF16),
        vm((n_head, rows, gwidth), BF16),
        vm((n_seq * rows, wrows), BF16),
        vm((n_head - 1, rows, gwidth), BF16),
        vm((n_head - 1, rows, gwidth), BF16),
        vm((rows, width), F32),
        vm((rows, gwidth), F32),
        vm((heads, rows, rows), F32),
        vm((heads, rows, rows), BF16),
        vm((heads, rows, HD), F32),
        vm((heads, rows, HD), F32),
        vm((heads, HD, HD), BF16),
        vm((rows, width), BF16),
        vm((heads, 8, HD), F32),
        vm((hops, heads, 8, HD), F32),
        vm((hops, heads, 8, HD), F32),
        vm((heads, HD, HD), BF16),
        vm((heads, HD, HD), BF16),
        vm((hops, heads, HD, HD), BF16),
        vm((hops, heads, HD, HD), BF16),
        dma(2 * chips + 1), dma(2 * chips + 1), dma(2 * chips + 1), dma(2 * chips + 1),
        dma(2 * n_head - 2), dma(2 * n_head - 2), dma(n_seq - 1), dma(n_seq - 1), dma(n_head - 1), dma(n_head - 1),
        dma(hops), dma(hops), dma(hops), dma(hops), dma(hops), dma(hops), dma(hops), dma(hops),
    ]
    spec = pl.BlockSpec(memory_space=pltpu.VMEM)
    return pl.pallas_call(
        functools.partial(kernel, n_seq, n_head, hops),
        out_shape=[vm((rows, gwidth), BF16)] + [vm((rows, width), BF16)] * 3 + [vm((wrows, width), F32)],
        in_specs=[pl.BlockSpec(memory_space=pltpu.SMEM)] + [spec] * 6,
        out_specs=[spec] * 5,
        scratch_shapes=scratch,
        compiler_params=pltpu.CompilerParams(
            collective_id=0, has_side_effects=True, vmem_limit_bytes=61360 * 1024
        ),
    )(lengths, queries, keys, values, log_decay, out_weight, out_grad)


def solution(mesh):
    both = P("seq", "head")
    in_specs = (both, both, both, P("head", "seq"), P(), both, both)
    return jax.shard_map(
        functools.partial(body, mesh.shape["seq"], mesh.shape["head"]),
        mesh=mesh, in_specs=in_specs, out_specs=(both,) * 5, check_vma=False,
    )
```

```python
import functools
import math

import jax
import jax.numpy as jnp
from jax import lax
from jax.experimental import pallas as pl
from jax.experimental.pallas import tpu as pltpu
from jax.sharding import PartitionSpec as P

MESH = pl.DeviceIdType.MESH
F32 = jnp.float32
BF16 = jnp.bfloat16
HD = 128
TILE = 256


def dot(a, b, ca, cb):
    return lax.dot_general(a, b, (((ca,), (cb,)), ((), ())), preferred_element_type=F32)


def kernel(
    n_seq, n_head, hops,
    lengths, q_ref, k_ref, v_ref, ld_ref, w_ref, g_ref,
    mixed_ref, gq_ref, gk_ref, gv_ref, gw_ref,
    w_full, a_full, g_full, g_cols, part_send, part_recv,
    local, local2, decay_s, attn_s, enter_s, leave_s, state_s, ga_s, thr, thr_prev, thr_next,
    sum_f, sum_b, recv_f, recv_b,
    w_ss, w_rs, a_ss, a_rs, g_ss, g_rs, c_ss, c_rs, p_ss, p_rs,
    f_ss, f_rs, b_ss, b_rs, tp_ss, tp_rs, tn_ss, tn_rs,
):
    s, h = lax.axis_index("seq"), lax.axis_index("head")
    rows, width = q_ref.shape
    heads = width // HD
    wrows = w_ref.shape[0]
    gwidth = g_ref.shape[1]
    chips = n_seq // 2
    side = math.isqrt(chips)
    chip, core = s // 2, s % 2
    x, y = chip % side, chip // side
    partner = chip * 2 + (1 - core)
    offs = [(dy, dx) for dy in range(side) for dx in range(side) if (dy, dx) != (0, 0)]

    def rcopy(src, dst, ss, rs, seq, head):
        return pltpu.make_async_remote_copy(
            src_ref=src, dst_ref=dst, send_sem=ss, recv_sem=rs,
            device_id=(seq, head), device_id_type=MESH,
        )

    def away(i, sign):
        dy, dx = offs[i]
        if sign > 0:
            return ((y + dy) % side) * side + (x + dx) % side
        return ((y + side - dy) % side) * side + (x + side - dx) % side

    barrier = pltpu.get_barrier_semaphore()
    for j in range(1, n_seq):
        pl.semaphore_signal(barrier, inc=1, device_id=((s + j) % n_seq, h), device_id_type=MESH)
    for j in range(1, n_head):
        pl.semaphore_signal(barrier, inc=1, device_id=(s, (h + j) % n_head), device_id_type=MESH)
    pl.semaphore_wait(barrier, n_seq + n_head - 2)

    xn, yn, dn = y * side + (1 - x), (1 - y) * side + x, (1 - y) * side + (1 - x)

    class Plane:
        def __init__(self, src, full, size, ss, rs):
            self.src, self.full, self.size, self.ss, self.rs = src, full, size, ss, rs
            self.sent = []

        def block(self, index, half=None):
            at, size = index * self.size, self.size
            if half is not None:
                size = self.size // 2
                at = at + half * size
            return self.full.at[pl.ds(pl.multiple_of(at, size), size)]

        def send(self, src, dst, index, seq):
            copy = rcopy(src, dst, self.ss.at[index], self.rs.at[index], seq, h)
            copy.start()
            self.sent.append(copy)

        def arrived(self, ref, index):
            rcopy(ref, ref, self.ss.at[index], self.rs.at[index], partner, h).wait_recv()

        def pass_on(self, ref, index, cross):
            self.arrived(ref, index)
            self.send(ref, ref, cross, partner)

        def start(self):
            mine = self.block(s)
            if side == 2:
                self.send(self.src, mine, 0, xn * 2 + core)
                self.send(self.src, mine, 1, yn * 2 + core)
            else:
                for i in range(chips - 1):
                    self.send(self.src, mine, i, away(i, 1) * 2 + core)
            self.send(self.src, mine, 2 * chips, partner)

        def forward(self):
            if side == 2:
                bx, by = self.block(xn * 2 + core), self.block(yn * 2 + core)
                hx, hy = self.block(xn * 2 + core, 0), self.block(yn * 2 + core, 1)
                self.arrived(bx, 0)
                self.send(hx, hx, 2, yn * 2 + core)
                self.arrived(by, 1)
                self.send(hy, hy, 3, xn * 2 + core)
                self.send(bx, bx, chips, partner)
                self.send(by, by, chips + 1, partner)

        def finish(self):
            if side == 2:
                for half in range(2):
                    self.pass_on(self.block(dn * 2 + core, half), 2 + half, chips + 2 + half)
            else:
                for i in range(chips - 1):
                    self.pass_on(self.block(away(i, -1) * 2 + core), i, chips + i)

        def near(self):
            other = 1 - core
            if side == 2:
                self.arrived(self.block(xn * 2 + other), chips)
                self.arrived(self.block(yn * 2 + other), chips + 1)
            self.arrived(self.block(partner), 2 * chips)

        def far(self):
            other = 1 - core
            if side == 2:
                for half in range(2):
                    self.arrived(self.block(dn * 2 + other, half), chips + 2 + half)
            else:
                for i in range(chips - 1):
                    self.arrived(self.block(away(i, -1) * 2 + other), chips + i)

        def drain(self):
            for copy in self.sent:
                copy.wait_send()

    w_plane = Plane(w_ref, w_full, wrows, w_ss, w_rs)
    w_plane.start()

    def g_right(d):
        b = (h + n_head - d + 1) % n_head
        src = g_ref if d == 1 else g_full.at[b]
        return rcopy(src, g_full.at[b], g_ss.at[d - 1], g_rs.at[d - 1], s, (h + 1) % n_head)

    def g_left(d):
        b, i = (h + d - 1) % n_head, n_head - 2 + d
        src = g_ref if d == 1 else g_full.at[b]
        return rcopy(src, g_full.at[b], g_ss.at[i], g_rs.at[i], s, (h + n_head - 1) % n_head)

    def g_each(d, act):
        @pl.when(jnp.logical_and(h + 1 < n_head, h >= d - 1))
        def _():
            act(g_right(d))

        @pl.when(jnp.logical_and(h >= 1, h + d - 1 < n_head))
        def _():
            act(g_left(d))

    def g_step(d):
        @pl.when(h >= d)
        def _():
            slot = g_full.at[(h + n_head - d) % n_head]
            rcopy(slot, slot, g_ss.at[d - 1], g_rs.at[d - 1], s, (h + 1) % n_head).wait_recv()

        @pl.when(h + d < n_head)
        def _():
            slot = g_full.at[(h + d) % n_head]
            i = n_head - 2 + d
            rcopy(slot, slot, g_ss.at[i], g_rs.at[i], s, (h + 1) % n_head).wait_recv()

        if d + 1 < n_head:
            g_each(d + 1, lambda copy: copy.start())

    g_each(1, lambda copy: copy.start())

    g_full[h] = g_ref[...]
    w_full[pl.ds(pl.multiple_of(s * wrows, wrows), wrows), :] = w_ref[...]

    first = s * rows
    r_i = lax.broadcasted_iota(jnp.int32, (rows, rows), 0)
    c_i = lax.broadcasted_iota(jnp.int32, (rows, rows), 1)
    p_col = first + lax.broadcasted_iota(jnp.int32, (rows, 1), 0)
    p_row = first + lax.broadcasted_iota(jnp.int32, (1, rows), 1)
    doc_col = jnp.full((rows, 1), -1, jnp.int32)
    doc_row = jnp.full((1, rows), -1, jnp.int32)
    edges = [jnp.full((1, 1), -1, jnp.int32) for _ in range(3)]
    points = [jnp.full((1, 1), 0, jnp.int32) + p for p in (first - 1, first + rows - 1, first + rows)]
    begin = jnp.int32(0)
    for j in range(lengths.shape[0]):
        doc_col = doc_col + jnp.where(p_col >= begin, 1, 0)
        doc_row = doc_row + jnp.where(p_row >= begin, 1, 0)
        edges = [e + jnp.where(p >= begin, 1, 0) for e, p in zip(edges, points)]
        begin = begin + lengths[j]
    prev_doc, last_doc, next_doc = edges
    tri = r_i >= c_i
    eye = r_i == c_i
    joint = jnp.logical_and(tri, doc_col == doc_row)

    def lanes(i):
        return pl.ds(pl.multiple_of(i * HD, HD), HD)

    def pass1(i, carry):
        at = lanes(i)
        q, k, v = q_ref[:, at], k_ref[:, at], v_ref[:, at]
        ld = ld_ref[pl.ds(i, 1), :]
        cum = jnp.sum(jnp.where(tri, ld, 0.0), axis=1, keepdims=True)
        cum_row = jnp.sum(jnp.where(eye, cum, 0.0), axis=0, keepdims=True)
        total = cum[rows - 1 : rows, :]
        decay = jnp.where(joint, jnp.exp(jnp.where(joint, cum - cum_row, 0.0)), 0.0)
        tail = jnp.exp(total - cum)
        enter = jnp.where(doc_col == prev_doc, jnp.exp(cum), 0.0)
        keep = jnp.where(doc_col == last_doc, tail, 0.0)
        leave = jnp.where(doc_col == next_doc, tail, 0.0)
        through = jnp.where(prev_doc == last_doc, jnp.exp(total), 0.0)
        thr[i] = jnp.broadcast_to(through, (8, HD))
        enter_s[i] = jnp.broadcast_to(enter, (rows, HD))
        leave_s[i] = jnp.broadcast_to(leave, (rows, HD))
        sum_f[i] = dot((k.astype(F32) * keep).astype(BF16), v, 0, 0).astype(BF16)
        decay_s[i] = decay
        attn = (dot(q, k, 1, 1) * decay).astype(BF16)
        attn_s[i] = attn
        local[:, at] = dot(attn, v, 1, 0)
        return carry

    lax.fori_loop(0, heads, pass1, 0)

    def fwd_copy(d):
        return rcopy(sum_f, recv_f.at[d - 1], f_ss.at[d - 1], f_rs.at[d - 1], (s + d) % n_seq, h)

    def bwd_copy(d):
        return rcopy(sum_b, recv_b.at[d - 1], b_ss.at[d - 1], b_rs.at[d - 1], (s + n_seq - d) % n_seq, h)

    def thr_copies(d):
        return (
            rcopy(thr, thr_prev.at[d - 1], tp_ss.at[d - 1], tp_rs.at[d - 1], (s + d) % n_seq, h),
            rcopy(thr, thr_next.at[d - 1], tn_ss.at[d - 1], tn_rs.at[d - 1], (s + n_seq - d) % n_seq, h),
        )

    for d in range(1, hops + 1):
        fwd_copy(d).start()
        for copy in thr_copies(d):
            copy.start()
    g_step(1)
    w_plane.forward()
    for d in range(2, n_head - 1):
        g_step(d)
    for d in range(1, hops + 1):
        fwd_copy(d).wait_recv()
        for copy in thr_copies(d):
            copy.wait_recv()

    def combined(i, recv, factors, valid):
        total = jnp.zeros((HD, HD), F32)
        scale = jnp.ones((1, HD), F32)
        for d in range(1, hops + 1):
            total = total + jnp.where(valid(d), recv[d - 1, i].astype(F32) * scale, 0.0)
            scale = scale * factors[d - 1, i, 0:1, :]
        return total.astype(BF16)

    def pass2(i, carry):
        at = lanes(i)
        state = combined(i, recv_f, thr_prev, lambda d: s >= d)
        state_s[i] = state
        out = local[:, at] + dot(q_ref[:, at], state, 1, 0) * enter_s[i]
        a_full[pl.ds(pl.multiple_of(s * rows, rows), rows), at] = out.astype(BF16)
        return carry

    lax.fori_loop(0, heads, pass2, 0)

    a_plane = Plane(a_full.at[pl.ds(pl.multiple_of(s * rows, rows), rows)], a_full, rows, a_ss, a_rs)
    a_plane.start()

    per = gwidth // wrows

    def col_copy(j):
        t = (s + j) % n_seq
        src = g_full.at[t // per, :, pl.ds(pl.multiple_of((t % per) * wrows, wrows), wrows)]
        dst = g_cols.at[pl.ds(pl.multiple_of(s * rows, rows), rows)]
        return rcopy(src, dst, c_ss.at[j - 1], c_rs.at[j - 1], t, h)


    def part(target, store):
        def tile(j, carry):
            at = pl.multiple_of(target * gwidth + j * TILE, TILE)
            value = dot(
                a_full[pl.ds(pl.multiple_of(s * rows, rows), rows), :], w_full[pl.ds(at, TILE), :], 1, 1
            )
            store(pl.ds(pl.multiple_of(j * TILE, TILE), TILE), value)
            return carry

        lax.fori_loop(0, gwidth // TILE, tile, 0)

    def part_copy(j):
        return rcopy(
            part_send.at[j - 1], part_recv.at[j - 1], p_ss.at[j - 1], p_rs.at[j - 1], s, (h + j) % n_head
        )

    def send_part(target, j):
        def keep_part(at, value):
            part_send[j, :, at] = value.astype(BF16)

        part(target, keep_part)
        rcopy(part_send.at[j], part_recv.at[j], p_ss.at[j], p_rs.at[j], s, target).start()

    def send_if_other(target):
        @pl.when(target != h)
        def _():
            send_part(target, (target + n_head - h) % n_head - 1)

    by_chip = side == 2 and n_head == chips and gwidth == 2 * wrows
    w_plane.near()
    if by_chip:
        for target in (chip, xn, yn):
            send_if_other(target)
    g_step(n_head - 1)
    g_cols[pl.ds(pl.multiple_of(s * rows, rows), rows), :] = g_full[
        s // per, :, pl.ds(pl.multiple_of((s % per) * wrows, wrows), wrows)
    ]
    w_plane.finish()
    w_plane.far()
    if by_chip:
        send_if_other(dn)
    else:
        for j in range(1, n_head):
            send_part((h + j) % n_head, j - 1)

    for j in range(1, n_seq // 2):
        col_copy(j).start()

    def pull(j, carry):
        at = pl.ds(pl.multiple_of(j * TILE, TILE), TILE)
        value = jnp.zeros((rows, TILE), F32)
        for b in range(n_head):
            value = value + dot(g_full[b], w_full[b * gwidth : (b + 1) * gwidth, at], 1, 0)
        ga_s[:, at] = value.astype(BF16)
        return carry

    lax.fori_loop(0, width // TILE, pull, 0)

    def pass3(i, carry):
        at = lanes(i)
        g = ga_s[:, at]
        sum_b[i] = dot((q_ref[:, at].astype(F32) * enter_s[i]).astype(BF16), g, 0, 0).astype(BF16)
        return carry

    lax.fori_loop(0, heads, pass3, 0)

    for d in range(1, hops + 1):
        bwd_copy(d).start()
    for j in range(n_seq // 2, n_seq):
        col_copy(j).start()
    a_plane.forward()

    def own_part(at, value):
        local2[:, at] = value

    part(h, own_part)

    def pass4(i, carry):
        at = lanes(i)
        q, k, v, g = q_ref[:, at], k_ref[:, at], v_ref[:, at], ga_s[:, at]
        back = (dot(g, v, 1, 1) * decay_s[i]).astype(BF16)
        gq = dot(back, k, 1, 0) + dot(g, state_s[i], 1, 1) * enter_s[i]
        gq_ref[:, at] = gq.astype(BF16)
        local[:, at] = dot(back, q, 0, 0)
        return carry

    lax.fori_loop(0, heads, pass4, 0)

    a_plane.finish()
    for d in range(1, hops + 1):
        bwd_copy(d).wait_recv()

    def pass5(i, carry):
        at = lanes(i)
        k, v, g = k_ref[:, at], v_ref[:, at], ga_s[:, at]
        state = combined(i, recv_b, thr_next, lambda d: s + d < n_seq)
        gk = local[:, at] + dot(v, state, 1, 1) * leave_s[i]
        gv = dot(attn_s[i], g, 0, 0) + dot(k, state, 1, 0) * leave_s[i]
        gk_ref[:, at] = gk.astype(BF16)
        gv_ref[:, at] = gv.astype(BF16)
        return carry

    lax.fori_loop(0, heads, pass5, 0)

    a_plane.near()
    a_plane.far()
    for j in range(1, n_seq):
        slot = g_cols.at[pl.ds(pl.multiple_of(((s + n_seq - j) % n_seq) * rows, rows), rows)]
        rcopy(slot, slot, c_ss.at[j - 1], c_rs.at[j - 1], (s + j) % n_seq, h).wait_recv()

    mt = min(TILE, wrows)
    depth = min(2048, n_seq * rows)
    for b in range(n_seq * rows // depth):

        def outer(j, carry, b=b):
            m, n = j // (width // TILE), j % (width // TILE)
            rm = pl.ds(pl.multiple_of(m * mt, mt), mt)
            rn = pl.ds(pl.multiple_of(n * TILE, TILE), TILE)
            value = dot(
                g_cols[b * depth : (b + 1) * depth, rm], a_full[b * depth : (b + 1) * depth, rn], 0, 0
            )
            if b > 0:
                value = value + gw_ref[rm, rn]
            gw_ref[rm, rn] = value
            return carry

        lax.fori_loop(0, (wrows // mt) * (width // TILE), outer, 0)

    for j in range(1, n_head):
        part_copy(j).wait_recv()
    total = local2[...]
    for j in range(1, n_head):
        total = total + part_recv[j - 1].astype(F32)
    mixed_ref[...] = total.astype(BF16)

    w_plane.drain()
    a_plane.drain()
    for j in range(1, n_head):
        g_each(j, lambda copy: copy.wait_send())
        part_copy(j).wait_send()
    for j in range(1, n_seq):
        col_copy(j).wait_send()
    for d in range(1, hops + 1):
        fwd_copy(d).wait_send()
        bwd_copy(d).wait_send()
        for copy in thr_copies(d):
            copy.wait_send()


def square_kernel(
    n_head,
    lengths, q_ref, k_ref, v_ref, ld_ref, w_ref, g_ref,
    mixed_ref, gq_ref, gk_ref, gv_ref, gw_ref,
    w_full, g_full, g_pair, a_pair, z_send, near, fold, merged, wg_send, wg_recv,
    local, local2, decay_s, attn_s, enter_s, leave_s, ga_s, thr,
    sum_f, raw_f, out_f, in_f, sum_b, raw_b, out_b, in_b,
    w_ss, w_rs, g_ss, g_rs, x_ss, x_rs, a_ss, a_rs, z_ss, n_rs, f_rs, m_rs, wg_ss, wg_rs, st_ss, st_rs,
):
    s, h = lax.axis_index("seq"), lax.axis_index("head")
    n_seq = 8
    rows, width = q_ref.shape
    heads = width // HD
    wrows = w_ref.shape[0]
    gwidth = g_ref.shape[1]
    half = wrows // 2
    chip, core = s // 2, s % 2
    other = 1 - core
    x, y = chip % 2, chip // 2
    partner = chip * 2 + other
    xn, yn, dn = y * 2 + (1 - x), (1 - y) * 2 + x, (1 - y) * 2 + (1 - x)
    sent = []

    def rcopy(src, dst, ss, rs, seq, head):
        return pltpu.make_async_remote_copy(
            src_ref=src, dst_ref=dst, send_sem=ss, recv_sem=rs,
            device_id=(seq, head), device_id_type=MESH,
        )

    def ship(src, dst, ss, rs, i, seq):
        copy = rcopy(src, dst, ss.at[i], rs.at[i], seq, h)
        copy.start()
        sent.append(copy)

    def got(ref, ss, rs, i):
        rcopy(ref, ref, ss.at[i], rs.at[i], partner, h).wait_recv()

    barrier = pltpu.get_barrier_semaphore()
    for j in range(1, n_seq):
        pl.semaphore_signal(barrier, inc=1, device_id=((s + j) % n_seq, h), device_id_type=MESH)
    for j in range(1, n_head):
        pl.semaphore_signal(barrier, inc=1, device_id=(s, (h + j) % n_head), device_id_type=MESH)
    pl.semaphore_wait(barrier, n_seq + n_head - 2)

    def w_at(seq, part):
        return w_full.at[pl.ds(pl.multiple_of(seq * wrows + part * half, half), half)]

    def w_own(part):
        return w_ref.at[pl.ds(part * half, half)]

    xs, ys = xn * 2 + core, yn * 2 + core
    ship(w_own(0), w_at(s, 0), w_ss, w_rs, 0, xs)
    ship(w_own(1), w_at(s, 1), w_ss, w_rs, 2, ys)

    def g_right(d):
        b = (h + n_head - d + 1) % n_head
        src = g_ref if d == 1 else g_full.at[b]
        return rcopy(src, g_full.at[b], g_ss.at[d - 1], g_rs.at[d - 1], s, (h + 1) % n_head)

    def g_left(d):
        b, i = (h + d - 1) % n_head, n_head - 2 + d
        src = g_ref if d == 1 else g_full.at[b]
        return rcopy(src, g_full.at[b], g_ss.at[i], g_rs.at[i], s, (h + n_head - 1) % n_head)

    def g_each(d, act):
        @pl.when(jnp.logical_and(h + 1 < n_head, h >= d - 1))
        def _():
            act(g_right(d))

        @pl.when(jnp.logical_and(h >= 1, h + d - 1 < n_head))
        def _():
            act(g_left(d))

    def core_cols(c):
        return pl.ds(pl.multiple_of(c * wrows, wrows), wrows)

    def core_rows(c):
        return pl.ds(pl.multiple_of(c * rows, rows), rows)

    def g_cross(f, src):
        return rcopy(src.at[:, core_cols(other)], g_pair.at[f, core_rows(core)], x_ss.at[f], x_rs.at[f], partner, h)

    def g_across(f):
        g_cross(f, g_full.at[f]).start()
        g_pair[f, core_rows(core), :] = g_full[f, :, core_cols(core)]

    def g_step(d):
        @pl.when(h >= d)
        def _():
            slot = g_full.at[(h + n_head - d) % n_head]
            rcopy(slot, slot, g_ss.at[d - 1], g_rs.at[d - 1], s, (h + 1) % n_head).wait_recv()

        @pl.when(h + d < n_head)
        def _():
            slot = g_full.at[(h + d) % n_head]
            i = n_head - 2 + d
            rcopy(slot, slot, g_ss.at[i], g_rs.at[i], s, (h + 1) % n_head).wait_recv()

        if d + 1 < n_head:
            g_each(d + 1, lambda copy: copy.start())

        @pl.when(h >= d)
        def _():
            g_across((h + n_head - d) % n_head)

        @pl.when(h + d < n_head)
        def _():
            g_across((h + d) % n_head)

    g_each(1, lambda copy: copy.start())
    ship(w_ref, w_full.at[pl.ds(pl.multiple_of(s * wrows, wrows), wrows)], w_ss, w_rs, 8, partner)

    g_full[h] = g_ref[...]
    g_cross(h, g_ref).start()
    g_pair[h, core_rows(core), :] = g_ref[:, core_cols(core)]
    w_full[pl.ds(pl.multiple_of(s * wrows, wrows), wrows), :] = w_ref[...]

    first = s * rows
    r_i = lax.broadcasted_iota(jnp.int32, (rows, rows), 0)
    c_i = lax.broadcasted_iota(jnp.int32, (rows, rows), 1)
    p_col = first + lax.broadcasted_iota(jnp.int32, (rows, 1), 0)
    p_row = first + lax.broadcasted_iota(jnp.int32, (1, rows), 1)
    doc_col = jnp.full((rows, 1), -1, jnp.int32)
    doc_row = jnp.full((1, rows), -1, jnp.int32)
    edges = [jnp.full((1, 1), -1, jnp.int32) for _ in range(3)]
    points = [jnp.full((1, 1), 0, jnp.int32) + p for p in (first - 1, first + rows - 1, first + rows)]
    begin = jnp.int32(0)
    for j in range(lengths.shape[0]):
        doc_col = doc_col + jnp.where(p_col >= begin, 1, 0)
        doc_row = doc_row + jnp.where(p_row >= begin, 1, 0)
        edges = [e + jnp.where(p >= begin, 1, 0) for e, p in zip(edges, points)]
        begin = begin + lengths[j]
    prev_doc, last_doc, next_doc = edges
    tri = r_i >= c_i
    eye = r_i == c_i
    joint = jnp.logical_and(tri, doc_col == doc_row)

    def lanes(i):
        return pl.ds(pl.multiple_of(i * HD, HD), HD)

    def pass1(i, carry):
        at = lanes(i)
        q, k, v = q_ref[:, at], k_ref[:, at], v_ref[:, at]
        ld = ld_ref[pl.ds(i, 1), :]
        cum = jnp.sum(jnp.where(tri, ld, 0.0), axis=1, keepdims=True)
        cum_row = jnp.sum(jnp.where(eye, cum, 0.0), axis=0, keepdims=True)
        total = cum[rows - 1 : rows, :]
        decay = jnp.where(joint, jnp.exp(jnp.where(joint, cum - cum_row, 0.0)), 0.0)
        tail = jnp.exp(total - cum)
        enter = jnp.where(doc_col == prev_doc, jnp.exp(cum), 0.0)
        keep = jnp.where(doc_col == last_doc, tail, 0.0)
        leave = jnp.where(doc_col == next_doc, tail, 0.0)
        through = jnp.where(prev_doc == last_doc, jnp.exp(total), 0.0)
        thr[i] = jnp.broadcast_to(through, (8, HD))
        enter_s[i] = jnp.broadcast_to(enter, (rows, HD))
        leave_s[i] = jnp.broadcast_to(leave, (rows, HD))
        sum_f[i] = dot((k.astype(F32) * keep).astype(BF16), v, 0, 0).astype(BF16)
        decay_s[i] = decay
        attn = (dot(q, k, 1, 1) * decay).astype(BF16)
        attn_s[i] = attn
        local[:, at] = dot(attn, v, 1, 0)
        return carry

    lax.fori_loop(0, heads, pass1, 0)

    def chain(lead, step, sums, raw, out, inn, i):
        to = (s + n_seq + step) % n_seq
        has_next = s < n_seq - 1 if step > 0 else s > 0
        has_last = s > 0 if step > 0 else s < n_seq - 1
        raw_copy = rcopy(sums, raw, st_ss.at[i], st_rs.at[i], to, h)
        out_copy = rcopy(out, inn, st_ss.at[i + 1], st_rs.at[i + 1], to, h)
        leads = core == lead

        def add(base):
            def one(j, carry):
                out[j] = (sums[j].astype(F32) + base[j].astype(F32) * thr[j, 0:1, :]).astype(BF16)
                return carry

            lax.fori_loop(0, heads, one, 0)

        def begin():
            @pl.when(leads)
            def _():
                raw_copy.start()

            @pl.when(jnp.logical_not(leads))
            def _():
                raw_copy.wait_recv()

                @pl.when(has_next)
                def _():
                    add(raw)
                    out_copy.start()

        def end():
            @pl.when(has_last)
            def _():
                out_copy.wait_recv()

            @pl.when(jnp.logical_not(has_last))
            def _():
                inn[...] = jnp.zeros_like(inn)

            @pl.when(leads)
            def _():
                add(inn)
                out_copy.start()

        def drain():
            @pl.when(leads)
            def _():
                raw_copy.wait_send()

            @pl.when(jnp.logical_or(leads, has_next))
            def _():
                out_copy.wait_send()

        return begin, end, drain

    f_begin, f_end, f_drain = chain(0, 1, sum_f, raw_f, out_f, in_f, 0)
    b_begin, b_end, b_drain = chain(1, -1, sum_b, raw_b, out_b, in_b, 2)

    f_begin()
    ship(w_own(1), w_at(s, 1), w_ss, w_rs, 1, xs)
    ship(w_own(0), w_at(s, 0), w_ss, w_rs, 3, ys)

    def w_pass(i, seq, part, ahead, to, across):
        ref = w_at(seq, part)
        got(ref, w_ss, w_rs, i)
        if ahead is not None:
            ship(ref, ref, w_ss, w_rs, ahead, to)
        ship(ref, ref, w_ss, w_rs, across, partner)

    w_pass(0, xs, 0, 4, ys, 9)
    w_pass(2, ys, 1, 5, xs, 10)
    g_step(1)

    f_end()

    def pass2(i, carry):
        at = lanes(i)
        out = local[:, at] + dot(q_ref[:, at], in_f[i], 1, 0) * enter_s[i]
        a_pair[core_rows(core), at] = out.astype(BF16)
        return carry

    lax.fori_loop(0, heads, pass2, 0)

    mine = a_pair.at[core_rows(core)]
    ship(mine, mine, a_ss, a_rs, 0, partner)

    inner = jnp.logical_and(h > 0, h < n_head - 1)
    mate = h + 1 - 2 * (h % 2)

    def part(target, p, store):
        def tile(c, carry):
            at = pl.multiple_of(target * gwidth + c * wrows + p * half, half)
            value = dot(a_pair[core_rows(core), :], w_full[pl.ds(at, half), :], 1, 1)
            store(c, value)
            return carry

        lax.fori_loop(0, gwidth // wrows, tile, 0)

    def chunk_cols(c):
        return pl.ds(pl.multiple_of(c * half, half), half)

    def z_copy(b, p, dst, rs, to):
        return rcopy(z_send.at[b, p], dst, z_ss.at[b * 2 + p], rs, s, to)

    def z_near(b, p):
        z_copy(b, p, near.at[p], n_rs.at[p], mate).start()

    def z_fold(b, p):
        return z_copy(b, p, fold.at[b % 2, p], f_rs.at[(b % 2) * 2 + p], mate)

    def make_parts(chunks):
        for b, p in chunks:

            @pl.when(b != h)
            def _(b=b, p=p):
                def keep_part(c, value):
                    z_send[b, p, :, chunk_cols(c)] = value.astype(BF16)

                part(b, p, keep_part)

            @pl.when(jnp.logical_and(jnp.logical_not(inner), b == mate))
            def _(b=b, p=p):
                z_near(b, p)

            @pl.when(jnp.logical_and(jnp.logical_not(inner), jnp.logical_and(b != h, b != mate)))
            def _(b=b, p=p):
                z_fold(b, p).start()

    def pass_parts(chunks):
        for b, p in chunks:

            @pl.when(jnp.logical_and(inner, b == mate))
            def _(b=b, p=p):
                z_near(b, p)

            @pl.when(jnp.logical_and(inner, jnp.logical_and(b != h, b != mate)))
            def _(b=b, p=p):
                z_fold(b, p).wait_recv()
                z_send[b, p] = (z_send[b, p].astype(F32) + fold[b % 2, p].astype(F32)).astype(BF16)
                z_copy(b, p, merged.at[p], m_rs.at[p], b).start()

    xo, yo, do = xn * 2 + other, yn * 2 + other, dn * 2 + other
    got(w_full.at[pl.ds(pl.multiple_of(partner * wrows, wrows), wrows)], w_ss, w_rs, 8)
    got(w_at(xo, 0), w_ss, w_rs, 9)
    got(w_at(yo, 1), w_ss, w_rs, 10)
    early = [(chip, 0), (chip, 1), (xn, 0), (yn, 1)]
    make_parts(early)

    w_pass(1, xs, 1, None, None, 11)
    w_pass(3, ys, 0, None, None, 12)
    g_step(2)
    got(w_at(xo, 1), w_ss, w_rs, 11)
    got(w_at(yo, 0), w_ss, w_rs, 12)
    middle = [(xn, 1), (yn, 0)]
    make_parts(middle)
    other_half = a_pair.at[core_rows(other)]
    got(other_half, a_ss, a_rs, 0)

    last = n_head - 1 - h
    for f in range(n_head):

        @pl.when(jnp.logical_or(inner, f != last))
        def _(f=f):
            got(g_pair.at[f, core_rows(other)], x_ss, x_rs, f)

    def gw_block(f, part, store):
        def tile(j, carry):
            at = pl.ds(pl.multiple_of(j * TILE, TILE), TILE)
            store(at, dot(g_pair[f, :, part * half : (part + 1) * half], a_pair[:, at], 0, 0))
            return carry

        lax.fori_loop(0, width // TILE, tile, 0)

    def send_gw(i, f, part, to, extra=None):
        def keep_gw(at, value):
            if extra is not None:
                value = value + wg_recv[extra, :, at].astype(F32)
            wg_send[i, :, at] = value.astype(BF16)

        gw_block(f, part, keep_gw)
        ship(wg_send.at[i], wg_recv.at[i], wg_ss, wg_rs, i, to)

    swap = jnp.where(jnp.logical_and(jnp.logical_not(inner), dn == last), 1, 0)
    send_gw(2 * swap, swap * xn + (1 - swap) * dn, 0, xs)
    send_gw(1 + 2 * swap, swap * yn + (1 - swap) * dn, 1, ys)

    w_pass(4, dn * 2 + core, 0, None, None, 13)
    w_pass(5, dn * 2 + core, 1, None, None, 14)
    for d in range(3, n_head):
        g_step(d)
    got(w_at(do, 0), w_ss, w_rs, 13)
    got(w_at(do, 1), w_ss, w_rs, 14)
    late = [(dn, 0), (dn, 1)]
    make_parts(late)

    @pl.when(jnp.logical_not(inner))
    def _():
        got(g_pair.at[last, core_rows(other)], x_ss, x_rs, last)

    send_gw(2 - 2 * swap, swap * dn + (1 - swap) * xn, 0, xs)
    send_gw(3 - 2 * swap, swap * dn + (1 - swap) * yn, 1, ys)
    pass_parts(early)

    def pull(j, carry):
        at = pl.ds(pl.multiple_of(j * TILE, TILE), TILE)
        value = jnp.zeros((rows, TILE), F32)
        for b in range(n_head):
            value = value + dot(g_full[b], w_full[b * gwidth : (b + 1) * gwidth, at], 1, 0)
        ga_s[:, at] = value.astype(BF16)
        return carry

    lax.fori_loop(0, width // TILE, pull, 0)

    def pass3(i, carry):
        at = lanes(i)
        g = ga_s[:, at]
        sum_b[i] = dot((q_ref[:, at].astype(F32) * enter_s[i]).astype(BF16), g, 0, 0).astype(BF16)
        return carry

    lax.fori_loop(0, heads, pass3, 0)
    b_begin()

    got(wg_recv.at[0], wg_ss, wg_rs, 0)
    send_gw(4, yn, 0, ys, 0)
    got(wg_recv.at[1], wg_ss, wg_rs, 1)
    send_gw(5, xn, 1, xs, 1)
    pass_parts(middle + late)

    def pass4(i, carry):
        at = lanes(i)
        q, k, v, g = q_ref[:, at], k_ref[:, at], v_ref[:, at], ga_s[:, at]
        back = (dot(g, v, 1, 1) * decay_s[i]).astype(BF16)
        gq = dot(back, k, 1, 0) + dot(g, in_f[i], 1, 1) * enter_s[i]
        gq_ref[:, at] = gq.astype(BF16)
        local[:, at] = dot(back, q, 0, 0)
        return carry

    lax.fori_loop(0, heads, pass4, 0)

    b_end()

    def pass5(i, carry):
        at = lanes(i)
        k, v, g = k_ref[:, at], v_ref[:, at], ga_s[:, at]
        gk = local[:, at] + dot(v, in_b[i], 1, 1) * leave_s[i]
        gv = dot(attn_s[i], g, 0, 0) + dot(k, in_b[i], 1, 0) * leave_s[i]
        gk_ref[:, at] = gk.astype(BF16)
        gv_ref[:, at] = gv.astype(BF16)
        return carry

    lax.fori_loop(0, heads, pass5, 0)

    for p in range(2):

        def own_part(c, value, p=p):
            local2[:, pl.ds(pl.multiple_of(c * wrows + p * half, half), half)] = value

        part(h, p, own_part)

    for p in range(2):
        got(wg_recv.at[2 + p], wg_ss, wg_rs, 2 + p)

        def keep_own(at, value, p=p):
            gw_ref[p * half : (p + 1) * half, at] = value + wg_recv[2 + p, :, at].astype(F32)

        gw_block(chip, p, keep_own)

    for p in range(2):
        rcopy(near.at[p], near.at[p], z_ss.at[0], n_rs.at[p], s, mate).wait_recv()
        rcopy(merged.at[p], merged.at[p], z_ss.at[0], m_rs.at[p], s, mate).wait_recv()
        for c in range(gwidth // wrows):
            at, cols = pl.ds(c * wrows + p * half, half), pl.ds(c * half, half)
            total = local2[:, at] + near[p, :, cols].astype(F32) + merged[p, :, cols].astype(F32)
            mixed_ref[:, at] = total.astype(BF16)

    for p in range(2):
        got(wg_recv.at[4 + p], wg_ss, wg_rs, 4 + p)
        at = pl.ds(p * half, half)
        gw_ref[at, :] = gw_ref[at, :] + wg_recv[4 + p].astype(F32)

    for copy in sent:
        copy.wait_send()
    for f in range(n_head):
        g_cross(f, g_full.at[f]).wait_send()
    for j in range(1, n_head):
        g_each(j, lambda copy: copy.wait_send())
        for p in range(2):
            z_copy((h + j) % n_head, p, near.at[p], n_rs.at[p], mate).wait_send()
    f_drain()
    b_drain()


def square_call(n_head, queries, keys, values, log_decay, lengths, out_weight, out_grad):
    rows, width = queries.shape
    heads = log_decay.shape[0]
    wrows = out_weight.shape[0]
    gwidth = out_grad.shape[1]
    dma = lambda n: pltpu.SemaphoreType.DMA((n,))
    vm = pltpu.VMEM
    scratch = [
        vm((8 * wrows, width), BF16),
        vm((n_head, rows, gwidth), BF16),
        vm((n_head, 2 * rows, wrows), BF16),
        vm((2 * rows, width), BF16),
        vm((n_head, 2, rows, wrows), BF16),
        vm((2, rows, wrows), BF16),
        vm((2, 2, rows, wrows), BF16),
        vm((2, rows, wrows), BF16),
        vm((6, wrows // 2, width), BF16),
        vm((6, wrows // 2, width), BF16),
        vm((rows, width), F32),
        vm((rows, gwidth), F32),
        vm((heads, rows, rows), F32),
        vm((heads, rows, rows), BF16),
        vm((heads, rows, HD), F32),
        vm((heads, rows, HD), F32),
        vm((rows, width), BF16),
        vm((heads, 8, HD), F32),
    ] + [vm((heads, HD, HD), BF16)] * 8 + [
        dma(15), dma(15), dma(2 * n_head - 2), dma(2 * n_head - 2), dma(n_head), dma(n_head), dma(1), dma(1),
        dma(2 * n_head), dma(2), dma(4), dma(2), dma(6), dma(6), dma(4), dma(4),
    ]
    spec = pl.BlockSpec(memory_space=pltpu.VMEM)
    return pl.pallas_call(
        functools.partial(square_kernel, n_head),
        out_shape=[vm((rows, gwidth), BF16)] + [vm((rows, width), BF16)] * 3 + [vm((wrows, width), F32)],
        in_specs=[pl.BlockSpec(memory_space=pltpu.SMEM)] + [spec] * 6,
        out_specs=[spec] * 5,
        scratch_shapes=scratch,
        compiler_params=pltpu.CompilerParams(
            collective_id=1, has_side_effects=True, vmem_limit_bytes=61360 * 1024
        ),
    )(lengths, queries, keys, values, log_decay, out_weight, out_grad)


def body(n_seq, n_head, queries, keys, values, log_decay, lengths, out_weight, out_grad):
    rows, width = queries.shape
    heads = log_decay.shape[0]
    wrows = out_weight.shape[0]
    gwidth = out_grad.shape[1]
    chips = n_seq // 2
    longest = n_seq * rows // 4
    hops = (longest - 1) // rows + 1
    if chips == 4 and n_head == 4 and gwidth == 2 * wrows and wrows % 32 == 0 and hops == 2:
        return square_call(n_head, queries, keys, values, log_decay, lengths, out_weight, out_grad)
    dma = lambda n: pltpu.SemaphoreType.DMA((n,))
    vm = pltpu.VMEM
    scratch = [
        vm((n_seq * wrows, width), BF16),
        vm((n_seq * rows, width), BF16),
        vm((n_head, rows, gwidth), BF16),
        vm((n_seq * rows, wrows), BF16),
        vm((n_head - 1, rows, gwidth), BF16),
        vm((n_head - 1, rows, gwidth), BF16),
        vm((rows, width), F32),
        vm((rows, gwidth), F32),
        vm((heads, rows, rows), F32),
        vm((heads, rows, rows), BF16),
        vm((heads, rows, HD), F32),
        vm((heads, rows, HD), F32),
        vm((heads, HD, HD), BF16),
        vm((rows, width), BF16),
        vm((heads, 8, HD), F32),
        vm((hops, heads, 8, HD), F32),
        vm((hops, heads, 8, HD), F32),
        vm((heads, HD, HD), BF16),
        vm((heads, HD, HD), BF16),
        vm((hops, heads, HD, HD), BF16),
        vm((hops, heads, HD, HD), BF16),
        dma(2 * chips + 1), dma(2 * chips + 1), dma(2 * chips + 1), dma(2 * chips + 1),
        dma(2 * n_head - 2), dma(2 * n_head - 2), dma(n_seq - 1), dma(n_seq - 1), dma(n_head - 1), dma(n_head - 1),
        dma(hops), dma(hops), dma(hops), dma(hops), dma(hops), dma(hops), dma(hops), dma(hops),
    ]
    spec = pl.BlockSpec(memory_space=pltpu.VMEM)
    return pl.pallas_call(
        functools.partial(kernel, n_seq, n_head, hops),
        out_shape=[vm((rows, gwidth), BF16)] + [vm((rows, width), BF16)] * 3 + [vm((wrows, width), F32)],
        in_specs=[pl.BlockSpec(memory_space=pltpu.SMEM)] + [spec] * 6,
        out_specs=[spec] * 5,
        scratch_shapes=scratch,
        compiler_params=pltpu.CompilerParams(
            collective_id=0, has_side_effects=True, vmem_limit_bytes=61360 * 1024
        ),
    )(lengths, queries, keys, values, log_decay, out_weight, out_grad)


def solution(mesh):
    both = P("seq", "head")
    in_specs = (both, both, both, P("head", "seq"), P(), both, both)
    return jax.shard_map(
        functools.partial(body, mesh.shape["seq"], mesh.shape["head"]),
        mesh=mesh, in_specs=in_specs, out_specs=(both,) * 5, check_vma=False,
    )
```

```python
import functools
import math

import jax
import jax.numpy as jnp
from jax import lax
from jax.experimental import pallas as pl
from jax.experimental.pallas import tpu as pltpu
from jax.sharding import PartitionSpec as P

MESH = pl.DeviceIdType.MESH
F32 = jnp.float32
BF16 = jnp.bfloat16
HD = 128
TILE = 256


def dot(a, b, ca, cb):
    return lax.dot_general(a, b, (((ca,), (cb,)), ((), ())), preferred_element_type=F32)


def kernel(
    n_seq, n_head, hops,
    lengths, q_ref, k_ref, v_ref, ld_ref, w_ref, g_ref,
    mixed_ref, gq_ref, gk_ref, gv_ref, gw_ref,
    w_full, a_full, g_full, g_cols, part_send, part_recv,
    local, local2, decay_s, attn_s, enter_s, leave_s, state_s, ga_s, thr, thr_prev, thr_next,
    sum_f, sum_b, recv_f, recv_b,
    w_ss, w_rs, a_ss, a_rs, g_ss, g_rs, c_ss, c_rs, p_ss, p_rs,
    f_ss, f_rs, b_ss, b_rs, tp_ss, tp_rs, tn_ss, tn_rs,
):
    s, h = lax.axis_index("seq"), lax.axis_index("head")
    rows, width = q_ref.shape
    heads = width // HD
    wrows = w_ref.shape[0]
    gwidth = g_ref.shape[1]
    chips = n_seq // 2
    side = math.isqrt(chips)
    chip, core = s // 2, s % 2
    x, y = chip % side, chip // side
    partner = chip * 2 + (1 - core)
    offs = [(dy, dx) for dy in range(side) for dx in range(side) if (dy, dx) != (0, 0)]

    def rcopy(src, dst, ss, rs, seq, head):
        return pltpu.make_async_remote_copy(
            src_ref=src, dst_ref=dst, send_sem=ss, recv_sem=rs,
            device_id=(seq, head), device_id_type=MESH,
        )

    def away(i, sign):
        dy, dx = offs[i]
        if sign > 0:
            return ((y + dy) % side) * side + (x + dx) % side
        return ((y + side - dy) % side) * side + (x + side - dx) % side

    barrier = pltpu.get_barrier_semaphore()
    for j in range(1, n_seq):
        pl.semaphore_signal(barrier, inc=1, device_id=((s + j) % n_seq, h), device_id_type=MESH)
    for j in range(1, n_head):
        pl.semaphore_signal(barrier, inc=1, device_id=(s, (h + j) % n_head), device_id_type=MESH)
    pl.semaphore_wait(barrier, n_seq + n_head - 2)

    xn, yn, dn = y * side + (1 - x), (1 - y) * side + x, (1 - y) * side + (1 - x)

    class Plane:
        def __init__(self, src, full, size, ss, rs):
            self.src, self.full, self.size, self.ss, self.rs = src, full, size, ss, rs
            self.sent = []

        def block(self, index, half=None):
            at, size = index * self.size, self.size
            if half is not None:
                size = self.size // 2
                at = at + half * size
            return self.full.at[pl.ds(pl.multiple_of(at, size), size)]

        def send(self, src, dst, index, seq):
            copy = rcopy(src, dst, self.ss.at[index], self.rs.at[index], seq, h)
            copy.start()
            self.sent.append(copy)

        def arrived(self, ref, index):
            rcopy(ref, ref, self.ss.at[index], self.rs.at[index], partner, h).wait_recv()

        def pass_on(self, ref, index, cross):
            self.arrived(ref, index)
            self.send(ref, ref, cross, partner)

        def start(self):
            mine = self.block(s)
            if side == 2:
                self.send(self.src, mine, 0, xn * 2 + core)
                self.send(self.src, mine, 1, yn * 2 + core)
            else:
                for i in range(chips - 1):
                    self.send(self.src, mine, i, away(i, 1) * 2 + core)
            self.send(self.src, mine, 2 * chips, partner)

        def forward(self):
            if side == 2:
                bx, by = self.block(xn * 2 + core), self.block(yn * 2 + core)
                hx, hy = self.block(xn * 2 + core, 0), self.block(yn * 2 + core, 1)
                self.arrived(bx, 0)
                self.send(hx, hx, 2, yn * 2 + core)
                self.arrived(by, 1)
                self.send(hy, hy, 3, xn * 2 + core)
                self.send(bx, bx, chips, partner)
                self.send(by, by, chips + 1, partner)

        def finish(self):
            if side == 2:
                for half in range(2):
                    self.pass_on(self.block(dn * 2 + core, half), 2 + half, chips + 2 + half)
            else:
                for i in range(chips - 1):
                    self.pass_on(self.block(away(i, -1) * 2 + core), i, chips + i)

        def near(self):
            other = 1 - core
            if side == 2:
                self.arrived(self.block(xn * 2 + other), chips)
                self.arrived(self.block(yn * 2 + other), chips + 1)
            self.arrived(self.block(partner), 2 * chips)

        def far(self):
            other = 1 - core
            if side == 2:
                for half in range(2):
                    self.arrived(self.block(dn * 2 + other, half), chips + 2 + half)
            else:
                for i in range(chips - 1):
                    self.arrived(self.block(away(i, -1) * 2 + other), chips + i)

        def drain(self):
            for copy in self.sent:
                copy.wait_send()

    w_plane = Plane(w_ref, w_full, wrows, w_ss, w_rs)
    w_plane.start()

    def g_right(d):
        b = (h + n_head - d + 1) % n_head
        src = g_ref if d == 1 else g_full.at[b]
        return rcopy(src, g_full.at[b], g_ss.at[d - 1], g_rs.at[d - 1], s, (h + 1) % n_head)

    def g_left(d):
        b, i = (h + d - 1) % n_head, n_head - 2 + d
        src = g_ref if d == 1 else g_full.at[b]
        return rcopy(src, g_full.at[b], g_ss.at[i], g_rs.at[i], s, (h + n_head - 1) % n_head)

    def g_each(d, act):
        @pl.when(jnp.logical_and(h + 1 < n_head, h >= d - 1))
        def _():
            act(g_right(d))

        @pl.when(jnp.logical_and(h >= 1, h + d - 1 < n_head))
        def _():
            act(g_left(d))

    def g_step(d):
        @pl.when(h >= d)
        def _():
            slot = g_full.at[(h + n_head - d) % n_head]
            rcopy(slot, slot, g_ss.at[d - 1], g_rs.at[d - 1], s, (h + 1) % n_head).wait_recv()

        @pl.when(h + d < n_head)
        def _():
            slot = g_full.at[(h + d) % n_head]
            i = n_head - 2 + d
            rcopy(slot, slot, g_ss.at[i], g_rs.at[i], s, (h + 1) % n_head).wait_recv()

        if d + 1 < n_head:
            g_each(d + 1, lambda copy: copy.start())

    g_each(1, lambda copy: copy.start())

    g_full[h] = g_ref[...]
    w_full[pl.ds(pl.multiple_of(s * wrows, wrows), wrows), :] = w_ref[...]

    first = s * rows
    r_i = lax.broadcasted_iota(jnp.int32, (rows, rows), 0)
    c_i = lax.broadcasted_iota(jnp.int32, (rows, rows), 1)
    p_col = first + lax.broadcasted_iota(jnp.int32, (rows, 1), 0)
    p_row = first + lax.broadcasted_iota(jnp.int32, (1, rows), 1)
    doc_col = jnp.full((rows, 1), -1, jnp.int32)
    doc_row = jnp.full((1, rows), -1, jnp.int32)
    edges = [jnp.full((1, 1), -1, jnp.int32) for _ in range(3)]
    points = [jnp.full((1, 1), 0, jnp.int32) + p for p in (first - 1, first + rows - 1, first + rows)]
    begin = jnp.int32(0)
    for j in range(lengths.shape[0]):
        doc_col = doc_col + jnp.where(p_col >= begin, 1, 0)
        doc_row = doc_row + jnp.where(p_row >= begin, 1, 0)
        edges = [e + jnp.where(p >= begin, 1, 0) for e, p in zip(edges, points)]
        begin = begin + lengths[j]
    prev_doc, last_doc, next_doc = edges
    tri = r_i >= c_i
    eye = r_i == c_i
    joint = jnp.logical_and(tri, doc_col == doc_row)

    def lanes(i):
        return pl.ds(pl.multiple_of(i * HD, HD), HD)

    def pass1(i, carry):
        at = lanes(i)
        q, k, v = q_ref[:, at], k_ref[:, at], v_ref[:, at]
        ld = ld_ref[pl.ds(i, 1), :]
        cum = jnp.sum(jnp.where(tri, ld, 0.0), axis=1, keepdims=True)
        cum_row = jnp.sum(jnp.where(eye, cum, 0.0), axis=0, keepdims=True)
        total = cum[rows - 1 : rows, :]
        decay = jnp.where(joint, jnp.exp(jnp.where(joint, cum - cum_row, 0.0)), 0.0)
        tail = jnp.exp(total - cum)
        enter = jnp.where(doc_col == prev_doc, jnp.exp(cum), 0.0)
        keep = jnp.where(doc_col == last_doc, tail, 0.0)
        leave = jnp.where(doc_col == next_doc, tail, 0.0)
        through = jnp.where(prev_doc == last_doc, jnp.exp(total), 0.0)
        thr[i] = jnp.broadcast_to(through, (8, HD))
        enter_s[i] = jnp.broadcast_to(enter, (rows, HD))
        leave_s[i] = jnp.broadcast_to(leave, (rows, HD))
        sum_f[i] = dot((k.astype(F32) * keep).astype(BF16), v, 0, 0).astype(BF16)
        decay_s[i] = decay
        attn = (dot(q, k, 1, 1) * decay).astype(BF16)
        attn_s[i] = attn
        local[:, at] = dot(attn, v, 1, 0)
        return carry

    lax.fori_loop(0, heads, pass1, 0)

    def fwd_copy(d):
        return rcopy(sum_f, recv_f.at[d - 1], f_ss.at[d - 1], f_rs.at[d - 1], (s + d) % n_seq, h)

    def bwd_copy(d):
        return rcopy(sum_b, recv_b.at[d - 1], b_ss.at[d - 1], b_rs.at[d - 1], (s + n_seq - d) % n_seq, h)

    def thr_copies(d):
        return (
            rcopy(thr, thr_prev.at[d - 1], tp_ss.at[d - 1], tp_rs.at[d - 1], (s + d) % n_seq, h),
            rcopy(thr, thr_next.at[d - 1], tn_ss.at[d - 1], tn_rs.at[d - 1], (s + n_seq - d) % n_seq, h),
        )

    for d in range(1, hops + 1):
        fwd_copy(d).start()
        for copy in thr_copies(d):
            copy.start()
    g_step(1)
    w_plane.forward()
    for d in range(2, n_head - 1):
        g_step(d)
    for d in range(1, hops + 1):
        fwd_copy(d).wait_recv()
        for copy in thr_copies(d):
            copy.wait_recv()

    def combined(i, recv, factors, valid):
        total = jnp.zeros((HD, HD), F32)
        scale = jnp.ones((1, HD), F32)
        for d in range(1, hops + 1):
            total = total + jnp.where(valid(d), recv[d - 1, i].astype(F32) * scale, 0.0)
            scale = scale * factors[d - 1, i, 0:1, :]
        return total.astype(BF16)

    def pass2(i, carry):
        at = lanes(i)
        state = combined(i, recv_f, thr_prev, lambda d: s >= d)
        state_s[i] = state
        out = local[:, at] + dot(q_ref[:, at], state, 1, 0) * enter_s[i]
        a_full[pl.ds(pl.multiple_of(s * rows, rows), rows), at] = out.astype(BF16)
        return carry

    lax.fori_loop(0, heads, pass2, 0)

    a_plane = Plane(a_full.at[pl.ds(pl.multiple_of(s * rows, rows), rows)], a_full, rows, a_ss, a_rs)
    a_plane.start()

    per = gwidth // wrows

    def col_copy(j):
        t = (s + j) % n_seq
        src = g_full.at[t // per, :, pl.ds(pl.multiple_of((t % per) * wrows, wrows), wrows)]
        dst = g_cols.at[pl.ds(pl.multiple_of(s * rows, rows), rows)]
        return rcopy(src, dst, c_ss.at[j - 1], c_rs.at[j - 1], t, h)


    def part(target, store):
        def tile(j, carry):
            at = pl.multiple_of(target * gwidth + j * TILE, TILE)
            value = dot(
                a_full[pl.ds(pl.multiple_of(s * rows, rows), rows), :], w_full[pl.ds(at, TILE), :], 1, 1
            )
            store(pl.ds(pl.multiple_of(j * TILE, TILE), TILE), value)
            return carry

        lax.fori_loop(0, gwidth // TILE, tile, 0)

    def part_copy(j):
        return rcopy(
            part_send.at[j - 1], part_recv.at[j - 1], p_ss.at[j - 1], p_rs.at[j - 1], s, (h + j) % n_head
        )

    def send_part(target, j):
        def keep_part(at, value):
            part_send[j, :, at] = value.astype(BF16)

        part(target, keep_part)
        rcopy(part_send.at[j], part_recv.at[j], p_ss.at[j], p_rs.at[j], s, target).start()

    def send_if_other(target):
        @pl.when(target != h)
        def _():
            send_part(target, (target + n_head - h) % n_head - 1)

    by_chip = side == 2 and n_head == chips and gwidth == 2 * wrows
    w_plane.near()
    if by_chip:
        for target in (chip, xn, yn):
            send_if_other(target)
    g_step(n_head - 1)
    g_cols[pl.ds(pl.multiple_of(s * rows, rows), rows), :] = g_full[
        s // per, :, pl.ds(pl.multiple_of((s % per) * wrows, wrows), wrows)
    ]
    w_plane.finish()
    w_plane.far()
    if by_chip:
        send_if_other(dn)
    else:
        for j in range(1, n_head):
            send_part((h + j) % n_head, j - 1)

    for j in range(1, n_seq // 2):
        col_copy(j).start()

    def pull(j, carry):
        at = pl.ds(pl.multiple_of(j * TILE, TILE), TILE)
        value = jnp.zeros((rows, TILE), F32)
        for b in range(n_head):
            value = value + dot(g_full[b], w_full[b * gwidth : (b + 1) * gwidth, at], 1, 0)
        ga_s[:, at] = value.astype(BF16)
        return carry

    lax.fori_loop(0, width // TILE, pull, 0)

    def pass3(i, carry):
        at = lanes(i)
        g = ga_s[:, at]
        sum_b[i] = dot((q_ref[:, at].astype(F32) * enter_s[i]).astype(BF16), g, 0, 0).astype(BF16)
        return carry

    lax.fori_loop(0, heads, pass3, 0)

    for d in range(1, hops + 1):
        bwd_copy(d).start()
    for j in range(n_seq // 2, n_seq):
        col_copy(j).start()
    a_plane.forward()

    def own_part(at, value):
        local2[:, at] = value

    part(h, own_part)

    def pass4(i, carry):
        at = lanes(i)
        q, k, v, g = q_ref[:, at], k_ref[:, at], v_ref[:, at], ga_s[:, at]
        back = (dot(g, v, 1, 1) * decay_s[i]).astype(BF16)
        gq = dot(back, k, 1, 0) + dot(g, state_s[i], 1, 1) * enter_s[i]
        gq_ref[:, at] = gq.astype(BF16)
        local[:, at] = dot(back, q, 0, 0)
        return carry

    lax.fori_loop(0, heads, pass4, 0)

    a_plane.finish()
    for d in range(1, hops + 1):
        bwd_copy(d).wait_recv()

    def pass5(i, carry):
        at = lanes(i)
        k, v, g = k_ref[:, at], v_ref[:, at], ga_s[:, at]
        state = combined(i, recv_b, thr_next, lambda d: s + d < n_seq)
        gk = local[:, at] + dot(v, state, 1, 1) * leave_s[i]
        gv = dot(attn_s[i], g, 0, 0) + dot(k, state, 1, 0) * leave_s[i]
        gk_ref[:, at] = gk.astype(BF16)
        gv_ref[:, at] = gv.astype(BF16)
        return carry

    lax.fori_loop(0, heads, pass5, 0)

    a_plane.near()
    a_plane.far()
    for j in range(1, n_seq):
        slot = g_cols.at[pl.ds(pl.multiple_of(((s + n_seq - j) % n_seq) * rows, rows), rows)]
        rcopy(slot, slot, c_ss.at[j - 1], c_rs.at[j - 1], (s + j) % n_seq, h).wait_recv()

    mt = min(TILE, wrows)
    depth = min(2048, n_seq * rows)
    for b in range(n_seq * rows // depth):

        def outer(j, carry, b=b):
            m, n = j // (width // TILE), j % (width // TILE)
            rm = pl.ds(pl.multiple_of(m * mt, mt), mt)
            rn = pl.ds(pl.multiple_of(n * TILE, TILE), TILE)
            value = dot(
                g_cols[b * depth : (b + 1) * depth, rm], a_full[b * depth : (b + 1) * depth, rn], 0, 0
            )
            if b > 0:
                value = value + gw_ref[rm, rn]
            gw_ref[rm, rn] = value
            return carry

        lax.fori_loop(0, (wrows // mt) * (width // TILE), outer, 0)

    for j in range(1, n_head):
        part_copy(j).wait_recv()
    total = local2[...]
    for j in range(1, n_head):
        total = total + part_recv[j - 1].astype(F32)
    mixed_ref[...] = total.astype(BF16)

    w_plane.drain()
    a_plane.drain()
    for j in range(1, n_head):
        g_each(j, lambda copy: copy.wait_send())
        part_copy(j).wait_send()
    for j in range(1, n_seq):
        col_copy(j).wait_send()
    for d in range(1, hops + 1):
        fwd_copy(d).wait_send()
        bwd_copy(d).wait_send()
        for copy in thr_copies(d):
            copy.wait_send()


def square_kernel(
    n_head,
    lengths, q_in, k_in, v_in, ld_ref, w_in, g_in,
    mixed_ref, gq_ref, gk_ref, gv_ref, gw_ref,
    q_ref, k_ref, v_ref, w_full, g_full, g_pair, a_pair, z_send, near, fold, merged, wg_send, wg_recv,
    local, local2, decay_s, attn_s, enter_s, leave_s, ga_s, thr,
    sum_f, raw_f, out_f, in_f, sum_b, raw_b, out_b, in_b,
    w_ss, w_rs, g_ss, g_rs, x_ss, x_rs, a_ss, a_rs, z_ss, n_rs, f_rs, m_rs, wg_ss, wg_rs, st_ss, st_rs, l_s,
):
    s, h = lax.axis_index("seq"), lax.axis_index("head")
    n_seq = 8
    rows, width = q_ref.shape
    heads = width // HD
    wrows = w_in.shape[0]
    gwidth = g_in.shape[1]
    half = wrows // 2
    chip, core = s // 2, s % 2
    other = 1 - core
    x, y = chip % 2, chip // 2
    partner = chip * 2 + other
    xn, yn, dn = y * 2 + (1 - x), (1 - y) * 2 + x, (1 - y) * 2 + (1 - x)
    sent = []

    def rcopy(src, dst, ss, rs, seq, head):
        return pltpu.make_async_remote_copy(
            src_ref=src, dst_ref=dst, send_sem=ss, recv_sem=rs,
            device_id=(seq, head), device_id_type=MESH,
        )

    def ship(src, dst, ss, rs, i, seq):
        copy = rcopy(src, dst, ss.at[i], rs.at[i], seq, h)
        copy.start()
        sent.append(copy)

    def got(ref, ss, rs, i):
        rcopy(ref, ref, ss.at[i], rs.at[i], partner, h).wait_recv()

    barrier = pltpu.get_barrier_semaphore()
    for j in range(1, n_seq):
        pl.semaphore_signal(barrier, inc=1, device_id=((s + j) % n_seq, h), device_id_type=MESH)
    for j in range(1, n_head):
        pl.semaphore_signal(barrier, inc=1, device_id=(s, (h + j) % n_head), device_id_type=MESH)

    w_ref = w_full.at[pl.ds(pl.multiple_of(s * wrows, wrows), wrows)]
    g_ref = g_full.at[h]
    loads = [
        pltpu.make_async_copy(src, dst, l_s.at[i])
        for i, (src, dst) in enumerate(
            [(w_in, w_ref), (g_in, g_ref), (q_in, q_ref), (k_in, k_ref), (v_in, v_ref)]
        )
    ]
    for load in loads:
        load.start()
    loads[0].wait()
    loads[1].wait()
    pl.semaphore_wait(barrier, n_seq + n_head - 2)

    def w_at(seq, part):
        return w_full.at[pl.ds(pl.multiple_of(seq * wrows + part * half, half), half)]

    xs, ys = xn * 2 + core, yn * 2 + core
    ship(w_at(s, 0), w_at(s, 0), w_ss, w_rs, 0, xs)
    ship(w_at(s, 1), w_at(s, 1), w_ss, w_rs, 2, ys)

    def g_right(d):
        b = (h + n_head - d + 1) % n_head
        return rcopy(g_full.at[b], g_full.at[b], g_ss.at[d - 1], g_rs.at[d - 1], s, (h + 1) % n_head)

    def g_left(d):
        b, i = (h + d - 1) % n_head, n_head - 2 + d
        return rcopy(g_full.at[b], g_full.at[b], g_ss.at[i], g_rs.at[i], s, (h + n_head - 1) % n_head)

    def g_each(d, act):
        @pl.when(jnp.logical_and(h + 1 < n_head, h >= d - 1))
        def _():
            act(g_right(d))

        @pl.when(jnp.logical_and(h >= 1, h + d - 1 < n_head))
        def _():
            act(g_left(d))

    def core_cols(c):
        return pl.ds(pl.multiple_of(c * wrows, wrows), wrows)

    def core_rows(c):
        return pl.ds(pl.multiple_of(c * rows, rows), rows)

    def g_cross(f, src):
        return rcopy(src.at[:, core_cols(other)], g_pair.at[f, core_rows(core)], x_ss.at[f], x_rs.at[f], partner, h)

    def g_across(f):
        g_cross(f, g_full.at[f]).start()
        g_pair[f, core_rows(core), :] = g_full[f, :, core_cols(core)]

    def g_step(d):
        @pl.when(h >= d)
        def _():
            slot = g_full.at[(h + n_head - d) % n_head]
            rcopy(slot, slot, g_ss.at[d - 1], g_rs.at[d - 1], s, (h + 1) % n_head).wait_recv()

        @pl.when(h + d < n_head)
        def _():
            slot = g_full.at[(h + d) % n_head]
            i = n_head - 2 + d
            rcopy(slot, slot, g_ss.at[i], g_rs.at[i], s, (h + 1) % n_head).wait_recv()

        if d + 1 < n_head:
            g_each(d + 1, lambda copy: copy.start())

        @pl.when(h >= d)
        def _():
            g_across((h + n_head - d) % n_head)

        @pl.when(h + d < n_head)
        def _():
            g_across((h + d) % n_head)

    g_each(1, lambda copy: copy.start())
    ship(w_ref, w_ref, w_ss, w_rs, 8, partner)

    g_across(h)
    for load in loads[2:]:
        load.wait()

    first = s * rows
    r_i = lax.broadcasted_iota(jnp.int32, (rows, rows), 0)
    c_i = lax.broadcasted_iota(jnp.int32, (rows, rows), 1)
    p_col = first + lax.broadcasted_iota(jnp.int32, (rows, 1), 0)
    p_row = first + lax.broadcasted_iota(jnp.int32, (1, rows), 1)
    doc_col = jnp.full((rows, 1), -1, jnp.int32)
    doc_row = jnp.full((1, rows), -1, jnp.int32)
    edges = [jnp.full((1, 1), -1, jnp.int32) for _ in range(3)]
    points = [jnp.full((1, 1), 0, jnp.int32) + p for p in (first - 1, first + rows - 1, first + rows)]
    begin = jnp.int32(0)
    for j in range(lengths.shape[0]):
        doc_col = doc_col + jnp.where(p_col >= begin, 1, 0)
        doc_row = doc_row + jnp.where(p_row >= begin, 1, 0)
        edges = [e + jnp.where(p >= begin, 1, 0) for e, p in zip(edges, points)]
        begin = begin + lengths[j]
    prev_doc, last_doc, next_doc = edges
    tri = r_i >= c_i
    eye = r_i == c_i
    joint = jnp.logical_and(tri, doc_col == doc_row)

    def lanes(i):
        return pl.ds(pl.multiple_of(i * HD, HD), HD)

    def pass1(i, carry):
        at = lanes(i)
        q, k, v = q_ref[:, at], k_ref[:, at], v_ref[:, at]
        ld = ld_ref[pl.ds(i, 1), :]
        cum = jnp.sum(jnp.where(tri, ld, 0.0), axis=1, keepdims=True)
        cum_row = jnp.sum(jnp.where(eye, cum, 0.0), axis=0, keepdims=True)
        total = cum[rows - 1 : rows, :]
        decay = jnp.where(joint, jnp.exp(jnp.where(joint, cum - cum_row, 0.0)), 0.0)
        tail = jnp.exp(total - cum)
        enter = jnp.where(doc_col == prev_doc, jnp.exp(cum), 0.0)
        keep = jnp.where(doc_col == last_doc, tail, 0.0)
        leave = jnp.where(doc_col == next_doc, tail, 0.0)
        through = jnp.where(prev_doc == last_doc, jnp.exp(total), 0.0)
        thr[i] = jnp.broadcast_to(through, (8, HD))
        enter_s[i] = jnp.broadcast_to(enter, (rows, HD))
        leave_s[i] = jnp.broadcast_to(leave, (rows, HD))
        sum_f[i] = dot((k.astype(F32) * keep).astype(BF16), v, 0, 0).astype(BF16)
        decay_s[i] = decay
        attn = (dot(q, k, 1, 1) * decay).astype(BF16)
        attn_s[i] = attn
        local[:, at] = dot(attn, v, 1, 0)
        return carry

    lax.fori_loop(0, heads, pass1, 0)

    def chain(lead, step, sums, raw, out, inn, i):
        to = (s + n_seq + step) % n_seq
        has_next = s < n_seq - 1 if step > 0 else s > 0
        has_last = s > 0 if step > 0 else s < n_seq - 1
        raw_copy = rcopy(sums, raw, st_ss.at[i], st_rs.at[i], to, h)
        out_copy = rcopy(out, inn, st_ss.at[i + 1], st_rs.at[i + 1], to, h)
        leads = core == lead

        def add(base):
            def one(j, carry):
                out[j] = (sums[j].astype(F32) + base[j].astype(F32) * thr[j, 0:1, :]).astype(BF16)
                return carry

            lax.fori_loop(0, heads, one, 0)

        def begin():
            @pl.when(leads)
            def _():
                raw_copy.start()

            @pl.when(jnp.logical_not(leads))
            def _():
                raw_copy.wait_recv()

                @pl.when(has_next)
                def _():
                    add(raw)
                    out_copy.start()

        def end():
            @pl.when(has_last)
            def _():
                out_copy.wait_recv()

            @pl.when(jnp.logical_not(has_last))
            def _():
                inn[...] = jnp.zeros_like(inn)

            @pl.when(leads)
            def _():
                add(inn)
                out_copy.start()

        def drain():
            @pl.when(leads)
            def _():
                raw_copy.wait_send()

            @pl.when(jnp.logical_or(leads, has_next))
            def _():
                out_copy.wait_send()

        return begin, end, drain

    f_begin, f_end, f_drain = chain(0, 1, sum_f, raw_f, out_f, in_f, 0)
    b_begin, b_end, b_drain = chain(1, -1, sum_b, raw_b, out_b, in_b, 2)

    f_begin()
    ship(w_at(s, 1), w_at(s, 1), w_ss, w_rs, 1, xs)
    ship(w_at(s, 0), w_at(s, 0), w_ss, w_rs, 3, ys)

    def w_pass(i, seq, part, ahead, to, across):
        ref = w_at(seq, part)
        got(ref, w_ss, w_rs, i)
        if ahead is not None:
            ship(ref, ref, w_ss, w_rs, ahead, to)
        ship(ref, ref, w_ss, w_rs, across, partner)

    w_pass(0, xs, 0, 4, ys, 9)
    w_pass(2, ys, 1, 5, xs, 10)
    g_step(1)

    f_end()

    def pass2(i, carry):
        at = lanes(i)
        out = local[:, at] + dot(q_ref[:, at], in_f[i], 1, 0) * enter_s[i]
        a_pair[core_rows(core), at] = out.astype(BF16)
        return carry

    lax.fori_loop(0, heads, pass2, 0)

    mine = a_pair.at[core_rows(core)]
    ship(mine, mine, a_ss, a_rs, 0, partner)

    inner = jnp.logical_and(h > 0, h < n_head - 1)
    mate = h + 1 - 2 * (h % 2)

    def part(target, p, store):
        def tile(c, carry):
            at = pl.multiple_of(target * gwidth + c * wrows + p * half, half)
            value = dot(a_pair[core_rows(core), :], w_full[pl.ds(at, half), :], 1, 1)
            store(c, value)
            return carry

        lax.fori_loop(0, gwidth // wrows, tile, 0)

    def chunk_cols(c):
        return pl.ds(pl.multiple_of(c * half, half), half)

    def z_copy(b, p, dst, rs, to):
        return rcopy(z_send.at[b, p], dst, z_ss.at[b * 2 + p], rs, s, to)

    def z_near(b, p):
        z_copy(b, p, near.at[p], n_rs.at[p], mate).start()

    def z_fold(b, p):
        return z_copy(b, p, fold.at[b % 2, p], f_rs.at[(b % 2) * 2 + p], mate)

    def make_parts(chunks):
        for b, p in chunks:

            @pl.when(b != h)
            def _(b=b, p=p):
                def keep_part(c, value):
                    z_send[b, p, :, chunk_cols(c)] = value.astype(BF16)

                part(b, p, keep_part)

            @pl.when(jnp.logical_and(jnp.logical_not(inner), b == mate))
            def _(b=b, p=p):
                z_near(b, p)

            @pl.when(jnp.logical_and(jnp.logical_not(inner), jnp.logical_and(b != h, b != mate)))
            def _(b=b, p=p):
                z_fold(b, p).start()

    def pass_parts(chunks):
        for b, p in chunks:

            @pl.when(jnp.logical_and(inner, b == mate))
            def _(b=b, p=p):
                z_near(b, p)

            @pl.when(jnp.logical_and(inner, jnp.logical_and(b != h, b != mate)))
            def _(b=b, p=p):
                z_fold(b, p).wait_recv()
                z_send[b, p] = (z_send[b, p].astype(F32) + fold[b % 2, p].astype(F32)).astype(BF16)
                z_copy(b, p, merged.at[p], m_rs.at[p], b).start()

    xo, yo, do = xn * 2 + other, yn * 2 + other, dn * 2 + other
    got(w_full.at[pl.ds(pl.multiple_of(partner * wrows, wrows), wrows)], w_ss, w_rs, 8)
    got(w_at(xo, 0), w_ss, w_rs, 9)
    got(w_at(yo, 1), w_ss, w_rs, 10)
    early = [(chip, 0), (chip, 1), (xn, 0), (yn, 1)]
    make_parts(early)

    w_pass(1, xs, 1, None, None, 11)
    w_pass(3, ys, 0, None, None, 12)
    g_step(2)
    got(w_at(xo, 1), w_ss, w_rs, 11)
    got(w_at(yo, 0), w_ss, w_rs, 12)
    middle = [(xn, 1), (yn, 0)]
    make_parts(middle)
    other_half = a_pair.at[core_rows(other)]
    got(other_half, a_ss, a_rs, 0)

    last = n_head - 1 - h
    for f in range(n_head):

        @pl.when(jnp.logical_or(inner, f != last))
        def _(f=f):
            got(g_pair.at[f, core_rows(other)], x_ss, x_rs, f)

    def gw_block(f, part, store):
        def tile(j, carry):
            at = pl.ds(pl.multiple_of(j * TILE, TILE), TILE)
            store(at, dot(g_pair[f, :, part * half : (part + 1) * half], a_pair[:, at], 0, 0))
            return carry

        lax.fori_loop(0, width // TILE, tile, 0)

    def send_gw(i, f, part, to, extra=None):
        def keep_gw(at, value):
            if extra is not None:
                value = value + wg_recv[extra, :, at].astype(F32)
            wg_send[i, :, at] = value.astype(BF16)

        gw_block(f, part, keep_gw)
        ship(wg_send.at[i], wg_recv.at[i], wg_ss, wg_rs, i, to)

    swap = jnp.where(jnp.logical_and(jnp.logical_not(inner), dn == last), 1, 0)
    send_gw(2 * swap, swap * xn + (1 - swap) * dn, 0, xs)
    send_gw(1 + 2 * swap, swap * yn + (1 - swap) * dn, 1, ys)

    w_pass(4, dn * 2 + core, 0, None, None, 13)
    w_pass(5, dn * 2 + core, 1, None, None, 14)
    for d in range(3, n_head):
        g_step(d)
    got(w_at(do, 0), w_ss, w_rs, 13)
    got(w_at(do, 1), w_ss, w_rs, 14)
    late = [(dn, 0), (dn, 1)]
    make_parts(late)

    @pl.when(jnp.logical_not(inner))
    def _():
        got(g_pair.at[last, core_rows(other)], x_ss, x_rs, last)

    send_gw(2 - 2 * swap, swap * dn + (1 - swap) * xn, 0, xs)
    send_gw(3 - 2 * swap, swap * dn + (1 - swap) * yn, 1, ys)
    pass_parts(early)

    def pull(j, carry):
        at = pl.ds(pl.multiple_of(j * TILE, TILE), TILE)
        value = jnp.zeros((rows, TILE), F32)
        for b in range(n_head):
            value = value + dot(g_full[b], w_full[b * gwidth : (b + 1) * gwidth, at], 1, 0)
        ga_s[:, at] = value.astype(BF16)
        return carry

    lax.fori_loop(0, width // TILE, pull, 0)

    def pass3(i, carry):
        at = lanes(i)
        g = ga_s[:, at]
        sum_b[i] = dot((q_ref[:, at].astype(F32) * enter_s[i]).astype(BF16), g, 0, 0).astype(BF16)
        return carry

    lax.fori_loop(0, heads, pass3, 0)
    b_begin()

    got(wg_recv.at[0], wg_ss, wg_rs, 0)
    send_gw(4, yn, 0, ys, 0)
    got(wg_recv.at[1], wg_ss, wg_rs, 1)
    send_gw(5, xn, 1, xs, 1)
    pass_parts(middle + late)

    def pass4(i, carry):
        at = lanes(i)
        q, k, v, g = q_ref[:, at], k_ref[:, at], v_ref[:, at], ga_s[:, at]
        back = (dot(g, v, 1, 1) * decay_s[i]).astype(BF16)
        gq = dot(back, k, 1, 0) + dot(g, in_f[i], 1, 1) * enter_s[i]
        gq_ref[:, at] = gq.astype(BF16)
        local[:, at] = dot(back, q, 0, 0)
        return carry

    lax.fori_loop(0, heads, pass4, 0)

    b_end()

    def pass5(i, carry):
        at = lanes(i)
        k, v, g = k_ref[:, at], v_ref[:, at], ga_s[:, at]
        gk = local[:, at] + dot(v, in_b[i], 1, 1) * leave_s[i]
        gv = dot(attn_s[i], g, 0, 0) + dot(k, in_b[i], 1, 0) * leave_s[i]
        gk_ref[:, at] = gk.astype(BF16)
        gv_ref[:, at] = gv.astype(BF16)
        return carry

    lax.fori_loop(0, heads, pass5, 0)

    for p in range(2):

        def own_part(c, value, p=p):
            local2[:, pl.ds(pl.multiple_of(c * wrows + p * half, half), half)] = value

        part(h, p, own_part)

    for p in range(2):
        got(wg_recv.at[2 + p], wg_ss, wg_rs, 2 + p)

        def keep_own(at, value, p=p):
            gw_ref[p * half : (p + 1) * half, at] = value + wg_recv[2 + p, :, at].astype(F32)

        gw_block(chip, p, keep_own)

    for p in range(2):
        rcopy(near.at[p], near.at[p], z_ss.at[0], n_rs.at[p], s, mate).wait_recv()
        rcopy(merged.at[p], merged.at[p], z_ss.at[0], m_rs.at[p], s, mate).wait_recv()
        for c in range(gwidth // wrows):
            at, cols = pl.ds(c * wrows + p * half, half), pl.ds(c * half, half)
            total = local2[:, at] + near[p, :, cols].astype(F32) + merged[p, :, cols].astype(F32)
            mixed_ref[:, at] = total.astype(BF16)

    for p in range(2):
        got(wg_recv.at[4 + p], wg_ss, wg_rs, 4 + p)
        at = pl.ds(p * half, half)
        gw_ref[at, :] = gw_ref[at, :] + wg_recv[4 + p].astype(F32)

    for copy in sent:
        copy.wait_send()
    for f in range(n_head):
        g_cross(f, g_full.at[f]).wait_send()
    for j in range(1, n_head):
        g_each(j, lambda copy: copy.wait_send())
        for p in range(2):
            z_copy((h + j) % n_head, p, near.at[p], n_rs.at[p], mate).wait_send()
    f_drain()
    b_drain()


def store_kernel(*refs):
    copies = [pltpu.make_async_copy(refs[i], refs[5 + i], refs[10].at[i]) for i in range(5)]
    for copy in copies:
        copy.start()
    for copy in copies:
        copy.wait()


def square_call(n_head, queries, keys, values, log_decay, lengths, out_weight, out_grad):
    rows, width = queries.shape
    heads = log_decay.shape[0]
    wrows = out_weight.shape[0]
    gwidth = out_grad.shape[1]
    dma = lambda n: pltpu.SemaphoreType.DMA((n,))
    vm = pltpu.VMEM
    scratch = [vm((rows, width), BF16)] * 3 + [
        vm((8 * wrows, width), BF16),
        vm((n_head, rows, gwidth), BF16),
        vm((n_head, 2 * rows, wrows), BF16),
        vm((2 * rows, width), BF16),
        vm((n_head, 2, rows, wrows), BF16),
        vm((2, rows, wrows), BF16),
        vm((2, 2, rows, wrows), BF16),
        vm((2, rows, wrows), BF16),
        vm((6, wrows // 2, width), BF16),
        vm((6, wrows // 2, width), BF16),
        vm((rows, width), F32),
        vm((rows, gwidth), F32),
        vm((heads, rows, rows), F32),
        vm((heads, rows, rows), BF16),
        vm((heads, rows, HD), F32),
        vm((heads, rows, HD), F32),
        vm((rows, width), BF16),
        vm((heads, 8, HD), F32),
    ] + [vm((heads, HD, HD), BF16)] * 8 + [
        dma(15), dma(15), dma(2 * n_head - 2), dma(2 * n_head - 2), dma(n_head), dma(n_head), dma(1), dma(1),
        dma(2 * n_head), dma(2), dma(4), dma(2), dma(6), dma(6), dma(4), dma(4), dma(5),
    ]
    spec = pl.BlockSpec(memory_space=pltpu.VMEM)
    anywhere = pl.BlockSpec(memory_space=pl.ANY)
    outs = pl.pallas_call(
        functools.partial(square_kernel, n_head),
        out_shape=[vm((rows, gwidth), BF16)] + [vm((rows, width), BF16)] * 3 + [vm((wrows, width), F32)],
        in_specs=[pl.BlockSpec(memory_space=pltpu.SMEM)] + [anywhere] * 3 + [spec] + [anywhere] * 2,
        out_specs=[spec] * 5,
        scratch_shapes=scratch,
        compiler_params=pltpu.CompilerParams(
            collective_id=1, has_side_effects=True, vmem_limit_bytes=61360 * 1024
        ),
    )(lengths, queries, keys, values, log_decay, out_weight, out_grad)
    return pl.pallas_call(
        store_kernel,
        out_shape=[jax.ShapeDtypeStruct(o.shape, o.dtype) for o in outs],
        in_specs=[spec] * 5,
        out_specs=[anywhere] * 5,
        scratch_shapes=[dma(5)],
        compiler_params=pltpu.CompilerParams(vmem_limit_bytes=1 << 20),
        cost_estimate=pl.CostEstimate(flops=0, bytes_accessed=4 << 20, transcendentals=0),
    )(*[pltpu.with_memory_space_constraint(o, pltpu.VMEM) for o in outs])


def body(n_seq, n_head, queries, keys, values, log_decay, lengths, out_weight, out_grad):
    rows, width = queries.shape
    heads = log_decay.shape[0]
    wrows = out_weight.shape[0]
    gwidth = out_grad.shape[1]
    chips = n_seq // 2
    longest = n_seq * rows // 4
    hops = (longest - 1) // rows + 1
    if chips == 4 and n_head == 4 and gwidth == 2 * wrows and wrows % 32 == 0 and hops == 2:
        return square_call(n_head, queries, keys, values, log_decay, lengths, out_weight, out_grad)
    dma = lambda n: pltpu.SemaphoreType.DMA((n,))
    vm = pltpu.VMEM
    scratch = [
        vm((n_seq * wrows, width), BF16),
        vm((n_seq * rows, width), BF16),
        vm((n_head, rows, gwidth), BF16),
        vm((n_seq * rows, wrows), BF16),
        vm((n_head - 1, rows, gwidth), BF16),
        vm((n_head - 1, rows, gwidth), BF16),
        vm((rows, width), F32),
        vm((rows, gwidth), F32),
        vm((heads, rows, rows), F32),
        vm((heads, rows, rows), BF16),
        vm((heads, rows, HD), F32),
        vm((heads, rows, HD), F32),
        vm((heads, HD, HD), BF16),
        vm((rows, width), BF16),
        vm((heads, 8, HD), F32),
        vm((hops, heads, 8, HD), F32),
        vm((hops, heads, 8, HD), F32),
        vm((heads, HD, HD), BF16),
        vm((heads, HD, HD), BF16),
        vm((hops, heads, HD, HD), BF16),
        vm((hops, heads, HD, HD), BF16),
        dma(2 * chips + 1), dma(2 * chips + 1), dma(2 * chips + 1), dma(2 * chips + 1),
        dma(2 * n_head - 2), dma(2 * n_head - 2), dma(n_seq - 1), dma(n_seq - 1), dma(n_head - 1), dma(n_head - 1),
        dma(hops), dma(hops), dma(hops), dma(hops), dma(hops), dma(hops), dma(hops), dma(hops),
    ]
    spec = pl.BlockSpec(memory_space=pltpu.VMEM)
    return pl.pallas_call(
        functools.partial(kernel, n_seq, n_head, hops),
        out_shape=[vm((rows, gwidth), BF16)] + [vm((rows, width), BF16)] * 3 + [vm((wrows, width), F32)],
        in_specs=[pl.BlockSpec(memory_space=pltpu.SMEM)] + [spec] * 6,
        out_specs=[spec] * 5,
        scratch_shapes=scratch,
        compiler_params=pltpu.CompilerParams(
            collective_id=0, has_side_effects=True, vmem_limit_bytes=61360 * 1024
        ),
    )(lengths, queries, keys, values, log_decay, out_weight, out_grad)


def solution(mesh):
    both = P("seq", "head")
    in_specs = (both, both, both, P("head", "seq"), P(), both, both)
    return jax.shard_map(
        functools.partial(body, mesh.shape["seq"], mesh.shape["head"]),
        mesh=mesh, in_specs=in_specs, out_specs=(both,) * 5, check_vma=False,
    )
```

```python
import functools
import math

import jax
import jax.numpy as jnp
from jax import lax
from jax.experimental import pallas as pl
from jax.experimental.pallas import tpu as pltpu
from jax.sharding import PartitionSpec as P

MESH = pl.DeviceIdType.MESH
F32 = jnp.float32
BF16 = jnp.bfloat16
HD = 128
TILE = 256


def dot(a, b, ca, cb):
    return lax.dot_general(a, b, (((ca,), (cb,)), ((), ())), preferred_element_type=F32)


def kernel(
    n_seq, n_head, hops,
    lengths, q_ref, k_ref, v_ref, ld_ref, w_ref, g_ref,
    mixed_ref, gq_ref, gk_ref, gv_ref, gw_ref,
    w_full, a_full, g_full, g_cols, part_send, part_recv,
    local, local2, decay_s, attn_s, enter_s, leave_s, state_s, ga_s, thr, thr_prev, thr_next,
    sum_f, sum_b, recv_f, recv_b,
    w_ss, w_rs, a_ss, a_rs, g_ss, g_rs, c_ss, c_rs, p_ss, p_rs,
    f_ss, f_rs, b_ss, b_rs, tp_ss, tp_rs, tn_ss, tn_rs,
):
    s, h = lax.axis_index("seq"), lax.axis_index("head")
    rows, width = q_ref.shape
    heads = width // HD
    wrows = w_ref.shape[0]
    gwidth = g_ref.shape[1]
    chips = n_seq // 2
    side = math.isqrt(chips)
    chip, core = s // 2, s % 2
    x, y = chip % side, chip // side
    partner = chip * 2 + (1 - core)
    offs = [(dy, dx) for dy in range(side) for dx in range(side) if (dy, dx) != (0, 0)]

    def rcopy(src, dst, ss, rs, seq, head):
        return pltpu.make_async_remote_copy(
            src_ref=src, dst_ref=dst, send_sem=ss, recv_sem=rs,
            device_id=(seq, head), device_id_type=MESH,
        )

    def away(i, sign):
        dy, dx = offs[i]
        if sign > 0:
            return ((y + dy) % side) * side + (x + dx) % side
        return ((y + side - dy) % side) * side + (x + side - dx) % side

    barrier = pltpu.get_barrier_semaphore()
    for j in range(1, n_seq):
        pl.semaphore_signal(barrier, inc=1, device_id=((s + j) % n_seq, h), device_id_type=MESH)
    for j in range(1, n_head):
        pl.semaphore_signal(barrier, inc=1, device_id=(s, (h + j) % n_head), device_id_type=MESH)
    pl.semaphore_wait(barrier, n_seq + n_head - 2)

    xn, yn, dn = y * side + (1 - x), (1 - y) * side + x, (1 - y) * side + (1 - x)

    class Plane:
        def __init__(self, src, full, size, ss, rs):
            self.src, self.full, self.size, self.ss, self.rs = src, full, size, ss, rs
            self.sent = []

        def block(self, index, half=None):
            at, size = index * self.size, self.size
            if half is not None:
                size = self.size // 2
                at = at + half * size
            return self.full.at[pl.ds(pl.multiple_of(at, size), size)]

        def send(self, src, dst, index, seq):
            copy = rcopy(src, dst, self.ss.at[index], self.rs.at[index], seq, h)
            copy.start()
            self.sent.append(copy)

        def arrived(self, ref, index):
            rcopy(ref, ref, self.ss.at[index], self.rs.at[index], partner, h).wait_recv()

        def pass_on(self, ref, index, cross):
            self.arrived(ref, index)
            self.send(ref, ref, cross, partner)

        def start(self):
            mine = self.block(s)
            if side == 2:
                self.send(self.src, mine, 0, xn * 2 + core)
                self.send(self.src, mine, 1, yn * 2 + core)
            else:
                for i in range(chips - 1):
                    self.send(self.src, mine, i, away(i, 1) * 2 + core)
            self.send(self.src, mine, 2 * chips, partner)

        def forward(self):
            if side == 2:
                bx, by = self.block(xn * 2 + core), self.block(yn * 2 + core)
                hx, hy = self.block(xn * 2 + core, 0), self.block(yn * 2 + core, 1)
                self.arrived(bx, 0)
                self.send(hx, hx, 2, yn * 2 + core)
                self.arrived(by, 1)
                self.send(hy, hy, 3, xn * 2 + core)
                self.send(bx, bx, chips, partner)
                self.send(by, by, chips + 1, partner)

        def finish(self):
            if side == 2:
                for half in range(2):
                    self.pass_on(self.block(dn * 2 + core, half), 2 + half, chips + 2 + half)
            else:
                for i in range(chips - 1):
                    self.pass_on(self.block(away(i, -1) * 2 + core), i, chips + i)

        def near(self):
            other = 1 - core
            if side == 2:
                self.arrived(self.block(xn * 2 + other), chips)
                self.arrived(self.block(yn * 2 + other), chips + 1)
            self.arrived(self.block(partner), 2 * chips)

        def far(self):
            other = 1 - core
            if side == 2:
                for half in range(2):
                    self.arrived(self.block(dn * 2 + other, half), chips + 2 + half)
            else:
                for i in range(chips - 1):
                    self.arrived(self.block(away(i, -1) * 2 + other), chips + i)

        def drain(self):
            for copy in self.sent:
                copy.wait_send()

    w_plane = Plane(w_ref, w_full, wrows, w_ss, w_rs)
    w_plane.start()

    def g_right(d):
        b = (h + n_head - d + 1) % n_head
        src = g_ref if d == 1 else g_full.at[b]
        return rcopy(src, g_full.at[b], g_ss.at[d - 1], g_rs.at[d - 1], s, (h + 1) % n_head)

    def g_left(d):
        b, i = (h + d - 1) % n_head, n_head - 2 + d
        src = g_ref if d == 1 else g_full.at[b]
        return rcopy(src, g_full.at[b], g_ss.at[i], g_rs.at[i], s, (h + n_head - 1) % n_head)

    def g_each(d, act):
        @pl.when(jnp.logical_and(h + 1 < n_head, h >= d - 1))
        def _():
            act(g_right(d))

        @pl.when(jnp.logical_and(h >= 1, h + d - 1 < n_head))
        def _():
            act(g_left(d))

    def g_step(d):
        @pl.when(h >= d)
        def _():
            slot = g_full.at[(h + n_head - d) % n_head]
            rcopy(slot, slot, g_ss.at[d - 1], g_rs.at[d - 1], s, (h + 1) % n_head).wait_recv()

        @pl.when(h + d < n_head)
        def _():
            slot = g_full.at[(h + d) % n_head]
            i = n_head - 2 + d
            rcopy(slot, slot, g_ss.at[i], g_rs.at[i], s, (h + 1) % n_head).wait_recv()

        if d + 1 < n_head:
            g_each(d + 1, lambda copy: copy.start())

    g_each(1, lambda copy: copy.start())

    g_full[h] = g_ref[...]
    w_full[pl.ds(pl.multiple_of(s * wrows, wrows), wrows), :] = w_ref[...]

    first = s * rows
    r_i = lax.broadcasted_iota(jnp.int32, (rows, rows), 0)
    c_i = lax.broadcasted_iota(jnp.int32, (rows, rows), 1)
    p_col = first + lax.broadcasted_iota(jnp.int32, (rows, 1), 0)
    p_row = first + lax.broadcasted_iota(jnp.int32, (1, rows), 1)
    doc_col = jnp.full((rows, 1), -1, jnp.int32)
    doc_row = jnp.full((1, rows), -1, jnp.int32)
    edges = [jnp.full((1, 1), -1, jnp.int32) for _ in range(3)]
    points = [jnp.full((1, 1), 0, jnp.int32) + p for p in (first - 1, first + rows - 1, first + rows)]
    begin = jnp.int32(0)
    for j in range(lengths.shape[0]):
        doc_col = doc_col + jnp.where(p_col >= begin, 1, 0)
        doc_row = doc_row + jnp.where(p_row >= begin, 1, 0)
        edges = [e + jnp.where(p >= begin, 1, 0) for e, p in zip(edges, points)]
        begin = begin + lengths[j]
    prev_doc, last_doc, next_doc = edges
    tri = r_i >= c_i
    eye = r_i == c_i
    joint = jnp.logical_and(tri, doc_col == doc_row)

    def lanes(i):
        return pl.ds(pl.multiple_of(i * HD, HD), HD)

    def pass1(i, carry):
        at = lanes(i)
        q, k, v = q_ref[:, at], k_ref[:, at], v_ref[:, at]
        ld = ld_ref[pl.ds(i, 1), :]
        cum = jnp.sum(jnp.where(tri, ld, 0.0), axis=1, keepdims=True)
        cum_row = jnp.sum(jnp.where(eye, cum, 0.0), axis=0, keepdims=True)
        total = cum[rows - 1 : rows, :]
        decay = jnp.where(joint, jnp.exp(jnp.where(joint, cum - cum_row, 0.0)), 0.0)
        tail = jnp.exp(total - cum)
        enter = jnp.where(doc_col == prev_doc, jnp.exp(cum), 0.0)
        keep = jnp.where(doc_col == last_doc, tail, 0.0)
        leave = jnp.where(doc_col == next_doc, tail, 0.0)
        through = jnp.where(prev_doc == last_doc, jnp.exp(total), 0.0)
        thr[i] = jnp.broadcast_to(through, (8, HD))
        enter_s[i] = jnp.broadcast_to(enter, (rows, HD))
        leave_s[i] = jnp.broadcast_to(leave, (rows, HD))
        sum_f[i] = dot((k.astype(F32) * keep).astype(BF16), v, 0, 0).astype(BF16)
        decay_s[i] = decay
        attn = (dot(q, k, 1, 1) * decay).astype(BF16)
        attn_s[i] = attn
        local[:, at] = dot(attn, v, 1, 0)
        return carry

    lax.fori_loop(0, heads, pass1, 0)

    def fwd_copy(d):
        return rcopy(sum_f, recv_f.at[d - 1], f_ss.at[d - 1], f_rs.at[d - 1], (s + d) % n_seq, h)

    def bwd_copy(d):
        return rcopy(sum_b, recv_b.at[d - 1], b_ss.at[d - 1], b_rs.at[d - 1], (s + n_seq - d) % n_seq, h)

    def thr_copies(d):
        return (
            rcopy(thr, thr_prev.at[d - 1], tp_ss.at[d - 1], tp_rs.at[d - 1], (s + d) % n_seq, h),
            rcopy(thr, thr_next.at[d - 1], tn_ss.at[d - 1], tn_rs.at[d - 1], (s + n_seq - d) % n_seq, h),
        )

    for d in range(1, hops + 1):
        fwd_copy(d).start()
        for copy in thr_copies(d):
            copy.start()
    g_step(1)
    w_plane.forward()
    for d in range(2, n_head - 1):
        g_step(d)
    for d in range(1, hops + 1):
        fwd_copy(d).wait_recv()
        for copy in thr_copies(d):
            copy.wait_recv()

    def combined(i, recv, factors, valid):
        total = jnp.zeros((HD, HD), F32)
        scale = jnp.ones((1, HD), F32)
        for d in range(1, hops + 1):
            total = total + jnp.where(valid(d), recv[d - 1, i].astype(F32) * scale, 0.0)
            scale = scale * factors[d - 1, i, 0:1, :]
        return total.astype(BF16)

    def pass2(i, carry):
        at = lanes(i)
        state = combined(i, recv_f, thr_prev, lambda d: s >= d)
        state_s[i] = state
        out = local[:, at] + dot(q_ref[:, at], state, 1, 0) * enter_s[i]
        a_full[pl.ds(pl.multiple_of(s * rows, rows), rows), at] = out.astype(BF16)
        return carry

    lax.fori_loop(0, heads, pass2, 0)

    a_plane = Plane(a_full.at[pl.ds(pl.multiple_of(s * rows, rows), rows)], a_full, rows, a_ss, a_rs)
    a_plane.start()

    per = gwidth // wrows

    def col_copy(j):
        t = (s + j) % n_seq
        src = g_full.at[t // per, :, pl.ds(pl.multiple_of((t % per) * wrows, wrows), wrows)]
        dst = g_cols.at[pl.ds(pl.multiple_of(s * rows, rows), rows)]
        return rcopy(src, dst, c_ss.at[j - 1], c_rs.at[j - 1], t, h)


    def part(target, store):
        def tile(j, carry):
            at = pl.multiple_of(target * gwidth + j * TILE, TILE)
            value = dot(
                a_full[pl.ds(pl.multiple_of(s * rows, rows), rows), :], w_full[pl.ds(at, TILE), :], 1, 1
            )
            store(pl.ds(pl.multiple_of(j * TILE, TILE), TILE), value)
            return carry

        lax.fori_loop(0, gwidth // TILE, tile, 0)

    def part_copy(j):
        return rcopy(
            part_send.at[j - 1], part_recv.at[j - 1], p_ss.at[j - 1], p_rs.at[j - 1], s, (h + j) % n_head
        )

    def send_part(target, j):
        def keep_part(at, value):
            part_send[j, :, at] = value.astype(BF16)

        part(target, keep_part)
        rcopy(part_send.at[j], part_recv.at[j], p_ss.at[j], p_rs.at[j], s, target).start()

    def send_if_other(target):
        @pl.when(target != h)
        def _():
            send_part(target, (target + n_head - h) % n_head - 1)

    by_chip = side == 2 and n_head == chips and gwidth == 2 * wrows
    w_plane.near()
    if by_chip:
        for target in (chip, xn, yn):
            send_if_other(target)
    g_step(n_head - 1)
    g_cols[pl.ds(pl.multiple_of(s * rows, rows), rows), :] = g_full[
        s // per, :, pl.ds(pl.multiple_of((s % per) * wrows, wrows), wrows)
    ]
    w_plane.finish()
    w_plane.far()
    if by_chip:
        send_if_other(dn)
    else:
        for j in range(1, n_head):
            send_part((h + j) % n_head, j - 1)

    for j in range(1, n_seq // 2):
        col_copy(j).start()

    def pull(j, carry):
        at = pl.ds(pl.multiple_of(j * TILE, TILE), TILE)
        value = jnp.zeros((rows, TILE), F32)
        for b in range(n_head):
            value = value + dot(g_full[b], w_full[b * gwidth : (b + 1) * gwidth, at], 1, 0)
        ga_s[:, at] = value.astype(BF16)
        return carry

    lax.fori_loop(0, width // TILE, pull, 0)

    def pass3(i, carry):
        at = lanes(i)
        g = ga_s[:, at]
        sum_b[i] = dot((q_ref[:, at].astype(F32) * enter_s[i]).astype(BF16), g, 0, 0).astype(BF16)
        return carry

    lax.fori_loop(0, heads, pass3, 0)

    for d in range(1, hops + 1):
        bwd_copy(d).start()
    for j in range(n_seq // 2, n_seq):
        col_copy(j).start()
    a_plane.forward()

    def own_part(at, value):
        local2[:, at] = value

    part(h, own_part)

    def pass4(i, carry):
        at = lanes(i)
        q, k, v, g = q_ref[:, at], k_ref[:, at], v_ref[:, at], ga_s[:, at]
        back = (dot(g, v, 1, 1) * decay_s[i]).astype(BF16)
        gq = dot(back, k, 1, 0) + dot(g, state_s[i], 1, 1) * enter_s[i]
        gq_ref[:, at] = gq.astype(BF16)
        local[:, at] = dot(back, q, 0, 0)
        return carry

    lax.fori_loop(0, heads, pass4, 0)

    a_plane.finish()
    for d in range(1, hops + 1):
        bwd_copy(d).wait_recv()

    def pass5(i, carry):
        at = lanes(i)
        k, v, g = k_ref[:, at], v_ref[:, at], ga_s[:, at]
        state = combined(i, recv_b, thr_next, lambda d: s + d < n_seq)
        gk = local[:, at] + dot(v, state, 1, 1) * leave_s[i]
        gv = dot(attn_s[i], g, 0, 0) + dot(k, state, 1, 0) * leave_s[i]
        gk_ref[:, at] = gk.astype(BF16)
        gv_ref[:, at] = gv.astype(BF16)
        return carry

    lax.fori_loop(0, heads, pass5, 0)

    a_plane.near()
    a_plane.far()
    for j in range(1, n_seq):
        slot = g_cols.at[pl.ds(pl.multiple_of(((s + n_seq - j) % n_seq) * rows, rows), rows)]
        rcopy(slot, slot, c_ss.at[j - 1], c_rs.at[j - 1], (s + j) % n_seq, h).wait_recv()

    mt = min(TILE, wrows)
    depth = min(2048, n_seq * rows)
    for b in range(n_seq * rows // depth):

        def outer(j, carry, b=b):
            m, n = j // (width // TILE), j % (width // TILE)
            rm = pl.ds(pl.multiple_of(m * mt, mt), mt)
            rn = pl.ds(pl.multiple_of(n * TILE, TILE), TILE)
            value = dot(
                g_cols[b * depth : (b + 1) * depth, rm], a_full[b * depth : (b + 1) * depth, rn], 0, 0
            )
            if b > 0:
                value = value + gw_ref[rm, rn]
            gw_ref[rm, rn] = value
            return carry

        lax.fori_loop(0, (wrows // mt) * (width // TILE), outer, 0)

    for j in range(1, n_head):
        part_copy(j).wait_recv()
    total = local2[...]
    for j in range(1, n_head):
        total = total + part_recv[j - 1].astype(F32)
    mixed_ref[...] = total.astype(BF16)

    w_plane.drain()
    a_plane.drain()
    for j in range(1, n_head):
        g_each(j, lambda copy: copy.wait_send())
        part_copy(j).wait_send()
    for j in range(1, n_seq):
        col_copy(j).wait_send()
    for d in range(1, hops + 1):
        fwd_copy(d).wait_send()
        bwd_copy(d).wait_send()
        for copy in thr_copies(d):
            copy.wait_send()


def square_kernel(
    n_head,
    lengths, q_in, k_in, v_in, ld_ref, w_in, g_in,
    mixed_ref, gq_ref, gk_ref, gv_ref, gw_ref,
    q_ref, k_ref, v_ref, w_full, g_full, g_pair, a_pair, z_send, near, fold, merged, wg_send, wg_recv,
    local, local2, decay_s, attn_s, enter_s, leave_s, ga_s, thr,
    sum_f, raw_f, out_f, in_f, sum_b, raw_b, out_b, in_b,
    w_ss, w_rs, g_ss, g_rs, x_ss, x_rs, a_ss, a_rs, z_ss, n_rs, f_rs, m_rs, wg_ss, wg_rs, st_ss, st_rs, l_s,
):
    s, h = lax.axis_index("seq"), lax.axis_index("head")
    n_seq = 8
    rows, width = q_ref.shape
    heads = width // HD
    wrows = w_in.shape[0]
    gwidth = g_in.shape[1]
    half = wrows // 2
    chip, core = s // 2, s % 2
    other = 1 - core
    x, y = chip % 2, chip // 2
    partner = chip * 2 + other
    xn, yn, dn = y * 2 + (1 - x), (1 - y) * 2 + x, (1 - y) * 2 + (1 - x)
    sent = []

    def rcopy(src, dst, ss, rs, seq, head):
        return pltpu.make_async_remote_copy(
            src_ref=src, dst_ref=dst, send_sem=ss, recv_sem=rs,
            device_id=(seq, head), device_id_type=MESH,
        )

    def ship(src, dst, ss, rs, i, seq):
        copy = rcopy(src, dst, ss.at[i], rs.at[i], seq, h)
        copy.start()
        sent.append(copy)

    def got(ref, ss, rs, i):
        rcopy(ref, ref, ss.at[i], rs.at[i], partner, h).wait_recv()

    barrier = pltpu.get_barrier_semaphore()
    for j in range(1, n_seq):
        pl.semaphore_signal(barrier, inc=1, device_id=((s + j) % n_seq, h), device_id_type=MESH)
    for j in range(1, n_head):
        pl.semaphore_signal(barrier, inc=1, device_id=(s, (h + j) % n_head), device_id_type=MESH)

    w_ref = w_full.at[pl.ds(pl.multiple_of(s * wrows, wrows), wrows)]
    g_ref = g_full.at[h]
    loads = [
        pltpu.make_async_copy(src, dst, l_s.at[i])
        for i, (src, dst) in enumerate(
            [(w_in, w_ref), (g_in, g_ref), (q_in, q_ref), (k_in, k_ref), (v_in, v_ref)]
        )
    ]
    for load in loads:
        load.start()
    loads[0].wait()
    loads[1].wait()
    pl.semaphore_wait(barrier, n_seq + n_head - 2)

    def w_at(seq, part):
        return w_full.at[pl.ds(pl.multiple_of(seq * wrows + part * half, half), half)]

    xs, ys = xn * 2 + core, yn * 2 + core
    ship(w_at(s, 0), w_at(s, 0), w_ss, w_rs, 0, xs)
    ship(w_at(s, 1), w_at(s, 1), w_ss, w_rs, 2, ys)

    def g_right(d):
        b = (h + n_head - d + 1) % n_head
        return rcopy(g_full.at[b], g_full.at[b], g_ss.at[d - 1], g_rs.at[d - 1], s, (h + 1) % n_head)

    def g_left(d):
        b, i = (h + d - 1) % n_head, n_head - 2 + d
        return rcopy(g_full.at[b], g_full.at[b], g_ss.at[i], g_rs.at[i], s, (h + n_head - 1) % n_head)

    def g_each(d, act):
        @pl.when(jnp.logical_and(h + 1 < n_head, h >= d - 1))
        def _():
            act(g_right(d))

        @pl.when(jnp.logical_and(h >= 1, h + d - 1 < n_head))
        def _():
            act(g_left(d))

    def core_cols(c):
        return pl.ds(pl.multiple_of(c * wrows, wrows), wrows)

    def core_rows(c):
        return pl.ds(pl.multiple_of(c * rows, rows), rows)

    def g_cross(f, src):
        return rcopy(src.at[:, core_cols(other)], g_pair.at[f, core_rows(core)], x_ss.at[f], x_rs.at[f], partner, h)

    def g_across(f):
        g_cross(f, g_full.at[f]).start()
        g_pair[f, core_rows(core), :] = g_full[f, :, core_cols(core)]

    def g_step(d):
        @pl.when(h >= d)
        def _():
            slot = g_full.at[(h + n_head - d) % n_head]
            rcopy(slot, slot, g_ss.at[d - 1], g_rs.at[d - 1], s, (h + 1) % n_head).wait_recv()

        @pl.when(h + d < n_head)
        def _():
            slot = g_full.at[(h + d) % n_head]
            i = n_head - 2 + d
            rcopy(slot, slot, g_ss.at[i], g_rs.at[i], s, (h + 1) % n_head).wait_recv()

        if d + 1 < n_head:
            g_each(d + 1, lambda copy: copy.start())

        @pl.when(h >= d)
        def _():
            g_across((h + n_head - d) % n_head)

        @pl.when(h + d < n_head)
        def _():
            g_across((h + d) % n_head)

    g_each(1, lambda copy: copy.start())
    ship(w_ref, w_ref, w_ss, w_rs, 8, partner)

    g_across(h)
    for load in loads[2:]:
        load.wait()

    first = s * rows
    r_i = lax.broadcasted_iota(jnp.int32, (rows, rows), 0)
    c_i = lax.broadcasted_iota(jnp.int32, (rows, rows), 1)
    p_col = first + lax.broadcasted_iota(jnp.int32, (rows, 1), 0)
    p_row = first + lax.broadcasted_iota(jnp.int32, (1, rows), 1)
    doc_col = jnp.full((rows, 1), -1, jnp.int32)
    doc_row = jnp.full((1, rows), -1, jnp.int32)
    edges = [jnp.full((1, 1), -1, jnp.int32) for _ in range(3)]
    points = [jnp.full((1, 1), 0, jnp.int32) + p for p in (first - 1, first + rows - 1, first + rows)]
    begin = jnp.int32(0)
    for j in range(lengths.shape[0]):
        doc_col = doc_col + jnp.where(p_col >= begin, 1, 0)
        doc_row = doc_row + jnp.where(p_row >= begin, 1, 0)
        edges = [e + jnp.where(p >= begin, 1, 0) for e, p in zip(edges, points)]
        begin = begin + lengths[j]
    prev_doc, last_doc, next_doc = edges
    tri = r_i >= c_i
    eye = r_i == c_i
    joint = jnp.logical_and(tri, doc_col == doc_row)

    def lanes(i):
        return pl.ds(pl.multiple_of(i * HD, HD), HD)

    def pass1(i, carry):
        at = lanes(i)
        q, k, v = q_ref[:, at], k_ref[:, at], v_ref[:, at]
        ld = ld_ref[pl.ds(i, 1), :]
        cum = jnp.sum(jnp.where(tri, ld, 0.0), axis=1, keepdims=True)
        cum_row = jnp.sum(jnp.where(eye, cum, 0.0), axis=0, keepdims=True)
        total = cum[rows - 1 : rows, :]
        decay = jnp.where(joint, jnp.exp(jnp.where(joint, cum - cum_row, 0.0)), 0.0)
        tail = jnp.exp(total - cum)
        enter = jnp.where(doc_col == prev_doc, jnp.exp(cum), 0.0)
        keep = jnp.where(doc_col == last_doc, tail, 0.0)
        leave = jnp.where(doc_col == next_doc, tail, 0.0)
        through = jnp.where(prev_doc == last_doc, jnp.exp(total), 0.0)
        thr[i] = jnp.broadcast_to(through, (8, HD))
        enter_s[i] = jnp.broadcast_to(enter, (rows, HD))
        leave_s[i] = jnp.broadcast_to(leave, (rows, HD))
        sum_f[i] = dot((k.astype(F32) * keep).astype(BF16), v, 0, 0).astype(BF16)
        decay_s[i] = decay
        attn = (dot(q, k, 1, 1) * decay).astype(BF16)
        attn_s[i] = attn
        local[:, at] = dot(attn, v, 1, 0)
        return carry

    lax.fori_loop(0, heads, pass1, 0)

    def chain(lead, step, sums, raw, out, inn, i):
        to = (s + n_seq + step) % n_seq
        has_next = s < n_seq - 1 if step > 0 else s > 0
        has_last = s > 0 if step > 0 else s < n_seq - 1
        raw_copy = rcopy(sums, raw, st_ss.at[i], st_rs.at[i], to, h)
        out_copy = rcopy(out, inn, st_ss.at[i + 1], st_rs.at[i + 1], to, h)
        leads = core == lead

        def add(base):
            def one(j, carry):
                out[j] = (sums[j].astype(F32) + base[j].astype(F32) * thr[j, 0:1, :]).astype(BF16)
                return carry

            lax.fori_loop(0, heads, one, 0)

        def begin():
            @pl.when(leads)
            def _():
                raw_copy.start()

            @pl.when(jnp.logical_not(leads))
            def _():
                raw_copy.wait_recv()

                @pl.when(has_next)
                def _():
                    add(raw)
                    out_copy.start()

        def end():
            @pl.when(has_last)
            def _():
                out_copy.wait_recv()

            @pl.when(jnp.logical_not(has_last))
            def _():
                inn[...] = jnp.zeros_like(inn)

            @pl.when(leads)
            def _():
                add(inn)
                out_copy.start()

        def drain():
            @pl.when(leads)
            def _():
                raw_copy.wait_send()

            @pl.when(jnp.logical_or(leads, has_next))
            def _():
                out_copy.wait_send()

        return begin, end, drain

    f_begin, f_end, f_drain = chain(0, 1, sum_f, raw_f, out_f, in_f, 0)
    b_begin, b_end, b_drain = chain(1, -1, sum_b, raw_b, out_b, in_b, 2)

    f_begin()
    ship(w_at(s, 1), w_at(s, 1), w_ss, w_rs, 1, xs)
    ship(w_at(s, 0), w_at(s, 0), w_ss, w_rs, 3, ys)

    skew = wrows // 8

    def w_some(seq, start, count):
        return w_full.at[pl.ds(pl.multiple_of(seq * wrows + start, skew), count)]

    def w_pass(i, ref, across, ahead=None, part=None, to=None):
        got(ref, w_ss, w_rs, i)
        if ahead is not None:
            ship(part, part, w_ss, w_rs, ahead, to)
        ship(ref, ref, w_ss, w_rs, across, partner)

    w_pass(0, w_at(xs, 0), 9, 4, w_at(xs, 0), ys)
    w_pass(2, w_at(ys, 1), 10, 5, w_some(ys, half + skew, half - skew), xs)
    g_step(1)

    f_end()

    def pass2(i, carry):
        at = lanes(i)
        out = local[:, at] + dot(q_ref[:, at], in_f[i], 1, 0) * enter_s[i]
        a_pair[core_rows(core), at] = out.astype(BF16)
        return carry

    lax.fori_loop(0, heads, pass2, 0)

    mine = a_pair.at[core_rows(core)]
    ship(mine, mine, a_ss, a_rs, 0, partner)

    inner = jnp.logical_and(h > 0, h < n_head - 1)
    mate = h + 1 - 2 * (h % 2)

    def part(target, p, store):
        def tile(c, carry):
            at = pl.multiple_of(target * gwidth + c * wrows + p * half, half)
            value = dot(a_pair[core_rows(core), :], w_full[pl.ds(at, half), :], 1, 1)
            store(c, value)
            return carry

        lax.fori_loop(0, gwidth // wrows, tile, 0)

    def chunk_cols(c):
        return pl.ds(pl.multiple_of(c * half, half), half)

    def z_copy(b, p, dst, rs, to):
        return rcopy(z_send.at[b, p], dst, z_ss.at[b * 2 + p], rs, s, to)

    def z_near(b, p):
        z_copy(b, p, near.at[p], n_rs.at[p], mate).start()

    def z_fold(b, p):
        return z_copy(b, p, fold.at[b % 2, p], f_rs.at[(b % 2) * 2 + p], mate)

    def make_parts(chunks):
        for b, p in chunks:

            @pl.when(b != h)
            def _(b=b, p=p):
                def keep_part(c, value):
                    z_send[b, p, :, chunk_cols(c)] = value.astype(BF16)

                part(b, p, keep_part)

            @pl.when(jnp.logical_and(jnp.logical_not(inner), jnp.logical_and(b != h, b != mate)))
            def _(b=b, p=p):
                z_fold(b, p).start()

    def pass_parts(chunks):
        for b, p in chunks:

            @pl.when(jnp.logical_and(inner, b == mate))
            def _(b=b, p=p):
                z_near(b, p)

            @pl.when(jnp.logical_and(inner, jnp.logical_and(b != h, b != mate)))
            def _(b=b, p=p):
                z_fold(b, p).wait_recv()
                z_send[b, p] = (z_send[b, p].astype(F32) + fold[b % 2, p].astype(F32)).astype(BF16)
                z_copy(b, p, merged.at[p], m_rs.at[p], b).start()

    xo, yo, do = xn * 2 + other, yn * 2 + other, dn * 2 + other
    got(w_full.at[pl.ds(pl.multiple_of(partner * wrows, wrows), wrows)], w_ss, w_rs, 8)
    got(w_at(xo, 0), w_ss, w_rs, 9)
    got(w_at(yo, 1), w_ss, w_rs, 10)
    early = [(chip, 0), (chip, 1), (xn, 0), (yn, 1)]
    make_parts(early)

    w_pass(1, w_at(xs, 1), 11, 6, w_some(xs, half, skew), ys)
    w_pass(3, w_at(ys, 0), 12)
    g_step(2)
    got(w_at(xo, 1), w_ss, w_rs, 11)
    got(w_at(yo, 0), w_ss, w_rs, 12)
    middle = [(xn, 1), (yn, 0)]
    make_parts(middle)
    other_half = a_pair.at[core_rows(other)]
    got(other_half, a_ss, a_rs, 0)

    last = n_head - 1 - h
    for f in range(n_head):

        @pl.when(jnp.logical_or(inner, f != last))
        def _(f=f):
            got(g_pair.at[f, core_rows(other)], x_ss, x_rs, f)

    def gw_block(f, part, store):
        def tile(j, carry):
            at = pl.ds(pl.multiple_of(j * TILE, TILE), TILE)
            store(at, dot(g_pair[f, :, part * half : (part + 1) * half], a_pair[:, at], 0, 0))
            return carry

        lax.fori_loop(0, width // TILE, tile, 0)

    def send_gw(i, f, part, to, extra=None):
        def keep_gw(at, value):
            if extra is not None:
                value = value + wg_recv[extra, :, at].astype(F32)
            wg_send[i, :, at] = value.astype(BF16)

        gw_block(f, part, keep_gw)
        ship(wg_send.at[i], wg_recv.at[i], wg_ss, wg_rs, i, to)

    def pull(f, store):
        def tile(j, carry):
            at = pl.ds(pl.multiple_of(j * TILE, TILE), TILE)
            store(at, dot(g_full[f], w_full[pl.ds(pl.multiple_of(f * gwidth, gwidth), gwidth), at], 1, 0))
            return carry

        lax.fori_loop(0, width // TILE, tile, 0)

    def pull_more(at, value):
        local[:, at] = local[:, at] + value

    def pull_last(at, value):
        ga_s[:, at] = (local[:, at] + value).astype(BF16)

    local[...] = jnp.zeros_like(local)
    for f in (chip, xn, yn):

        @pl.when(jnp.logical_or(inner, f != last))
        def _(f=f):
            pull(f, pull_more)

    swap = jnp.where(jnp.logical_and(jnp.logical_not(inner), dn == last), 1, 0)
    send_gw(2 * swap, swap * xn + (1 - swap) * dn, 0, xs)
    send_gw(1 + 2 * swap, swap * yn + (1 - swap) * dn, 1, ys)

    ds = dn * 2 + core
    w_pass(4, w_at(ds, 0), 13)
    w_pass(6, w_some(ds, half, skew), 15)
    w_pass(5, w_some(ds, half + skew, half - skew), 14)
    for d in range(3, n_head):
        g_step(d)
    got(w_at(do, 0), w_ss, w_rs, 13)
    got(w_some(do, half, skew), w_ss, w_rs, 15)
    got(w_some(do, half + skew, half - skew), w_ss, w_rs, 14)
    late = [(dn, 0), (dn, 1)]
    make_parts(late)

    @pl.when(jnp.logical_not(inner))
    def _():
        z_near(mate, 0)
        z_near(mate, 1)


    @pl.when(jnp.logical_not(inner))
    def _():
        got(g_pair.at[last, core_rows(other)], x_ss, x_rs, last)

    send_gw(2 - 2 * swap, swap * dn + (1 - swap) * xn, 0, xs)
    send_gw(3 - 2 * swap, swap * dn + (1 - swap) * yn, 1, ys)
    pass_parts(early)

    @pl.when(jnp.logical_and(jnp.logical_not(inner), dn != last))
    def _():
        pull(last, pull_more)

    pull(dn, pull_last)

    def pass3(i, carry):
        at = lanes(i)
        g = ga_s[:, at]
        sum_b[i] = dot((q_ref[:, at].astype(F32) * enter_s[i]).astype(BF16), g, 0, 0).astype(BF16)
        return carry

    lax.fori_loop(0, heads, pass3, 0)
    b_begin()
    pass_parts(middle)

    got(wg_recv.at[0], wg_ss, wg_rs, 0)
    send_gw(4, yn, 0, ys, 0)
    got(wg_recv.at[1], wg_ss, wg_rs, 1)
    send_gw(5, xn, 1, xs, 1)
    pass_parts(late)

    def pass4(i, carry):
        at = lanes(i)
        q, k, v, g = q_ref[:, at], k_ref[:, at], v_ref[:, at], ga_s[:, at]
        back = (dot(g, v, 1, 1) * decay_s[i]).astype(BF16)
        gq = dot(back, k, 1, 0) + dot(g, in_f[i], 1, 1) * enter_s[i]
        gq_ref[:, at] = gq.astype(BF16)
        local[:, at] = dot(back, q, 0, 0)
        return carry

    lax.fori_loop(0, heads, pass4, 0)

    for p in range(2):

        def own_part(c, value, p=p):
            local2[:, pl.ds(pl.multiple_of(c * wrows + p * half, half), half)] = value

        part(h, p, own_part)

    for p in range(2):

        def keep_own(at, value, p=p):
            gw_ref[p * half : (p + 1) * half, at] = value

        gw_block(chip, p, keep_own)

    b_end()

    def pass5(i, carry):
        at = lanes(i)
        k, v, g = k_ref[:, at], v_ref[:, at], ga_s[:, at]
        gk = local[:, at] + dot(v, in_b[i], 1, 1) * leave_s[i]
        gv = dot(attn_s[i], g, 0, 0) + dot(k, in_b[i], 1, 0) * leave_s[i]
        gk_ref[:, at] = gk.astype(BF16)
        gv_ref[:, at] = gv.astype(BF16)
        return carry

    lax.fori_loop(0, heads, pass5, 0)

    for p in range(2):
        rcopy(near.at[p], near.at[p], z_ss.at[0], n_rs.at[p], s, mate).wait_recv()
        rcopy(merged.at[p], merged.at[p], z_ss.at[0], m_rs.at[p], s, mate).wait_recv()
        for c in range(gwidth // wrows):
            at, cols = pl.ds(c * wrows + p * half, half), pl.ds(c * half, half)
            total = local2[:, at] + near[p, :, cols].astype(F32) + merged[p, :, cols].astype(F32)
            mixed_ref[:, at] = total.astype(BF16)

    for p in range(2):
        got(wg_recv.at[2 + p], wg_ss, wg_rs, 2 + p)
        got(wg_recv.at[4 + p], wg_ss, wg_rs, 4 + p)
        at = pl.ds(p * half, half)
        gw_ref[at, :] = gw_ref[at, :] + (wg_recv[2 + p].astype(F32) + wg_recv[4 + p].astype(F32))

    for copy in sent:
        copy.wait_send()
    for f in range(n_head):
        g_cross(f, g_full.at[f]).wait_send()
    for j in range(1, n_head):
        g_each(j, lambda copy: copy.wait_send())
        for p in range(2):
            z_copy((h + j) % n_head, p, near.at[p], n_rs.at[p], mate).wait_send()
    f_drain()
    b_drain()


def store_kernel(*refs):
    copies = [pltpu.make_async_copy(refs[i], refs[5 + i], refs[10].at[i]) for i in range(5)]
    for copy in copies:
        copy.start()
    for copy in copies:
        copy.wait()


def square_call(n_head, queries, keys, values, log_decay, lengths, out_weight, out_grad):
    rows, width = queries.shape
    heads = log_decay.shape[0]
    wrows = out_weight.shape[0]
    gwidth = out_grad.shape[1]
    dma = lambda n: pltpu.SemaphoreType.DMA((n,))
    vm = pltpu.VMEM
    scratch = [vm((rows, width), BF16)] * 3 + [
        vm((8 * wrows, width), BF16),
        vm((n_head, rows, gwidth), BF16),
        vm((n_head, 2 * rows, wrows), BF16),
        vm((2 * rows, width), BF16),
        vm((n_head, 2, rows, wrows), BF16),
        vm((2, rows, wrows), BF16),
        vm((2, 2, rows, wrows), BF16),
        vm((2, rows, wrows), BF16),
        vm((6, wrows // 2, width), BF16),
        vm((6, wrows // 2, width), BF16),
        vm((rows, width), F32),
        vm((rows, gwidth), F32),
        vm((heads, rows, rows), F32),
        vm((heads, rows, rows), BF16),
        vm((heads, rows, HD), F32),
        vm((heads, rows, HD), F32),
        vm((rows, width), BF16),
        vm((heads, 8, HD), F32),
    ] + [vm((heads, HD, HD), BF16)] * 8 + [
        dma(16), dma(16), dma(2 * n_head - 2), dma(2 * n_head - 2), dma(n_head), dma(n_head), dma(1), dma(1),
        dma(2 * n_head), dma(2), dma(4), dma(2), dma(6), dma(6), dma(4), dma(4), dma(5),
    ]
    spec = pl.BlockSpec(memory_space=pltpu.VMEM)
    anywhere = pl.BlockSpec(memory_space=pl.ANY)
    outs = pl.pallas_call(
        functools.partial(square_kernel, n_head),
        out_shape=[vm((rows, gwidth), BF16)] + [vm((rows, width), BF16)] * 3 + [vm((wrows, width), F32)],
        in_specs=[pl.BlockSpec(memory_space=pltpu.SMEM)] + [anywhere] * 3 + [spec] + [anywhere] * 2,
        out_specs=[spec] * 5,
        scratch_shapes=scratch,
        compiler_params=pltpu.CompilerParams(
            collective_id=1, has_side_effects=True, vmem_limit_bytes=61360 * 1024
        ),
    )(lengths, queries, keys, values, log_decay, out_weight, out_grad)
    return pl.pallas_call(
        store_kernel,
        out_shape=[jax.ShapeDtypeStruct(o.shape, o.dtype) for o in outs],
        in_specs=[spec] * 5,
        out_specs=[anywhere] * 5,
        scratch_shapes=[dma(5)],
        compiler_params=pltpu.CompilerParams(vmem_limit_bytes=1 << 20),
        cost_estimate=pl.CostEstimate(flops=0, bytes_accessed=4 << 20, transcendentals=0),
    )(*[pltpu.with_memory_space_constraint(o, pltpu.VMEM) for o in outs])


def body(n_seq, n_head, queries, keys, values, log_decay, lengths, out_weight, out_grad):
    rows, width = queries.shape
    heads = log_decay.shape[0]
    wrows = out_weight.shape[0]
    gwidth = out_grad.shape[1]
    chips = n_seq // 2
    longest = n_seq * rows // 4
    hops = (longest - 1) // rows + 1
    if chips == 4 and n_head == 4 and gwidth == 2 * wrows and wrows % 256 == 0 and hops == 2:
        return square_call(n_head, queries, keys, values, log_decay, lengths, out_weight, out_grad)
    dma = lambda n: pltpu.SemaphoreType.DMA((n,))
    vm = pltpu.VMEM
    scratch = [
        vm((n_seq * wrows, width), BF16),
        vm((n_seq * rows, width), BF16),
        vm((n_head, rows, gwidth), BF16),
        vm((n_seq * rows, wrows), BF16),
        vm((n_head - 1, rows, gwidth), BF16),
        vm((n_head - 1, rows, gwidth), BF16),
        vm((rows, width), F32),
        vm((rows, gwidth), F32),
        vm((heads, rows, rows), F32),
        vm((heads, rows, rows), BF16),
        vm((heads, rows, HD), F32),
        vm((heads, rows, HD), F32),
        vm((heads, HD, HD), BF16),
        vm((rows, width), BF16),
        vm((heads, 8, HD), F32),
        vm((hops, heads, 8, HD), F32),
        vm((hops, heads, 8, HD), F32),
        vm((heads, HD, HD), BF16),
        vm((heads, HD, HD), BF16),
        vm((hops, heads, HD, HD), BF16),
        vm((hops, heads, HD, HD), BF16),
        dma(2 * chips + 1), dma(2 * chips + 1), dma(2 * chips + 1), dma(2 * chips + 1),
        dma(2 * n_head - 2), dma(2 * n_head - 2), dma(n_seq - 1), dma(n_seq - 1), dma(n_head - 1), dma(n_head - 1),
        dma(hops), dma(hops), dma(hops), dma(hops), dma(hops), dma(hops), dma(hops), dma(hops),
    ]
    spec = pl.BlockSpec(memory_space=pltpu.VMEM)
    return pl.pallas_call(
        functools.partial(kernel, n_seq, n_head, hops),
        out_shape=[vm((rows, gwidth), BF16)] + [vm((rows, width), BF16)] * 3 + [vm((wrows, width), F32)],
        in_specs=[pl.BlockSpec(memory_space=pltpu.SMEM)] + [spec] * 6,
        out_specs=[spec] * 5,
        scratch_shapes=scratch,
        compiler_params=pltpu.CompilerParams(
            collective_id=0, has_side_effects=True, vmem_limit_bytes=61360 * 1024
        ),
    )(lengths, queries, keys, values, log_decay, out_weight, out_grad)


def solution(mesh):
    both = P("seq", "head")
    in_specs = (both, both, both, P("head", "seq"), P(), both, both)
    return jax.shard_map(
        functools.partial(body, mesh.shape["seq"], mesh.shape["head"]),
        mesh=mesh, in_specs=in_specs, out_specs=(both,) * 5, check_vma=False,
    )
```

```python
import functools
import math

import jax
import jax.numpy as jnp
from jax import lax
from jax.experimental import pallas as pl
from jax.experimental.pallas import tpu as pltpu
from jax.sharding import PartitionSpec as P

MESH = pl.DeviceIdType.MESH
F32 = jnp.float32
BF16 = jnp.bfloat16
HD = 128
TILE = 256


def dot(a, b, ca, cb):
    return lax.dot_general(a, b, (((ca,), (cb,)), ((), ())), preferred_element_type=F32)


def kernel(
    n_seq, n_head, hops,
    lengths, q_ref, k_ref, v_ref, ld_ref, w_ref, g_ref,
    mixed_ref, gq_ref, gk_ref, gv_ref, gw_ref,
    w_full, a_full, g_full, g_cols, part_send, part_recv,
    local, local2, decay_s, attn_s, enter_s, leave_s, state_s, ga_s, thr, thr_prev, thr_next,
    sum_f, sum_b, recv_f, recv_b,
    w_ss, w_rs, a_ss, a_rs, g_ss, g_rs, c_ss, c_rs, p_ss, p_rs,
    f_ss, f_rs, b_ss, b_rs, tp_ss, tp_rs, tn_ss, tn_rs,
):
    s, h = lax.axis_index("seq"), lax.axis_index("head")
    rows, width = q_ref.shape
    heads = width // HD
    wrows = w_ref.shape[0]
    gwidth = g_ref.shape[1]
    chips = n_seq // 2
    side = math.isqrt(chips)
    chip, core = s // 2, s % 2
    x, y = chip % side, chip // side
    partner = chip * 2 + (1 - core)
    offs = [(dy, dx) for dy in range(side) for dx in range(side) if (dy, dx) != (0, 0)]

    def rcopy(src, dst, ss, rs, seq, head):
        return pltpu.make_async_remote_copy(
            src_ref=src, dst_ref=dst, send_sem=ss, recv_sem=rs,
            device_id=(seq, head), device_id_type=MESH,
        )

    def away(i, sign):
        dy, dx = offs[i]
        if sign > 0:
            return ((y + dy) % side) * side + (x + dx) % side
        return ((y + side - dy) % side) * side + (x + side - dx) % side

    barrier = pltpu.get_barrier_semaphore()
    for j in range(1, n_seq):
        pl.semaphore_signal(barrier, inc=1, device_id=((s + j) % n_seq, h), device_id_type=MESH)
    for j in range(1, n_head):
        pl.semaphore_signal(barrier, inc=1, device_id=(s, (h + j) % n_head), device_id_type=MESH)
    pl.semaphore_wait(barrier, n_seq + n_head - 2)

    xn, yn, dn = y * side + (1 - x), (1 - y) * side + x, (1 - y) * side + (1 - x)

    class Plane:
        def __init__(self, src, full, size, ss, rs):
            self.src, self.full, self.size, self.ss, self.rs = src, full, size, ss, rs
            self.sent = []

        def block(self, index, half=None):
            at, size = index * self.size, self.size
            if half is not None:
                size = self.size // 2
                at = at + half * size
            return self.full.at[pl.ds(pl.multiple_of(at, size), size)]

        def send(self, src, dst, index, seq):
            copy = rcopy(src, dst, self.ss.at[index], self.rs.at[index], seq, h)
            copy.start()
            self.sent.append(copy)

        def arrived(self, ref, index):
            rcopy(ref, ref, self.ss.at[index], self.rs.at[index], partner, h).wait_recv()

        def pass_on(self, ref, index, cross):
            self.arrived(ref, index)
            self.send(ref, ref, cross, partner)

        def start(self):
            mine = self.block(s)
            if side == 2:
                self.send(self.src, mine, 0, xn * 2 + core)
                self.send(self.src, mine, 1, yn * 2 + core)
            else:
                for i in range(chips - 1):
                    self.send(self.src, mine, i, away(i, 1) * 2 + core)
            self.send(self.src, mine, 2 * chips, partner)

        def forward(self):
            if side == 2:
                bx, by = self.block(xn * 2 + core), self.block(yn * 2 + core)
                hx, hy = self.block(xn * 2 + core, 0), self.block(yn * 2 + core, 1)
                self.arrived(bx, 0)
                self.send(hx, hx, 2, yn * 2 + core)
                self.arrived(by, 1)
                self.send(hy, hy, 3, xn * 2 + core)
                self.send(bx, bx, chips, partner)
                self.send(by, by, chips + 1, partner)

        def finish(self):
            if side == 2:
                for half in range(2):
                    self.pass_on(self.block(dn * 2 + core, half), 2 + half, chips + 2 + half)
            else:
                for i in range(chips - 1):
                    self.pass_on(self.block(away(i, -1) * 2 + core), i, chips + i)

        def near(self):
            other = 1 - core
            if side == 2:
                self.arrived(self.block(xn * 2 + other), chips)
                self.arrived(self.block(yn * 2 + other), chips + 1)
            self.arrived(self.block(partner), 2 * chips)

        def far(self):
            other = 1 - core
            if side == 2:
                for half in range(2):
                    self.arrived(self.block(dn * 2 + other, half), chips + 2 + half)
            else:
                for i in range(chips - 1):
                    self.arrived(self.block(away(i, -1) * 2 + other), chips + i)

        def drain(self):
            for copy in self.sent:
                copy.wait_send()

    w_plane = Plane(w_ref, w_full, wrows, w_ss, w_rs)
    w_plane.start()

    def g_right(d):
        b = (h + n_head - d + 1) % n_head
        src = g_ref if d == 1 else g_full.at[b]
        return rcopy(src, g_full.at[b], g_ss.at[d - 1], g_rs.at[d - 1], s, (h + 1) % n_head)

    def g_left(d):
        b, i = (h + d - 1) % n_head, n_head - 2 + d
        src = g_ref if d == 1 else g_full.at[b]
        return rcopy(src, g_full.at[b], g_ss.at[i], g_rs.at[i], s, (h + n_head - 1) % n_head)

    def g_each(d, act):
        @pl.when(jnp.logical_and(h + 1 < n_head, h >= d - 1))
        def _():
            act(g_right(d))

        @pl.when(jnp.logical_and(h >= 1, h + d - 1 < n_head))
        def _():
            act(g_left(d))

    def g_step(d):
        @pl.when(h >= d)
        def _():
            slot = g_full.at[(h + n_head - d) % n_head]
            rcopy(slot, slot, g_ss.at[d - 1], g_rs.at[d - 1], s, (h + 1) % n_head).wait_recv()

        @pl.when(h + d < n_head)
        def _():
            slot = g_full.at[(h + d) % n_head]
            i = n_head - 2 + d
            rcopy(slot, slot, g_ss.at[i], g_rs.at[i], s, (h + 1) % n_head).wait_recv()

        if d + 1 < n_head:
            g_each(d + 1, lambda copy: copy.start())

    g_each(1, lambda copy: copy.start())

    g_full[h] = g_ref[...]
    w_full[pl.ds(pl.multiple_of(s * wrows, wrows), wrows), :] = w_ref[...]

    first = s * rows
    r_i = lax.broadcasted_iota(jnp.int32, (rows, rows), 0)
    c_i = lax.broadcasted_iota(jnp.int32, (rows, rows), 1)
    p_col = first + lax.broadcasted_iota(jnp.int32, (rows, 1), 0)
    p_row = first + lax.broadcasted_iota(jnp.int32, (1, rows), 1)
    doc_col = jnp.full((rows, 1), -1, jnp.int32)
    doc_row = jnp.full((1, rows), -1, jnp.int32)
    edges = [jnp.full((1, 1), -1, jnp.int32) for _ in range(3)]
    points = [jnp.full((1, 1), 0, jnp.int32) + p for p in (first - 1, first + rows - 1, first + rows)]
    begin = jnp.int32(0)
    for j in range(lengths.shape[0]):
        doc_col = doc_col + jnp.where(p_col >= begin, 1, 0)
        doc_row = doc_row + jnp.where(p_row >= begin, 1, 0)
        edges = [e + jnp.where(p >= begin, 1, 0) for e, p in zip(edges, points)]
        begin = begin + lengths[j]
    prev_doc, last_doc, next_doc = edges
    tri = r_i >= c_i
    eye = r_i == c_i
    joint = jnp.logical_and(tri, doc_col == doc_row)

    def lanes(i):
        return pl.ds(pl.multiple_of(i * HD, HD), HD)

    def pass1(i, carry):
        at = lanes(i)
        q, k, v = q_ref[:, at], k_ref[:, at], v_ref[:, at]
        ld = ld_ref[pl.ds(i, 1), :]
        cum = jnp.sum(jnp.where(tri, ld, 0.0), axis=1, keepdims=True)
        cum_row = jnp.sum(jnp.where(eye, cum, 0.0), axis=0, keepdims=True)
        total = cum[rows - 1 : rows, :]
        decay = jnp.where(joint, jnp.exp(jnp.where(joint, cum - cum_row, 0.0)), 0.0)
        tail = jnp.exp(total - cum)
        enter = jnp.where(doc_col == prev_doc, jnp.exp(cum), 0.0)
        keep = jnp.where(doc_col == last_doc, tail, 0.0)
        leave = jnp.where(doc_col == next_doc, tail, 0.0)
        through = jnp.where(prev_doc == last_doc, jnp.exp(total), 0.0)
        thr[i] = jnp.broadcast_to(through, (8, HD))
        enter_s[i] = jnp.broadcast_to(enter, (rows, HD))
        leave_s[i] = jnp.broadcast_to(leave, (rows, HD))
        sum_f[i] = dot((k.astype(F32) * keep).astype(BF16), v, 0, 0).astype(BF16)
        decay_s[i] = decay
        attn = (dot(q, k, 1, 1) * decay).astype(BF16)
        attn_s[i] = attn
        local[:, at] = dot(attn, v, 1, 0)
        return carry

    lax.fori_loop(0, heads, pass1, 0)

    def fwd_copy(d):
        return rcopy(sum_f, recv_f.at[d - 1], f_ss.at[d - 1], f_rs.at[d - 1], (s + d) % n_seq, h)

    def bwd_copy(d):
        return rcopy(sum_b, recv_b.at[d - 1], b_ss.at[d - 1], b_rs.at[d - 1], (s + n_seq - d) % n_seq, h)

    def thr_copies(d):
        return (
            rcopy(thr, thr_prev.at[d - 1], tp_ss.at[d - 1], tp_rs.at[d - 1], (s + d) % n_seq, h),
            rcopy(thr, thr_next.at[d - 1], tn_ss.at[d - 1], tn_rs.at[d - 1], (s + n_seq - d) % n_seq, h),
        )

    for d in range(1, hops + 1):
        fwd_copy(d).start()
        for copy in thr_copies(d):
            copy.start()
    g_step(1)
    w_plane.forward()
    for d in range(2, n_head - 1):
        g_step(d)
    for d in range(1, hops + 1):
        fwd_copy(d).wait_recv()
        for copy in thr_copies(d):
            copy.wait_recv()

    def combined(i, recv, factors, valid):
        total = jnp.zeros((HD, HD), F32)
        scale = jnp.ones((1, HD), F32)
        for d in range(1, hops + 1):
            total = total + jnp.where(valid(d), recv[d - 1, i].astype(F32) * scale, 0.0)
            scale = scale * factors[d - 1, i, 0:1, :]
        return total.astype(BF16)

    def pass2(i, carry):
        at = lanes(i)
        state = combined(i, recv_f, thr_prev, lambda d: s >= d)
        state_s[i] = state
        out = local[:, at] + dot(q_ref[:, at], state, 1, 0) * enter_s[i]
        a_full[pl.ds(pl.multiple_of(s * rows, rows), rows), at] = out.astype(BF16)
        return carry

    lax.fori_loop(0, heads, pass2, 0)

    a_plane = Plane(a_full.at[pl.ds(pl.multiple_of(s * rows, rows), rows)], a_full, rows, a_ss, a_rs)
    a_plane.start()

    per = gwidth // wrows

    def col_copy(j):
        t = (s + j) % n_seq
        src = g_full.at[t // per, :, pl.ds(pl.multiple_of((t % per) * wrows, wrows), wrows)]
        dst = g_cols.at[pl.ds(pl.multiple_of(s * rows, rows), rows)]
        return rcopy(src, dst, c_ss.at[j - 1], c_rs.at[j - 1], t, h)


    def part(target, store):
        def tile(j, carry):
            at = pl.multiple_of(target * gwidth + j * TILE, TILE)
            value = dot(
                a_full[pl.ds(pl.multiple_of(s * rows, rows), rows), :], w_full[pl.ds(at, TILE), :], 1, 1
            )
            store(pl.ds(pl.multiple_of(j * TILE, TILE), TILE), value)
            return carry

        lax.fori_loop(0, gwidth // TILE, tile, 0)

    def part_copy(j):
        return rcopy(
            part_send.at[j - 1], part_recv.at[j - 1], p_ss.at[j - 1], p_rs.at[j - 1], s, (h + j) % n_head
        )

    def send_part(target, j):
        def keep_part(at, value):
            part_send[j, :, at] = value.astype(BF16)

        part(target, keep_part)
        rcopy(part_send.at[j], part_recv.at[j], p_ss.at[j], p_rs.at[j], s, target).start()

    def send_if_other(target):
        @pl.when(target != h)
        def _():
            send_part(target, (target + n_head - h) % n_head - 1)

    by_chip = side == 2 and n_head == chips and gwidth == 2 * wrows
    w_plane.near()
    if by_chip:
        for target in (chip, xn, yn):
            send_if_other(target)
    g_step(n_head - 1)
    g_cols[pl.ds(pl.multiple_of(s * rows, rows), rows), :] = g_full[
        s // per, :, pl.ds(pl.multiple_of((s % per) * wrows, wrows), wrows)
    ]
    w_plane.finish()
    w_plane.far()
    if by_chip:
        send_if_other(dn)
    else:
        for j in range(1, n_head):
            send_part((h + j) % n_head, j - 1)

    for j in range(1, n_seq // 2):
        col_copy(j).start()

    def pull(j, carry):
        at = pl.ds(pl.multiple_of(j * TILE, TILE), TILE)
        value = jnp.zeros((rows, TILE), F32)
        for b in range(n_head):
            value = value + dot(g_full[b], w_full[b * gwidth : (b + 1) * gwidth, at], 1, 0)
        ga_s[:, at] = value.astype(BF16)
        return carry

    lax.fori_loop(0, width // TILE, pull, 0)

    def pass3(i, carry):
        at = lanes(i)
        g = ga_s[:, at]
        sum_b[i] = dot((q_ref[:, at].astype(F32) * enter_s[i]).astype(BF16), g, 0, 0).astype(BF16)
        return carry

    lax.fori_loop(0, heads, pass3, 0)

    for d in range(1, hops + 1):
        bwd_copy(d).start()
    for j in range(n_seq // 2, n_seq):
        col_copy(j).start()
    a_plane.forward()

    def own_part(at, value):
        local2[:, at] = value

    part(h, own_part)

    def pass4(i, carry):
        at = lanes(i)
        q, k, v, g = q_ref[:, at], k_ref[:, at], v_ref[:, at], ga_s[:, at]
        back = (dot(g, v, 1, 1) * decay_s[i]).astype(BF16)
        gq = dot(back, k, 1, 0) + dot(g, state_s[i], 1, 1) * enter_s[i]
        gq_ref[:, at] = gq.astype(BF16)
        local[:, at] = dot(back, q, 0, 0)
        return carry

    lax.fori_loop(0, heads, pass4, 0)

    a_plane.finish()
    for d in range(1, hops + 1):
        bwd_copy(d).wait_recv()

    def pass5(i, carry):
        at = lanes(i)
        k, v, g = k_ref[:, at], v_ref[:, at], ga_s[:, at]
        state = combined(i, recv_b, thr_next, lambda d: s + d < n_seq)
        gk = local[:, at] + dot(v, state, 1, 1) * leave_s[i]
        gv = dot(attn_s[i], g, 0, 0) + dot(k, state, 1, 0) * leave_s[i]
        gk_ref[:, at] = gk.astype(BF16)
        gv_ref[:, at] = gv.astype(BF16)
        return carry

    lax.fori_loop(0, heads, pass5, 0)

    a_plane.near()
    a_plane.far()
    for j in range(1, n_seq):
        slot = g_cols.at[pl.ds(pl.multiple_of(((s + n_seq - j) % n_seq) * rows, rows), rows)]
        rcopy(slot, slot, c_ss.at[j - 1], c_rs.at[j - 1], (s + j) % n_seq, h).wait_recv()

    mt = min(TILE, wrows)
    depth = min(2048, n_seq * rows)
    for b in range(n_seq * rows // depth):

        def outer(j, carry, b=b):
            m, n = j // (width // TILE), j % (width // TILE)
            rm = pl.ds(pl.multiple_of(m * mt, mt), mt)
            rn = pl.ds(pl.multiple_of(n * TILE, TILE), TILE)
            value = dot(
                g_cols[b * depth : (b + 1) * depth, rm], a_full[b * depth : (b + 1) * depth, rn], 0, 0
            )
            if b > 0:
                value = value + gw_ref[rm, rn]
            gw_ref[rm, rn] = value
            return carry

        lax.fori_loop(0, (wrows // mt) * (width // TILE), outer, 0)

    for j in range(1, n_head):
        part_copy(j).wait_recv()
    total = local2[...]
    for j in range(1, n_head):
        total = total + part_recv[j - 1].astype(F32)
    mixed_ref[...] = total.astype(BF16)

    w_plane.drain()
    a_plane.drain()
    for j in range(1, n_head):
        g_each(j, lambda copy: copy.wait_send())
        part_copy(j).wait_send()
    for j in range(1, n_seq):
        col_copy(j).wait_send()
    for d in range(1, hops + 1):
        fwd_copy(d).wait_send()
        bwd_copy(d).wait_send()
        for copy in thr_copies(d):
            copy.wait_send()


def square_kernel(
    n_head,
    lengths, q_in, k_in, v_in, ld_ref, w_in, g_in,
    mixed_ref, gq_ref, gk_ref, gv_ref, gw_ref,
    q_ref, k_ref, v_ref, w_full, g_full, g_pair, a_pair, z_send, near, fold, merged, wg_send, wg_recv,
    local, local2, decay_s, attn_s, enter_s, leave_s, ga_s, thr,
    sum_f, raw_f, out_f, in_f, sum_b, raw_b, out_b, in_b,
    w_ss, w_rs, g_ss, g_rs, x_ss, x_rs, a_ss, a_rs, z_ss, n_rs, f_rs, m_rs, wg_ss, wg_rs, st_ss, st_rs, l_s,
):
    s, h = lax.axis_index("seq"), lax.axis_index("head")
    n_seq = 8
    rows, width = q_ref.shape
    heads = width // HD
    wrows = w_in.shape[0]
    gwidth = g_in.shape[1]
    half = wrows // 2
    chip, core = s // 2, s % 2
    other = 1 - core
    x, y = chip % 2, chip // 2
    partner = chip * 2 + other
    xn, yn, dn = y * 2 + (1 - x), (1 - y) * 2 + x, (1 - y) * 2 + (1 - x)
    sent = []

    def rcopy(src, dst, ss, rs, seq, head):
        return pltpu.make_async_remote_copy(
            src_ref=src, dst_ref=dst, send_sem=ss, recv_sem=rs,
            device_id=(seq, head), device_id_type=MESH,
        )

    def ship(src, dst, ss, rs, i, seq):
        copy = rcopy(src, dst, ss.at[i], rs.at[i], seq, h)
        copy.start()
        sent.append(copy)

    def got(ref, ss, rs, i):
        rcopy(ref, ref, ss.at[i], rs.at[i], partner, h).wait_recv()

    barrier = pltpu.get_barrier_semaphore()
    for j in range(1, n_seq):
        pl.semaphore_signal(barrier, inc=1, device_id=((s + j) % n_seq, h), device_id_type=MESH)
    for j in range(1, n_head):
        pl.semaphore_signal(barrier, inc=1, device_id=(s, (h + j) % n_head), device_id_type=MESH)

    w_ref = w_full.at[pl.ds(pl.multiple_of(s * wrows, wrows), wrows)]
    g_ref = g_full.at[h]
    loads = [
        pltpu.make_async_copy(src, dst, l_s.at[i])
        for i, (src, dst) in enumerate(
            [(w_in, w_ref), (g_in, g_ref), (q_in, q_ref), (k_in, k_ref), (v_in, v_ref)]
        )
    ]
    for load in loads:
        load.start()
    loads[0].wait()
    loads[1].wait()
    pl.semaphore_wait(barrier, n_seq + n_head - 2)

    def w_at(seq, part):
        return w_full.at[pl.ds(pl.multiple_of(seq * wrows + part * half, half), half)]

    xs, ys = xn * 2 + core, yn * 2 + core
    ship(w_at(s, 0), w_at(s, 0), w_ss, w_rs, 0, xs)
    ship(w_at(s, 1), w_at(s, 1), w_ss, w_rs, 2, ys)

    def g_right(d):
        b = (h + n_head - d + 1) % n_head
        return rcopy(g_full.at[b], g_full.at[b], g_ss.at[d - 1], g_rs.at[d - 1], s, (h + 1) % n_head)

    def g_left(d):
        b, i = (h + d - 1) % n_head, n_head - 2 + d
        return rcopy(g_full.at[b], g_full.at[b], g_ss.at[i], g_rs.at[i], s, (h + n_head - 1) % n_head)

    def g_each(d, act):
        @pl.when(jnp.logical_and(h + 1 < n_head, h >= d - 1))
        def _():
            act(g_right(d))

        @pl.when(jnp.logical_and(h >= 1, h + d - 1 < n_head))
        def _():
            act(g_left(d))

    def core_cols(c):
        return pl.ds(pl.multiple_of(c * wrows, wrows), wrows)

    def core_rows(c):
        return pl.ds(pl.multiple_of(c * rows, rows), rows)

    def g_cross(f, src):
        return rcopy(src.at[:, core_cols(other)], g_pair.at[f, core_rows(core)], x_ss.at[f], x_rs.at[f], partner, h)

    def g_across(f):
        g_cross(f, g_full.at[f]).start()
        g_pair[f, core_rows(core), :] = g_full[f, :, core_cols(core)]

    def g_step(d):
        @pl.when(h >= d)
        def _():
            slot = g_full.at[(h + n_head - d) % n_head]
            rcopy(slot, slot, g_ss.at[d - 1], g_rs.at[d - 1], s, (h + 1) % n_head).wait_recv()

        @pl.when(h + d < n_head)
        def _():
            slot = g_full.at[(h + d) % n_head]
            i = n_head - 2 + d
            rcopy(slot, slot, g_ss.at[i], g_rs.at[i], s, (h + 1) % n_head).wait_recv()

        if d + 1 < n_head:
            g_each(d + 1, lambda copy: copy.start())

        @pl.when(h >= d)
        def _():
            g_across((h + n_head - d) % n_head)

        @pl.when(h + d < n_head)
        def _():
            g_across((h + d) % n_head)

    g_each(1, lambda copy: copy.start())
    ship(w_ref, w_ref, w_ss, w_rs, 8, partner)

    g_across(h)
    for load in loads[2:]:
        load.wait()

    first = s * rows
    r_i = lax.broadcasted_iota(jnp.int32, (rows, rows), 0)
    c_i = lax.broadcasted_iota(jnp.int32, (rows, rows), 1)
    p_col = first + lax.broadcasted_iota(jnp.int32, (rows, 1), 0)
    p_row = first + lax.broadcasted_iota(jnp.int32, (1, rows), 1)
    doc_col = jnp.full((rows, 1), -1, jnp.int32)
    doc_row = jnp.full((1, rows), -1, jnp.int32)
    edges = [jnp.full((1, 1), -1, jnp.int32) for _ in range(3)]
    points = [jnp.full((1, 1), 0, jnp.int32) + p for p in (first - 1, first + rows - 1, first + rows)]
    begin = jnp.int32(0)
    for j in range(lengths.shape[0]):
        doc_col = doc_col + jnp.where(p_col >= begin, 1, 0)
        doc_row = doc_row + jnp.where(p_row >= begin, 1, 0)
        edges = [e + jnp.where(p >= begin, 1, 0) for e, p in zip(edges, points)]
        begin = begin + lengths[j]
    prev_doc, last_doc, next_doc = edges
    tri = r_i >= c_i
    eye = r_i == c_i
    joint = jnp.logical_and(tri, doc_col == doc_row)

    def lanes(i):
        return pl.ds(pl.multiple_of(i * HD, HD), HD)

    def pass1(i, carry):
        at = lanes(i)
        q, k, v = q_ref[:, at], k_ref[:, at], v_ref[:, at]
        ld = ld_ref[pl.ds(i, 1), :]
        cum = jnp.sum(jnp.where(tri, ld, 0.0), axis=1, keepdims=True)
        cum_row = jnp.sum(jnp.where(eye, cum, 0.0), axis=0, keepdims=True)
        total = cum[rows - 1 : rows, :]
        decay = jnp.where(joint, jnp.exp(jnp.where(joint, cum - cum_row, 0.0)), 0.0)
        tail = jnp.exp(total - cum)
        enter = jnp.where(doc_col == prev_doc, jnp.exp(cum), 0.0)
        keep = jnp.where(doc_col == last_doc, tail, 0.0)
        leave = jnp.where(doc_col == next_doc, tail, 0.0)
        through = jnp.where(prev_doc == last_doc, jnp.exp(total), 0.0)
        thr[i] = jnp.broadcast_to(through, (8, HD))
        enter_s[i] = jnp.broadcast_to(enter, (rows, HD))
        leave_s[i] = jnp.broadcast_to(leave, (rows, HD))
        sum_f[i] = dot((k.astype(F32) * keep).astype(BF16), v, 0, 0).astype(BF16)
        decay_s[i] = decay
        attn = (dot(q, k, 1, 1) * decay).astype(BF16)
        attn_s[i] = attn
        local[:, at] = dot(attn, v, 1, 0)
        return carry

    lax.fori_loop(0, heads, pass1, 0)

    def chain(lead, step, sums, raw, out, inn, i):
        to = (s + n_seq + step) % n_seq
        has_next = s < n_seq - 1 if step > 0 else s > 0
        has_last = s > 0 if step > 0 else s < n_seq - 1
        raw_copy = rcopy(sums, raw, st_ss.at[i], st_rs.at[i], to, h)
        out_copy = rcopy(out, inn, st_ss.at[i + 1], st_rs.at[i + 1], to, h)
        leads = core == lead

        def add(base):
            def one(j, carry):
                out[j] = (sums[j].astype(F32) + base[j].astype(F32) * thr[j, 0:1, :]).astype(BF16)
                return carry

            lax.fori_loop(0, heads, one, 0)

        def begin():
            @pl.when(leads)
            def _():
                raw_copy.start()

            @pl.when(jnp.logical_not(leads))
            def _():
                raw_copy.wait_recv()

                @pl.when(has_next)
                def _():
                    add(raw)
                    out_copy.start()

        def end():
            @pl.when(has_last)
            def _():
                out_copy.wait_recv()

            @pl.when(jnp.logical_not(has_last))
            def _():
                inn[...] = jnp.zeros_like(inn)

            @pl.when(leads)
            def _():
                add(inn)
                out_copy.start()

        def drain():
            @pl.when(leads)
            def _():
                raw_copy.wait_send()

            @pl.when(jnp.logical_or(leads, has_next))
            def _():
                out_copy.wait_send()

        return begin, end, drain

    f_begin, f_end, f_drain = chain(0, 1, sum_f, raw_f, out_f, in_f, 0)
    b_begin, b_end, b_drain = chain(1, -1, sum_b, raw_b, out_b, in_b, 2)

    f_begin()
    ship(w_at(s, 1), w_at(s, 1), w_ss, w_rs, 1, xs)
    ship(w_at(s, 0), w_at(s, 0), w_ss, w_rs, 3, ys)

    skew = wrows // 8

    def w_some(seq, start, count):
        return w_full.at[pl.ds(pl.multiple_of(seq * wrows + start, skew), count)]

    def w_pass(i, ref, across, ahead=None, part=None, to=None):
        got(ref, w_ss, w_rs, i)
        if ahead is not None:
            ship(part, part, w_ss, w_rs, ahead, to)
        ship(ref, ref, w_ss, w_rs, across, partner)

    w_pass(0, w_at(xs, 0), 9, 4, w_at(xs, 0), ys)
    w_pass(2, w_at(ys, 1), 10, 5, w_some(ys, half + skew, half - skew), xs)
    g_step(1)

    f_end()

    def pass2(i, carry):
        at = lanes(i)
        out = local[:, at] + dot(q_ref[:, at], in_f[i], 1, 0) * enter_s[i]
        a_pair[core_rows(core), at] = out.astype(BF16)
        return carry

    lax.fori_loop(0, heads, pass2, 0)

    mine = a_pair.at[core_rows(core)]
    ship(mine, mine, a_ss, a_rs, 0, partner)

    inner = jnp.logical_and(h > 0, h < n_head - 1)
    mate = h + 1 - 2 * (h % 2)

    def part(target, p, store):
        def tile(c, carry):
            at = pl.multiple_of(target * gwidth + c * wrows + p * half, half)
            value = dot(a_pair[core_rows(core), :], w_full[pl.ds(at, half), :], 1, 1)
            store(c, value)
            return carry

        lax.fori_loop(0, gwidth // wrows, tile, 0)

    def chunk_cols(c):
        return pl.ds(pl.multiple_of(c * half, half), half)

    def z_copy(b, p, dst, rs, to):
        return rcopy(z_send.at[b, p], dst, z_ss.at[b * 2 + p], rs, s, to)

    def z_near(b, p):
        z_copy(b, p, near.at[p], n_rs.at[p], mate).start()

    def z_fold(b, p):
        return z_copy(b, p, fold.at[b % 2, p], f_rs.at[(b % 2) * 2 + p], mate)

    def make_parts(chunks):
        for b, p in chunks:

            @pl.when(b != h)
            def _(b=b, p=p):
                def keep_part(c, value):
                    z_send[b, p, :, chunk_cols(c)] = value.astype(BF16)

                part(b, p, keep_part)

            @pl.when(jnp.logical_and(jnp.logical_not(inner), jnp.logical_and(b != h, b != mate)))
            def _(b=b, p=p):
                z_fold(b, p).start()

    def pass_parts(chunks):
        for b, p in chunks:

            @pl.when(jnp.logical_and(inner, b == mate))
            def _(b=b, p=p):
                z_near(b, p)

            @pl.when(jnp.logical_and(inner, jnp.logical_and(b != h, b != mate)))
            def _(b=b, p=p):
                z_fold(b, p).wait_recv()
                z_send[b, p] = (z_send[b, p].astype(F32) + fold[b % 2, p].astype(F32)).astype(BF16)
                z_copy(b, p, merged.at[p], m_rs.at[p], b).start()

    xo, yo, do = xn * 2 + other, yn * 2 + other, dn * 2 + other
    got(w_full.at[pl.ds(pl.multiple_of(partner * wrows, wrows), wrows)], w_ss, w_rs, 8)
    got(w_at(xo, 0), w_ss, w_rs, 9)
    got(w_at(yo, 1), w_ss, w_rs, 10)
    early = [(chip, 0), (chip, 1), (xn, 0), (yn, 1)]
    make_parts(early)

    g_step(2)
    w_pass(1, w_at(xs, 1), 11, 6, w_some(xs, half, skew), ys)
    w_pass(3, w_at(ys, 0), 12)
    got(w_at(xo, 1), w_ss, w_rs, 11)
    got(w_at(yo, 0), w_ss, w_rs, 12)
    middle = [(xn, 1), (yn, 0)]
    make_parts(middle)
    other_half = a_pair.at[core_rows(other)]
    got(other_half, a_ss, a_rs, 0)

    last = n_head - 1 - h
    for f in range(n_head):

        @pl.when(jnp.logical_or(inner, f != last))
        def _(f=f):
            got(g_pair.at[f, core_rows(other)], x_ss, x_rs, f)

    def gw_block(f, part, store):
        def tile(j, carry):
            at = pl.ds(pl.multiple_of(j * TILE, TILE), TILE)
            store(at, dot(g_pair[f, :, part * half : (part + 1) * half], a_pair[:, at], 0, 0))
            return carry

        lax.fori_loop(0, width // TILE, tile, 0)

    def send_gw(i, f, part, to, extra=None):
        def keep_gw(at, value):
            if extra is not None:
                value = value + wg_recv[extra, :, at].astype(F32)
            wg_send[i, :, at] = value.astype(BF16)

        gw_block(f, part, keep_gw)
        ship(wg_send.at[i], wg_recv.at[i], wg_ss, wg_rs, i, to)

    def pull(f, store):
        def tile(j, carry):
            at = pl.ds(pl.multiple_of(j * TILE, TILE), TILE)
            store(at, dot(g_full[f], w_full[pl.ds(pl.multiple_of(f * gwidth, gwidth), gwidth), at], 1, 0))
            return carry

        lax.fori_loop(0, width // TILE, tile, 0)

    def pull_more(at, value):
        local[:, at] = local[:, at] + value

    def pull_last(at, value):
        ga_s[:, at] = (local[:, at] + value).astype(BF16)

    local[...] = jnp.zeros_like(local)
    for f in (chip, xn, yn):

        @pl.when(jnp.logical_or(inner, f != last))
        def _(f=f):
            pull(f, pull_more)

    swap = jnp.where(jnp.logical_and(jnp.logical_not(inner), dn == last), 1, 0)
    send_gw(2 * swap, swap * xn + (1 - swap) * dn, 0, xs)
    send_gw(1 + 2 * swap, swap * yn + (1 - swap) * dn, 1, ys)

    ds = dn * 2 + core
    w_pass(4, w_at(ds, 0), 13)
    w_pass(6, w_some(ds, half, skew), 15)
    w_pass(5, w_some(ds, half + skew, half - skew), 14)
    for d in range(3, n_head):
        g_step(d)
    got(w_at(do, 0), w_ss, w_rs, 13)
    got(w_some(do, half, skew), w_ss, w_rs, 15)
    got(w_some(do, half + skew, half - skew), w_ss, w_rs, 14)
    pass_parts(early)
    late = [(dn, 0), (dn, 1)]
    make_parts(late)

    @pl.when(jnp.logical_not(inner))
    def _():
        z_near(mate, 0)
        z_near(mate, 1)


    @pl.when(jnp.logical_not(inner))
    def _():
        got(g_pair.at[last, core_rows(other)], x_ss, x_rs, last)

    send_gw(2 - 2 * swap, swap * dn + (1 - swap) * xn, 0, xs)
    send_gw(3 - 2 * swap, swap * dn + (1 - swap) * yn, 1, ys)

    @pl.when(jnp.logical_and(jnp.logical_not(inner), dn != last))
    def _():
        pull(last, pull_more)

    pull(dn, pull_last)

    def pass3(i, carry):
        at = lanes(i)
        g = ga_s[:, at]
        sum_b[i] = dot((q_ref[:, at].astype(F32) * enter_s[i]).astype(BF16), g, 0, 0).astype(BF16)
        return carry

    lax.fori_loop(0, heads, pass3, 0)
    b_begin()
    pass_parts(middle)

    got(wg_recv.at[0], wg_ss, wg_rs, 0)
    send_gw(4, yn, 0, ys, 0)
    got(wg_recv.at[1], wg_ss, wg_rs, 1)
    send_gw(5, xn, 1, xs, 1)
    pass_parts(late)

    def pass4(i, carry):
        at = lanes(i)
        q, k, v, g = q_ref[:, at], k_ref[:, at], v_ref[:, at], ga_s[:, at]
        back = (dot(g, v, 1, 1) * decay_s[i]).astype(BF16)
        gq = dot(back, k, 1, 0) + dot(g, in_f[i], 1, 1) * enter_s[i]
        gq_ref[:, at] = gq.astype(BF16)
        local[:, at] = dot(back, q, 0, 0)
        return carry

    lax.fori_loop(0, heads, pass4, 0)

    for p in range(2):

        def own_part(c, value, p=p):
            local2[:, pl.ds(pl.multiple_of(c * wrows + p * half, half), half)] = value

        part(h, p, own_part)

    for p in range(2):

        def keep_own(at, value, p=p):
            gw_ref[p * half : (p + 1) * half, at] = value

        gw_block(chip, p, keep_own)

    b_end()

    def pass5(i, carry):
        at = lanes(i)
        k, v, g = k_ref[:, at], v_ref[:, at], ga_s[:, at]
        gk = local[:, at] + dot(v, in_b[i], 1, 1) * leave_s[i]
        gv = dot(attn_s[i], g, 0, 0) + dot(k, in_b[i], 1, 0) * leave_s[i]
        gk_ref[:, at] = gk.astype(BF16)
        gv_ref[:, at] = gv.astype(BF16)
        return carry

    lax.fori_loop(0, heads, pass5, 0)

    for p in range(2):
        rcopy(near.at[p], near.at[p], z_ss.at[0], n_rs.at[p], s, mate).wait_recv()
        rcopy(merged.at[p], merged.at[p], z_ss.at[0], m_rs.at[p], s, mate).wait_recv()
        for c in range(gwidth // wrows):
            at, cols = pl.ds(c * wrows + p * half, half), pl.ds(c * half, half)
            total = local2[:, at] + near[p, :, cols].astype(F32) + merged[p, :, cols].astype(F32)
            mixed_ref[:, at] = total.astype(BF16)

    for p in range(2):
        got(wg_recv.at[2 + p], wg_ss, wg_rs, 2 + p)
        got(wg_recv.at[4 + p], wg_ss, wg_rs, 4 + p)
        at = pl.ds(p * half, half)
        gw_ref[at, :] = gw_ref[at, :] + (wg_recv[2 + p].astype(F32) + wg_recv[4 + p].astype(F32))

    for copy in sent:
        copy.wait_send()
    for f in range(n_head):
        g_cross(f, g_full.at[f]).wait_send()
    for j in range(1, n_head):
        g_each(j, lambda copy: copy.wait_send())
        for p in range(2):
            z_copy((h + j) % n_head, p, near.at[p], n_rs.at[p], mate).wait_send()
    f_drain()
    b_drain()


def store_kernel(*refs):
    copies = []
    for i in range(5):
        src, dst = refs[i], refs[5 + i]
        pieces = 4 if i == 4 else 1
        rows = src.shape[0] // pieces
        for j in range(pieces):
            at = pl.ds(j * rows, rows)
            copies.append(pltpu.make_async_copy(src.at[at], dst.at[at], refs[10].at[len(copies)]))
    for copy in copies[::-1]:
        copy.start()
    for copy in copies:
        copy.wait()


def square_call(n_head, queries, keys, values, log_decay, lengths, out_weight, out_grad):
    rows, width = queries.shape
    heads = log_decay.shape[0]
    wrows = out_weight.shape[0]
    gwidth = out_grad.shape[1]
    dma = lambda n: pltpu.SemaphoreType.DMA((n,))
    vm = pltpu.VMEM
    scratch = [vm((rows, width), BF16)] * 3 + [
        vm((8 * wrows, width), BF16),
        vm((n_head, rows, gwidth), BF16),
        vm((n_head, 2 * rows, wrows), BF16),
        vm((2 * rows, width), BF16),
        vm((n_head, 2, rows, wrows), BF16),
        vm((2, rows, wrows), BF16),
        vm((2, 2, rows, wrows), BF16),
        vm((2, rows, wrows), BF16),
        vm((6, wrows // 2, width), BF16),
        vm((6, wrows // 2, width), BF16),
        vm((rows, width), F32),
        vm((rows, gwidth), F32),
        vm((heads, rows, rows), F32),
        vm((heads, rows, rows), BF16),
        vm((heads, rows, HD), F32),
        vm((heads, rows, HD), F32),
        vm((rows, width), BF16),
        vm((heads, 8, HD), F32),
    ] + [vm((heads, HD, HD), BF16)] * 8 + [
        dma(16), dma(16), dma(2 * n_head - 2), dma(2 * n_head - 2), dma(n_head), dma(n_head), dma(1), dma(1),
        dma(2 * n_head), dma(2), dma(4), dma(2), dma(6), dma(6), dma(4), dma(4), dma(5),
    ]
    spec = pl.BlockSpec(memory_space=pltpu.VMEM)
    anywhere = pl.BlockSpec(memory_space=pl.ANY)
    outs = pl.pallas_call(
        functools.partial(square_kernel, n_head),
        out_shape=[vm((rows, gwidth), BF16)] + [vm((rows, width), BF16)] * 3 + [vm((wrows, width), F32)],
        in_specs=[pl.BlockSpec(memory_space=pltpu.SMEM)] + [anywhere] * 3 + [spec] + [anywhere] * 2,
        out_specs=[spec] * 5,
        scratch_shapes=scratch,
        compiler_params=pltpu.CompilerParams(
            collective_id=1, has_side_effects=True, vmem_limit_bytes=61360 * 1024
        ),
    )(lengths, queries, keys, values, log_decay, out_weight, out_grad)
    return pl.pallas_call(
        store_kernel,
        out_shape=[jax.ShapeDtypeStruct(o.shape, o.dtype) for o in outs],
        in_specs=[spec] * 5,
        out_specs=[anywhere] * 5,
        scratch_shapes=[dma(8)],
        compiler_params=pltpu.CompilerParams(vmem_limit_bytes=1 << 20),
        cost_estimate=pl.CostEstimate(flops=0, bytes_accessed=4 << 20, transcendentals=0),
    )(*[pltpu.with_memory_space_constraint(o, pltpu.VMEM) for o in outs])


def body(n_seq, n_head, queries, keys, values, log_decay, lengths, out_weight, out_grad):
    rows, width = queries.shape
    heads = log_decay.shape[0]
    wrows = out_weight.shape[0]
    gwidth = out_grad.shape[1]
    chips = n_seq // 2
    longest = n_seq * rows // 4
    hops = (longest - 1) // rows + 1
    if chips == 4 and n_head == 4 and gwidth == 2 * wrows and wrows % 256 == 0 and hops == 2:
        return square_call(n_head, queries, keys, values, log_decay, lengths, out_weight, out_grad)
    dma = lambda n: pltpu.SemaphoreType.DMA((n,))
    vm = pltpu.VMEM
    scratch = [
        vm((n_seq * wrows, width), BF16),
        vm((n_seq * rows, width), BF16),
        vm((n_head, rows, gwidth), BF16),
        vm((n_seq * rows, wrows), BF16),
        vm((n_head - 1, rows, gwidth), BF16),
        vm((n_head - 1, rows, gwidth), BF16),
        vm((rows, width), F32),
        vm((rows, gwidth), F32),
        vm((heads, rows, rows), F32),
        vm((heads, rows, rows), BF16),
        vm((heads, rows, HD), F32),
        vm((heads, rows, HD), F32),
        vm((heads, HD, HD), BF16),
        vm((rows, width), BF16),
        vm((heads, 8, HD), F32),
        vm((hops, heads, 8, HD), F32),
        vm((hops, heads, 8, HD), F32),
        vm((heads, HD, HD), BF16),
        vm((heads, HD, HD), BF16),
        vm((hops, heads, HD, HD), BF16),
        vm((hops, heads, HD, HD), BF16),
        dma(2 * chips + 1), dma(2 * chips + 1), dma(2 * chips + 1), dma(2 * chips + 1),
        dma(2 * n_head - 2), dma(2 * n_head - 2), dma(n_seq - 1), dma(n_seq - 1), dma(n_head - 1), dma(n_head - 1),
        dma(hops), dma(hops), dma(hops), dma(hops), dma(hops), dma(hops), dma(hops), dma(hops),
    ]
    spec = pl.BlockSpec(memory_space=pltpu.VMEM)
    return pl.pallas_call(
        functools.partial(kernel, n_seq, n_head, hops),
        out_shape=[vm((rows, gwidth), BF16)] + [vm((rows, width), BF16)] * 3 + [vm((wrows, width), F32)],
        in_specs=[pl.BlockSpec(memory_space=pltpu.SMEM)] + [spec] * 6,
        out_specs=[spec] * 5,
        scratch_shapes=scratch,
        compiler_params=pltpu.CompilerParams(
            collective_id=0, has_side_effects=True, vmem_limit_bytes=61360 * 1024
        ),
    )(lengths, queries, keys, values, log_decay, out_weight, out_grad)


def solution(mesh):
    both = P("seq", "head")
    in_specs = (both, both, both, P("head", "seq"), P(), both, both)
    return jax.shard_map(
        functools.partial(body, mesh.shape["seq"], mesh.shape["head"]),
        mesh=mesh, in_specs=in_specs, out_specs=(both,) * 5, check_vma=False,
    )
```
